32 devices in a mesh: rep: 4 (over z), fsdp: 8 (over y, x, core).
Axes of the slice: x: 2, y: 2, z: 4, core: 2. Of those that a mesh axis runs over, the one named last changes fastest.
Arguments:
- tokens: bfloat16 [64, 512, 768], P(('rep', 'fsdp')), may hold values from -6 to 6
- cotangent: bfloat16 [64, 512, 768], P(('rep', 'fsdp')), may hold values from -6 to 6
- lengths: int32 [64], P(('rep', 'fsdp')), may hold values from 256 to 512, as said below
- live_batches: int32 [32], P(('rep', 'fsdp')), may hold values from 1 to 2, as said below
- w_qkv: bfloat16 [2, 768, 2304], P(None, 'fsdp'), may hold values from -0.21875 to 0.21875
- w_out: bfloat16 [2, 768, 768], P(None, 'fsdp'), may hold values from -0.875 to 0.875
- w_up: bfloat16 [2, 768, 3072], P(None, 'fsdp'), may hold values from -0.21875 to 0.21875
- w_down: bfloat16 [2, 3072, 768], P(None, 'fsdp'), may hold values from -0.109375 to 0.109375
- up_bias: float32 [2, 3072], P(None, 'fsdp'), may hold values from -3 to 3
- biases: float32 [2, 6, 768], P(None, None, 'fsdp'), may hold values from -3 to 3
- norm_gains: float32 [2, 2, 768], P(None, None, 'fsdp'), may hold values from 0.5 to 1.5
Outputs:
- outputs: bfloat16 [64, 512, 768], P(('rep', 'fsdp'))
- grad_tokens: bfloat16 [64, 512, 768], P(('rep', 'fsdp'))
- grad_qkv: float32 [2, 768, 2304], P(None, 'fsdp')
- grad_out: float32 [2, 768, 768], P(None, 'fsdp')
- grad_up: float32 [2, 768, 3072], P(None, 'fsdp')
- grad_down: float32 [2, 3072, 768], P(None, 'fsdp')
- grad_up_bias: float32 [2, 3072], P(None, 'fsdp')
- grad_biases: float32 [2, 6, 768], P(None, None, 'fsdp')
- grad_gains: float32 [2, 2, 768], P(None, None, 'fsdp')
The draws below stay inside these ranges and needn't reach their ends.
Inputs may be any that keep to these rules, and one draw needn't show every extreme that they name: `lengths`: positions from a sequence's length on are padding; 512 and 256 occur in every draw. `live_batches`: entry g counts the live sequences, from the first, among sequences g * 2 to g * 2 + 2 - 1 (the rows of one device); the others are empty; 1 and 2 occur in every draw.
All inputs are finite; a program needn't handle non-finite values.
Results may differ from the reference program's by a relative error of at most 0.035.
Values may be sent and summed in bfloat16 or wider, within the bound.
A program may use at most 384 MiB of HBM per device.

```python
import math
import jax
import jax.numpy as jnp
from jax import lax

D = 768
HEADS = 12
HEAD = 64
FF = 3072
SEQ = 512
LAYERS = 2
MB = 2
GROUPS = 32
SEQS = 64


def draw_lengths(key, part):
    first_key, second_key = jax.random.split(jax.random.fold_in(key, 11))
    draw_values = jax.random.randint(first_key, (SEQS,), SEQ // 2, SEQ + 1, dtype=jnp.int32)
    shuffled = jax.random.permutation(second_key, SEQS)
    draw_values = draw_values.at[shuffled[0]].set(SEQ).at[shuffled[1]].set(SEQ // 2)
    return draw_values.astype(jnp.int32)


def draw_live_batches(key, part):
    first_key, second_key = jax.random.split(jax.random.fold_in(key, 23))
    draw_values = jax.random.randint(first_key, (GROUPS,), 1, MB + 1, dtype=jnp.int32)
    shuffled = jax.random.permutation(second_key, GROUPS)
    draw_values = draw_values.at[shuffled[0]].set(MB).at[shuffled[1]].set(1)
    return draw_values.astype(jnp.int32)


def level_of(key, dims, shards, smallest, top_value):
    def one(position, parts):
        steps = jax.random.uniform(jax.random.fold_in(jax.random.fold_in(key, 6), position), (parts,), jnp.float32, smallest / len(shards), top_value / len(shards))
        return jnp.repeat(jnp.exp(steps), dims[position] // parts).reshape((-1,) + (1,) * (len(dims) - position - 1))

    level = one(*shards[0])
    for cut in shards[1:]:
        level = level * one(*cut)
    return level


def normal_values(key, dims, scale, limit, cuts=(), kind=jnp.bfloat16):
    level = level_of(key, dims, cuts, -0.22, 0.18) if cuts else 1.0
    values = jax.random.normal(key, dims, jnp.float32) * scale * level
    return jnp.minimum(jnp.maximum(values, -limit), limit).astype(kind)


def setup_inputs(seed: int = 0) -> dict:
    arg_keys = jax.random.split(jax.random.key(seed), 12)
    return {
        "tokens": normal_values(arg_keys[0], (SEQS, SEQ, D), 1.0, 6.0, ((0, 32),)),
        "cotangent": normal_values(arg_keys[1], (SEQS, SEQ, D), 1.0, 6.0, ((0, 32),)),
        "lengths": draw_lengths(jax.random.fold_in(arg_keys[11], 71), 0),
        "live_batches": draw_live_batches(jax.random.fold_in(arg_keys[11], 71), 0),
        "w_qkv": normal_values(arg_keys[4], (LAYERS, D, 3 * D), D ** -0.5, 0.21875, ((1, 8),)),
        "w_out": normal_values(arg_keys[5], (LAYERS, D, D), (D // 16) ** -0.5, 0.875, ((1, 8),)),
        "w_up": normal_values(arg_keys[6], (LAYERS, D, FF), D ** -0.5, 0.21875, ((1, 8),)),
        "w_down": normal_values(arg_keys[7], (LAYERS, FF, D), FF ** -0.5, 0.109375, ((1, 8),)),
        "up_bias": normal_values(arg_keys[8], (LAYERS, FF), 0.5, 3.0, ((1, 8),), jnp.float32),
        "biases": normal_values(arg_keys[9], (LAYERS, 6, D), 0.5, 3.0, ((2, 8),), jnp.float32),
        "norm_gains": jnp.clip(1.0 + 0.1 * jax.random.normal(arg_keys[10], (LAYERS, 2, D), jnp.float32), 0.5, 1.5),
    }


@jax.custom_vjp
def low(v):
    return lax.optimization_barrier(v.astype(jnp.bfloat16)).astype(jnp.float32)

@jax.custom_vjp
def low_back(v):
    return v

def low_keep(v):
    return (low(v), None)

def low_pass(kept, grad):
    return (grad,)

def back_keep(v):
    return (v, None)

def back_low(kept, grad):
    return (low(grad),)
low.defvjp(low_keep, low_pass)
low_back.defvjp(back_keep, back_low)
highest = lax.Precision.HIGHEST
epsilon = 1e-05
big_negative = -1000000000.0

def norm_rows(values, gain_row, shift_row):
    middle = lax.optimization_barrier(jnp.mean(values, axis=-1, keepdims=True))
    centred = values - middle
    spread = lax.optimization_barrier(jnp.mean(centred * centred, axis=-1, keepdims=True))
    return centred * lax.rsqrt(spread + epsilon) * gain_row + shift_row

def block_layer(hidden, key_mask, layer_params):
    w_qkv, w_out, w_up, w_down, up_bias, bias_rows, gain_rows = layer_params
    batches = hidden.shape[0]
    shaped = (batches, SEQ, HEADS, HEAD)
    base_low = low(hidden)
    projected = jnp.einsum('bsd,de->bse', base_low, w_qkv, precision=highest)
    queries = low(low_back((projected[..., :D] + bias_rows[0]) * HEAD ** (-0.5))).reshape(shaped)
    key_rows = low(low_back(projected[..., D:2 * D])).reshape(shaped)
    value_rows = low(low_back(projected[..., 2 * D:] + bias_rows[1])).reshape(shaped)
    scores = jnp.einsum('bqhe,bkhe->bhqk', queries, key_rows, precision=highest)
    scores = low_back(scores + key_mask[:, None, None, :])
    row_peak = lax.optimization_barrier(jnp.max(scores, axis=-1, keepdims=True))
    raised = jnp.exp(scores - row_peak)
    attention = raised / lax.optimization_barrier(jnp.sum(raised, axis=-1, keepdims=True))
    context = jnp.einsum('bhqk,bkhe->bqhe', low(attention), value_rows, precision=highest)
    context = low(low_back(context.reshape(batches, SEQ, D)))
    attn_out = low_back(jnp.einsum('bsd,de->bse', context, w_out, precision=highest) + bias_rows[2])
    mid_rows = norm_rows(hidden + attn_out, gain_rows[0], bias_rows[4])
    pre_act = low_back(jnp.einsum('bsd,df->bsf', low(mid_rows), w_up, precision=highest) + up_bias)
    act_rows = jax.nn.gelu(pre_act, approximate=False)
    ffn_out = low_back(jnp.einsum('bsf,fd->bsd', low(act_rows), w_down, precision=highest) + bias_rows[3])
    return norm_rows(mid_rows + ffn_out, gain_rows[1], bias_rows[5])

def reference(tokens, cotangent, lengths, live_batches, w_qkv, w_out, w_up, w_down, up_bias, biases, norm_gains):
    params = (w_qkv.astype(jnp.float32), w_out.astype(jnp.float32), w_up.astype(jnp.float32), w_down.astype(jnp.float32), up_bias.astype(jnp.float32), biases.astype(jnp.float32), norm_gains.astype(jnp.float32))
    places = jnp.arange(SEQ, dtype=jnp.int32)
    within = jnp.arange(SEQS, dtype=jnp.int32) % MB
    alive_rows = within < jnp.repeat(live_batches, MB)
    inside = places[None, :] < lengths[:, None]
    valid_rows = jnp.where(inside & alive_rows[:, None], 1.0, 0.0).astype(jnp.float32)
    key_masks = jnp.where(inside, 0.0, big_negative).astype(jnp.float32)
    group_size = math.gcd(SEQS, max(1, 4096 // SEQ))
    steps_count = SEQS // group_size

    def blocks_of(array):
        return array.reshape((steps_count, group_size) + array.shape[1:])

    def scan_step(totals, scan_items):
        block_in, block_cot, block_mask, block_valid = scan_items

        def forward(block_rows, all_params):
            hidden = block_rows
            for layer_idx in range(LAYERS):
                hidden = block_layer(hidden, block_mask, tuple((member[layer_idx] for member in all_params)))
            return hidden * block_valid[:, :, None]
        result, pullback = jax.vjp(forward, block_in, params)
        grad_block, grad_params = pullback(block_cot)
        totals = tuple((running + extra for running, extra in zip(totals, grad_params)))
        return (totals, (result.astype(jnp.bfloat16), grad_block.astype(jnp.bfloat16)))
    initial = tuple((jnp.zeros(member.shape, jnp.float32) for member in params))
    totals, (outputs, grad_tokens) = lax.scan(scan_step, initial, (blocks_of(tokens.astype(jnp.float32)), blocks_of(cotangent.astype(jnp.float32)), blocks_of(key_masks), blocks_of(valid_rows)))
    return (outputs.reshape(SEQS, SEQ, D), grad_tokens.reshape(SEQS, SEQ, D), totals[0], totals[1], totals[2], totals[3], totals[4], totals[5], totals[6])
```

```python
import functools

import jax
import jax.numpy as jnp
from jax import lax
from jax.experimental import pallas as pl
from jax.experimental.pallas import tpu as pltpu
from jax.sharding import PartitionSpec as P

HEAD = 64
LAYERS = 2
GROUP = 256
ROWS = 256
VMEM_BYTES = 60 * 1024 * 1024

epsilon = 1e-05
big_negative = -1000000000.0
root_half = 0.7071067811865476
inv_root_tau = 0.3989422804014327
f32 = jnp.float32
bf16 = jnp.bfloat16


def dot_nn(a, b):
    return lax.dot_general(a, b, (((1,), (0,)), ((), ())), preferred_element_type=f32)


def dot_nt(a, b):
    return lax.dot_general(a, b, (((1,), (1,)), ((), ())), preferred_element_type=f32)


def whole(shape):
    zeros = (0,) * len(shape)
    return pl.BlockSpec(shape, lambda *_: zeros, pipeline_mode=pl.Buffered(1))


def column_block(rows, width):
    return pl.BlockSpec((rows, width), lambda j, *_: (0, j))


ANY = pl.BlockSpec(memory_space=pl.ANY)


def piece_copies(me, pieces, target, sems):
    depth = pieces[0].shape[0]
    copies = []
    for mask, piece in enumerate(pieces):
        start = pl.multiple_of((me ^ mask) * depth, 16)
        copies.append(pltpu.make_async_copy(piece, target.at[pl.ds(start, depth), :], sems.at[mask]))
    return copies


def norm_forward(total, gain, shift):
    middle = jnp.mean(total, axis=-1, keepdims=True)
    centred = total - middle
    spread = jnp.mean(centred * centred, axis=-1, keepdims=True)
    scaling = lax.rsqrt(spread + epsilon)
    normed = centred * scaling
    return normed * gain + shift, normed, scaling


def norm_backward(grad, normed, scaling, gain):
    scaled = grad * gain
    first = jnp.mean(scaled, axis=-1, keepdims=True)
    second = jnp.mean(scaled * normed, axis=-1, keepdims=True)
    return scaling * (scaled - first - normed * second)


def head_mask(shape, head):
    lanes = lax.broadcasted_iota(jnp.int32, shape, 1)
    return (lanes >= head * HEAD) & (lanes < (head + 1) * HEAD)


def attend_forward_kernel(n, seqs, me_ref, x_ref, small_ref, mask_ref, *refs):
    qkv_pieces, out_pieces = refs[:n], refs[n : 2 * n]
    q_ref, k_ref, v_ref, ctx_ref, lse_ref, mid_ref, low_ref, n1_ref, r1_ref = refs[2 * n : 2 * n + 9]
    base, w_qkv, w_out, acc, sems = refs[2 * n + 9 :]
    step, steps = pl.program_id(0), pl.num_programs(0)
    rows, width = x_ref.shape
    seq = rows // seqs
    heads = GROUP // HEAD
    qkv_copies = piece_copies(me_ref[0], qkv_pieces, w_qkv, sems.at[0])
    out_copies = piece_copies(me_ref[0], out_pieces, w_out, sems.at[1])

    @pl.when(step == 0)
    def _():
        for copy in qkv_copies:
            copy.start()
        for copy in out_copies:
            copy.start()
        base[...] = x_ref[...].astype(bf16)
        for copy in qkv_copies:
            copy.wait()
        for copy in out_copies:
            copy.wait()

    columns = pl.multiple_of(step * GROUP, GROUP)
    q_bias = small_ref[0:1, pl.ds(columns, GROUP)]
    v_bias = small_ref[1:2, pl.ds(columns, GROUP)]

    def project(block, carry):
        at = pl.ds(pl.multiple_of(block * ROWS, ROWS), ROWS)
        low = base[at, :]
        q = dot_nn(low, w_qkv[:, pl.ds(columns, GROUP)])
        q_ref[at, :] = ((q + q_bias) * HEAD ** (-0.5)).astype(bf16)
        k = dot_nn(low, w_qkv[:, pl.ds(pl.multiple_of(width + columns, GROUP), GROUP)])
        k_ref[at, :] = k.astype(bf16)
        v = dot_nn(low, w_qkv[:, pl.ds(pl.multiple_of(2 * width + columns, GROUP), GROUP)])
        v_ref[at, :] = (v + v_bias).astype(bf16)
        return carry

    lax.fori_loop(0, rows // ROWS, project, 0)

    def attend(s, carry):
        at = pl.ds(pl.multiple_of(s * seq, seq), seq)
        q, k = q_ref[at, :], k_ref[at, :]
        v_turned = v_ref[at, :].T
        key_mask = mask_ref[at, :]
        parts = []
        for head in range(heads):
            q_head = jnp.where(head_mask(q.shape, head), q, jnp.zeros_like(q))
            scores = dot_nt(k, q_head) + key_mask
            peak = jnp.max(scores, axis=0, keepdims=True)
            raised = jnp.exp(scores - peak)
            total = jnp.sum(raised, axis=0, keepdims=True)
            mixed = dot_nn(v_turned[head * HEAD : (head + 1) * HEAD, :], raised.astype(bf16))
            parts.append((mixed / total).astype(bf16))
            lse_ref[0, pl.ds(s * heads + head, 1), :] = peak + jnp.log(total)
        ctx_ref[at, :] = jnp.concatenate(parts, axis=0).T
        return carry

    lax.fori_loop(0, seqs, attend, 0)

    def mix(block, carry):
        at = pl.ds(pl.multiple_of(block * ROWS, ROWS), ROWS)
        term = dot_nn(ctx_ref[at, :], w_out[pl.ds(columns, GROUP), :])

        @pl.when(step == 0)
        def _():
            acc[at, :] = term

        @pl.when(step > 0)
        def _():
            acc[at, :] += term

        @pl.when(step == steps - 1)
        def _():
            total = x_ref[at, :].astype(f32) + acc[at, :] + small_ref[2:3, :]
            mid, normed, scaling = norm_forward(total, small_ref[6:7, :], small_ref[4:5, :])
            mid_ref[at, :] = mid
            low_ref[at, :] = mid.astype(bf16)
            n1_ref[at, :] = normed.astype(bf16)
            r1_ref[at, :] = scaling

        return carry

    lax.fori_loop(0, rows // ROWS, mix, 0)


def attend_forward(me, x, small, key_mask, qkv_pieces, out_pieces, seqs):
    n = len(qkv_pieces)
    rows, width = x.shape
    steps = width // GROUP
    seq = rows // seqs
    wide = jax.ShapeDtypeStruct((rows, width), bf16)
    heads = GROUP // HEAD
    return pl.pallas_call(
        functools.partial(attend_forward_kernel, n, seqs),
        out_shape=(
            wide,
            wide,
            wide,
            wide,
            jax.ShapeDtypeStruct((steps, seqs * heads, seq), f32),
            jax.ShapeDtypeStruct((rows, width), f32),
            wide,
            wide,
            jax.ShapeDtypeStruct((rows, 1), f32),
        ),
        grid_spec=pltpu.PrefetchScalarGridSpec(
            num_scalar_prefetch=1,
            grid=(steps,),
            in_specs=[whole((rows, width)), whole(small.shape), whole((rows, 1))] + [ANY] * (2 * n),
            out_specs=[column_block(rows, GROUP)] * 4
            + [
                pl.BlockSpec((1, seqs * heads, seq), lambda j, *_: (j, 0, 0)),
                whole((rows, width)),
                whole((rows, width)),
                whole((rows, width)),
                whole((rows, 1)),
            ],
            scratch_shapes=[
                pltpu.VMEM((rows, width), bf16),
                pltpu.VMEM((width, 3 * width), bf16),
                pltpu.VMEM((width, width), bf16),
                pltpu.VMEM((rows, width), f32),
                pltpu.SemaphoreType.DMA((2, n)),
            ],
        ),
        compiler_params=pltpu.CompilerParams(
            dimension_semantics=("arbitrary",), vmem_limit_bytes=VMEM_BYTES
        ),
        cost_estimate=cost(8 * rows * width * width + 16 * rows * seq * width, 20 * rows * width),
        name="attend_forward",
    )(me, x, small, key_mask, *qkv_pieces, *out_pieces)


def ffn_forward_kernel(n, last, me_ref, mid_ref, low_ref, small_ref, up_bias_ref, valid_ref, *refs):
    up_pieces, down_pieces = refs[:n], refs[n : 2 * n]
    outs = refs[2 * n :]
    act_ref, slope_ref, n2_ref, r2_ref, hid_ref = outs[:5]
    if last:
        w_up, w_down, acc, sems = outs[5:]
    else:
        hid_low_ref, w_up, w_down, acc, sems = outs[5:]
    step, steps = pl.program_id(0), pl.num_programs(0)
    rows, width = mid_ref.shape
    chunk = act_ref.shape[1]
    up_copies = piece_copies(me_ref[0], up_pieces, w_up, sems.at[0])
    down_copies = piece_copies(me_ref[0], down_pieces, w_down, sems.at[1])

    @pl.when(step == 0)
    def _():
        for copy in up_copies:
            copy.start()
        for copy in down_copies:
            copy.start()
        for copy in up_copies:
            copy.wait()
        for copy in down_copies:
            copy.wait()

    columns = pl.multiple_of(step * chunk, chunk)
    tile = 256

    def block_step(block, carry):
        at = pl.ds(pl.multiple_of(block * ROWS, ROWS), ROWS)
        low = low_ref[at, :]
        for part in range(chunk // tile):
            inside = slice(part * tile, (part + 1) * tile)
            at_units = pl.ds(pl.multiple_of(columns + part * tile, tile), tile)
            pre = dot_nn(low, w_up[:, at_units]) + up_bias_ref[:, inside]
            share = 0.5 * (1.0 + lax.erf(pre * root_half))
            act_ref[at, inside] = (pre * share).astype(bf16)
            density = inv_root_tau * jnp.exp(-0.5 * pre * pre)
            slope_ref[at, inside] = (share + pre * density).astype(bf16)
        term = dot_nn(act_ref[at, :], w_down[pl.ds(columns, chunk), :])

        @pl.when(step == 0)
        def _():
            acc[at, :] = term

        @pl.when(step > 0)
        def _():
            acc[at, :] += term

        @pl.when(step == steps - 1)
        def _():
            total = mid_ref[at, :] + acc[at, :] + small_ref[3:4, :]
            hidden, normed, scaling = norm_forward(total, small_ref[7:8, :], small_ref[5:6, :])
            n2_ref[at, :] = normed.astype(bf16)
            r2_ref[at, :] = scaling
            if last:
                hid_ref[at, :] = (hidden * valid_ref[at, :]).astype(bf16)
            else:
                hid_ref[at, :] = hidden
                hid_low_ref[at, :] = hidden.astype(bf16)

        return carry

    lax.fori_loop(0, rows // ROWS, block_step, 0)


def ffn_forward(me, mid, low, small, up_bias, valid, up_pieces, down_pieces, last):
    n = len(up_pieces)
    rows, width = mid.shape
    units = up_bias.shape[1]
    chunk = width
    steps = units // chunk
    out_shape = [
        jax.ShapeDtypeStruct((rows, units), bf16),
        jax.ShapeDtypeStruct((rows, units), bf16),
        jax.ShapeDtypeStruct((rows, width), bf16),
        jax.ShapeDtypeStruct((rows, 1), f32),
        jax.ShapeDtypeStruct((rows, width), bf16 if last else f32),
    ]
    out_specs = [column_block(rows, chunk)] * 2 + [
        whole((rows, width)),
        whole((rows, 1)),
        whole((rows, width)),
    ]
    if not last:
        out_shape.append(jax.ShapeDtypeStruct((rows, width), bf16))
        out_specs.append(whole((rows, width)))
    return pl.pallas_call(
        functools.partial(ffn_forward_kernel, n, last),
        out_shape=tuple(out_shape),
        grid_spec=pltpu.PrefetchScalarGridSpec(
            num_scalar_prefetch=1,
            grid=(steps,),
            in_specs=[
                whole((rows, width)),
                whole((rows, width)),
                whole(small.shape),
                column_block(1, chunk),
                whole((rows, 1)),
            ]
            + [ANY] * (2 * n),
            out_specs=out_specs,
            scratch_shapes=[
                pltpu.VMEM((width, units), bf16),
                pltpu.VMEM((units, width), bf16),
                pltpu.VMEM((rows, width), f32),
                pltpu.SemaphoreType.DMA((2, n)),
            ],
        ),
        compiler_params=pltpu.CompilerParams(
            dimension_semantics=("arbitrary",), vmem_limit_bytes=VMEM_BYTES
        ),
        cost_estimate=cost(8 * rows * width * units, 8 * rows * units),
        name="ffn_forward",
    )(me, mid, low, small, up_bias, valid, *up_pieces, *down_pieces)


def shard_copies(n, me, source_of, keep_of, send_of, sems):
    def each(start):
        for owner in range(n):
            mask = me ^ owner
            place = mask // 2

            @pl.when(mask % 2 == 0)
            def _():
                copy = pltpu.make_async_copy(source_of(owner), keep_of(place), sems.at[owner])
                copy.start() if start else copy.wait()

            @pl.when(mask % 2 == 1)
            def _():
                copy = pltpu.make_async_copy(source_of(owner), send_of(place), sems.at[owner])
                copy.start() if start else copy.wait()

    return each


def ffn_backward_kernel(n, me_ref, g_ref, valid_ref, n2_ref, r2_ref, low_ref, n1_ref, r1_ref, small_ref, act_ref, slope_ref, *refs):
    up_pieces, down_pieces = refs[:n], refs[n : 2 * n]
    gs1_ref, ga1_ref, sums_ref, up_sum_ref, down_keep, down_send, up_keep, up_send = refs[2 * n : 2 * n + 8]
    w_up, w_down, gs2, gffn, gpre, acc, low_turned, d_down, d_up, sems, out_sems = refs[2 * n + 8 :]
    step, steps = pl.program_id(0), pl.num_programs(0)
    me = me_ref[0]
    rows, width = gs2.shape
    chunk = act_ref.shape[1]
    per_down = down_keep.shape[1]
    per_up = up_keep.shape[2]
    tile = 256
    up_copies = piece_copies(me, up_pieces, w_up, sems.at[0])
    down_copies = piece_copies(me, down_pieces, w_down, sems.at[1])

    @pl.when(step == 0)
    def _():
        for copy in down_copies:
            copy.start()
        for copy in up_copies:
            copy.start()
        sums_ref[...] = jnp.zeros_like(sums_ref)

        def prepare(block, carry):
            at = pl.ds(pl.multiple_of(block * ROWS, ROWS), ROWS)
            grad = g_ref[at, :].astype(f32) * valid_ref[at, :]
            normed = n2_ref[at, :].astype(f32)
            summed = norm_backward(grad, normed, r2_ref[at, :], small_ref[7:8, :])
            gs2[at, :] = summed
            low = summed.astype(bf16)
            gffn[at, :] = low
            sums_ref[0:1, :] += jnp.sum(grad * normed, axis=0, keepdims=True)
            sums_ref[1:2, :] += jnp.sum(grad, axis=0, keepdims=True)
            sums_ref[2:3, :] += jnp.sum(low.astype(f32), axis=0, keepdims=True)
            low_turned[:, at] = low_ref[at, :].T
            return carry

        lax.fori_loop(0, rows // ROWS, prepare, 0)
        for copy in down_copies:
            copy.wait()
        for copy in up_copies:
            copy.wait()

    columns = pl.multiple_of(step * chunk, chunk)
    up_sum_ref[...] = jnp.zeros_like(up_sum_ref)

    def through(block, carry):
        at = pl.ds(pl.multiple_of(block * ROWS, ROWS), ROWS)
        grad = gffn[at, :]
        for part in range(chunk // tile):
            inside = slice(part * tile, (part + 1) * tile)
            at_units = pl.ds(pl.multiple_of(columns + part * tile, tile), tile)
            grad_act = dot_nt(grad, w_down[at_units, :])
            low = (grad_act * slope_ref[at, inside].astype(f32)).astype(bf16)
            gpre[at, inside] = low
            up_sum_ref[:, inside] += jnp.sum(low.astype(f32), axis=0, keepdims=True)
        term = dot_nt(gpre[at, :], w_up[:, pl.ds(columns, chunk)])

        @pl.when(step == 0)
        def _():
            acc[at, :] = term

        @pl.when(step > 0)
        def _():
            acc[at, :] += term

        return carry

    lax.fori_loop(0, rows // ROWS, through, 0)

    def down_out(which):
        def run(start):
            for local in range(chunk // per_down):
                owner = which * (chunk // per_down) + local
                mask = me ^ owner
                source = d_down.at[pl.ds(local * per_down, per_down), :]
                place = mask // 2

                @pl.when(mask % 2 == 0)
                def _():
                    copy = pltpu.make_async_copy(source, down_keep.at[place], out_sems.at[0, local])
                    copy.start() if start else copy.wait()

                @pl.when(mask % 2 == 1)
                def _():
                    copy = pltpu.make_async_copy(source, down_send.at[place], out_sems.at[0, local])
                    copy.start() if start else copy.wait()

        return run

    def up_out(which):
        return shard_copies(
            n,
            me,
            lambda owner: d_up.at[pl.ds(owner * per_up, per_up), :],
            lambda place: up_keep.at[place, which],
            lambda place: up_send.at[place, which],
            out_sems.at[1],
        )

    @pl.when(step > 0)
    def _():
        down_out(step - 1)(False)

    def down_part(part, carry):
        at = pl.ds(pl.multiple_of(part * tile, tile), tile)
        turned = act_ref[:, at].T
        d_down[at, :] = dot_nn(turned, gffn[...]).astype(bf16)
        return carry

    lax.fori_loop(0, chunk // tile, down_part, 0)
    down_out(step)(True)

    @pl.when(step > 0)
    def _():
        up_out(step - 1)(False)

    def up_part(part, carry):
        at = pl.ds(pl.multiple_of(part * tile, tile), tile)
        d_up[at, :] = dot_nn(low_turned[at, :], gpre[...]).astype(bf16)
        return carry

    lax.fori_loop(0, width // tile, up_part, 0)
    up_out(step)(True)

    @pl.when(step == steps - 1)
    def _():
        def finish(block, carry):
            at = pl.ds(pl.multiple_of(block * ROWS, ROWS), ROWS)
            grad = gs2[at, :] + acc[at, :]
            normed = n1_ref[at, :].astype(f32)
            summed = norm_backward(grad, normed, r1_ref[at, :], small_ref[6:7, :])
            gs1_ref[at, :] = summed
            low = summed.astype(bf16)
            ga1_ref[at, :] = low
            sums_ref[3:4, :] += jnp.sum(grad * normed, axis=0, keepdims=True)
            sums_ref[4:5, :] += jnp.sum(grad, axis=0, keepdims=True)
            sums_ref[5:6, :] += jnp.sum(low.astype(f32), axis=0, keepdims=True)
            return carry

        lax.fori_loop(0, rows // ROWS, finish, 0)
        down_out(step)(False)
        up_out(step)(False)


def ffn_backward(me, grad, valid, n2, r2, low, n1, r1, small, act, slope, up_pieces, down_pieces):
    n = len(up_pieces)
    rows, width = grad.shape
    units = act.shape[1]
    chunk = width
    steps = units // chunk
    chips = n // 2
    down_half = jax.ShapeDtypeStruct((chips, units // n, width), bf16)
    up_half = jax.ShapeDtypeStruct((chips, steps, width // n, chunk), bf16)
    return pl.pallas_call(
        functools.partial(ffn_backward_kernel, n),
        out_shape=(
            jax.ShapeDtypeStruct((rows, width), f32),
            jax.ShapeDtypeStruct((rows, width), bf16),
            jax.ShapeDtypeStruct((8, width), f32),
            jax.ShapeDtypeStruct((1, units), f32),
            down_half,
            down_half,
            up_half,
            up_half,
        ),
        grid_spec=pltpu.PrefetchScalarGridSpec(
            num_scalar_prefetch=1,
            grid=(steps,),
            in_specs=[
                whole((rows, width)),
                whole((rows, 1)),
                whole((rows, width)),
                whole((rows, 1)),
                whole((rows, width)),
                whole((rows, width)),
                whole((rows, 1)),
                whole(small.shape),
                column_block(rows, chunk),
                column_block(rows, chunk),
            ]
            + [ANY] * (2 * n),
            out_specs=[
                whole((rows, width)),
                whole((rows, width)),
                whole((8, width)),
                column_block(1, chunk),
            ]
            + [ANY] * 4,
            scratch_shapes=[
                pltpu.VMEM((width, units), bf16),
                pltpu.VMEM((units, width), bf16),
                pltpu.VMEM((rows, width), f32),
                pltpu.VMEM((rows, width), bf16),
                pltpu.VMEM((rows, chunk), bf16),
                pltpu.VMEM((rows, width), f32),
                pltpu.VMEM((width, rows), bf16),
                pltpu.VMEM((chunk, width), bf16),
                pltpu.VMEM((width, chunk), bf16),
                pltpu.SemaphoreType.DMA((2, n)),
                pltpu.SemaphoreType.DMA((2, n)),
            ],
        ),
        compiler_params=pltpu.CompilerParams(
            dimension_semantics=("arbitrary",), vmem_limit_bytes=VMEM_BYTES
        ),
        cost_estimate=cost(10 * rows * width * units, 8 * rows * units),
        name="ffn_backward",
    )(me, grad, valid, n2, r2, low, n1, r1, small, act, slope, *up_pieces, *down_pieces)


def attend_backward_kernel(n, seqs, me_ref, ga_ref, gs_ref, base_ref, mask_ref, q_ref, k_ref, v_ref, ctx_ref, lse_ref, *refs):
    qkv_pieces, out_pieces = refs[:n], refs[n : 2 * n]
    gh_ref, sums_ref, qkv_keep, qkv_send, out_keep, out_send = refs[2 * n : 2 * n + 6]
    w_qkv, w_out, acc, base_turned, gctx, gproj, d_qkv, d_out, p_all, ds_all, sems, out_sems = refs[2 * n + 6 :]
    step, steps = pl.program_id(0), pl.num_programs(0)
    me = me_ref[0]
    rows, width = ga_ref.shape
    seq = rows // seqs
    heads = GROUP // HEAD
    per = width // n
    tile = 256
    qkv_copies = piece_copies(me, qkv_pieces, w_qkv, sems.at[0])
    out_copies = piece_copies(me, out_pieces, w_out, sems.at[1])

    @pl.when(step == 0)
    def _():
        for copy in out_copies:
            copy.start()
        for copy in qkv_copies:
            copy.start()

        def turn(block, carry):
            at = pl.ds(pl.multiple_of(block * ROWS, ROWS), ROWS)
            base_turned[:, at] = base_ref[at, :].T
            return carry

        lax.fori_loop(0, rows // ROWS, turn, 0)
        for copy in out_copies:
            copy.wait()
        for copy in qkv_copies:
            copy.wait()

    columns = pl.multiple_of(step * GROUP, GROUP)

    def through(block, carry):
        at = pl.ds(pl.multiple_of(block * ROWS, ROWS), ROWS)
        gctx[at, :] = dot_nt(ga_ref[at, :], w_out[pl.ds(columns, GROUP), :]).astype(bf16)
        return carry

    lax.fori_loop(0, rows // ROWS, through, 0)
    d_out[pl.ds(columns, GROUP), :] = dot_nn(ctx_ref[...].T, ga_ref[...]).astype(bf16)

    def attend(s, carry):
        at = pl.ds(pl.multiple_of(s * seq, seq), seq)
        q, k, v, grad = q_ref[at, :], k_ref[at, :], v_ref[at, :], gctx[at, :]
        k_turned = k.T
        key_mask = mask_ref[at, :]
        parts, q_heads, g_heads = [], [], []
        for head in range(heads):
            inside = head_mask(q.shape, head)
            q_head = jnp.where(inside, q, jnp.zeros_like(q))
            g_head = jnp.where(inside, grad, jnp.zeros_like(grad))
            scores = dot_nt(k, q_head) + key_mask
            attention = jnp.exp(scores - lse_ref[0, pl.ds(s * heads + head, 1), :])
            weighted = attention * dot_nt(v, g_head)
            inner = jnp.sum(weighted, axis=0, keepdims=True)
            grad_scores = (weighted - attention * inner).astype(bf16)
            here = slice(head * seq, (head + 1) * seq)
            p_all[:, here] = attention.astype(bf16)
            ds_all[:, here] = grad_scores
            turned = dot_nn(k_turned[head * HEAD : (head + 1) * HEAD, :], grad_scores)
            parts.append(turned.astype(bf16) * HEAD ** (-0.5))
            q_heads.append(q_head)
            g_heads.append(g_head)
        gproj[at, 0:GROUP] = jnp.concatenate(parts, axis=0).T
        gproj[at, GROUP : 2 * GROUP] = dot_nn(ds_all[...], jnp.concatenate(q_heads, axis=0)).astype(bf16)
        gproj[at, 2 * GROUP : 3 * GROUP] = dot_nn(p_all[...], jnp.concatenate(g_heads, axis=0)).astype(bf16)
        return carry

    lax.fori_loop(0, seqs, attend, 0)
    sums_ref[...] = jnp.zeros_like(sums_ref)

    def onward(block, carry):
        at = pl.ds(pl.multiple_of(block * ROWS, ROWS), ROWS)
        term = dot_nt(gproj[at, 0:GROUP], w_qkv[:, pl.ds(columns, GROUP)])
        term += dot_nt(gproj[at, GROUP : 2 * GROUP], w_qkv[:, pl.ds(pl.multiple_of(width + columns, GROUP), GROUP)])
        term += dot_nt(gproj[at, 2 * GROUP : 3 * GROUP], w_qkv[:, pl.ds(pl.multiple_of(2 * width + columns, GROUP), GROUP)])
        sums_ref[0:1, :] += jnp.sum(gproj[at, 0:GROUP].astype(f32), axis=0, keepdims=True)
        sums_ref[1:2, :] += jnp.sum(gproj[at, 2 * GROUP : 3 * GROUP].astype(f32), axis=0, keepdims=True)

        @pl.when(step == 0)
        def _():
            acc[at, :] = gs_ref[at, :] + term

        @pl.when(step > 0)
        def _():
            acc[at, :] += term

        @pl.when(step == steps - 1)
        def _():
            gh_ref[at, :] = acc[at, :].astype(gh_ref.dtype)

        return carry

    lax.fori_loop(0, rows // ROWS, onward, 0)

    def qkv_out(which, start):
        for part in range(3):
            at = pl.ds(pl.multiple_of(which * GROUP, GROUP), GROUP)
            shard_copies(
                n,
                me,
                lambda owner: d_qkv.at[pl.ds(owner * per, per), pl.ds(part * GROUP, GROUP)],
                lambda place: qkv_keep.at[place, part, :, at],
                lambda place: qkv_send.at[place, part, :, at],
                out_sems.at[part],
            )(start)

    @pl.when(step > 0)
    def _():
        qkv_out(step - 1, False)

    def weight_part(part, carry):
        at = pl.ds(pl.multiple_of(part * tile, tile), tile)
        d_qkv[at, :] = dot_nn(base_turned[at, :], gproj[...]).astype(bf16)
        return carry

    lax.fori_loop(0, width // tile, weight_part, 0)
    qkv_out(step, True)

    @pl.when(step == steps - 1)
    def _():
        out_copy = shard_copies(
            n,
            me,
            lambda owner: d_out.at[pl.ds(owner * per, per), :],
            lambda place: out_keep.at[place],
            lambda place: out_send.at[place],
            out_sems.at[3],
        )
        out_copy(True)
        qkv_out(step, False)
        out_copy(False)


def attend_backward(me, ga, gs, base, key_mask, q, k, v, ctx, lse, qkv_pieces, out_pieces, seqs, out_type):
    n = len(qkv_pieces)
    rows, width = ga.shape
    steps = width // GROUP
    seq = rows // seqs
    heads = GROUP // HEAD
    chips = n // 2
    qkv_half = jax.ShapeDtypeStruct((chips, 3, width // n, width), bf16)
    out_half = jax.ShapeDtypeStruct((chips, width // n, width), bf16)
    return pl.pallas_call(
        functools.partial(attend_backward_kernel, n, seqs),
        out_shape=(
            jax.ShapeDtypeStruct((rows, width), out_type),
            jax.ShapeDtypeStruct((8, width), f32),
            qkv_half,
            qkv_half,
            out_half,
            out_half,
        ),
        grid_spec=pltpu.PrefetchScalarGridSpec(
            num_scalar_prefetch=1,
            grid=(steps,),
            in_specs=[whole((rows, width))] * 3
            + [whole((rows, 1))]
            + [column_block(rows, GROUP)] * 4
            + [pl.BlockSpec((1, seqs * heads, seq), lambda j, *_: (j, 0, 0))]
            + [ANY] * (2 * n),
            out_specs=[whole((rows, width)), column_block(8, GROUP)] + [ANY] * 4,
            scratch_shapes=[
                pltpu.VMEM((width, 3 * width), bf16),
                pltpu.VMEM((width, width), bf16),
                pltpu.VMEM((rows, width), f32),
                pltpu.VMEM((width, rows), bf16),
                pltpu.VMEM((rows, GROUP), bf16),
                pltpu.VMEM((rows, 3 * GROUP), bf16),
                pltpu.VMEM((width, 3 * GROUP), bf16),
                pltpu.VMEM((width, width), bf16),
                pltpu.VMEM((seq, heads * seq), bf16),
                pltpu.VMEM((seq, heads * seq), bf16),
                pltpu.SemaphoreType.DMA((2, n)),
                pltpu.SemaphoreType.DMA((4, n)),
            ],
        ),
        compiler_params=pltpu.CompilerParams(
            dimension_semantics=("arbitrary",), vmem_limit_bytes=VMEM_BYTES
        ),
        cost_estimate=cost(16 * rows * width * width + 40 * rows * seq * width, 20 * rows * width),
        name="attend_backward",
    )(me, ga, gs, base, key_mask, q, k, v, ctx, lse, *qkv_pieces, *out_pieces)


def cost(flops, moved):
    return pl.CostEstimate(flops=int(flops), bytes_accessed=int(moved), transcendentals=0)


def swap(array, axis, count, mask):
    return lax.ppermute(array, axis, [(i, i ^ mask) for i in range(count)])


def gather_pieces(own, n, bits):
    pieces = {0: own}
    for bit in bits:
        for mask, piece in list(pieces.items()):
            pieces[mask | bit] = swap(piece, "fsdp", n, bit)
    return [pieces[mask] for mask in range(n)]


def scatter_pieces(keep, send, n, bits):
    other = swap(send, "fsdp", n, 1)
    terms = {place: [keep[place], other[place]] for place in range(n // 2)}

    def total(items):
        return sum(item.astype(f32) for item in items)

    for bit in bits:
        half = bit // 2
        leaving = [place for place in sorted(terms) if place & half]
        packed = jnp.stack([total(terms[place]).astype(bf16) for place in leaving])
        arrived = swap(packed, "fsdp", n, bit)
        for slot, place in enumerate(leaving):
            terms[place ^ half].append(arrived[slot])
            del terms[place]
    return total(terms[0])


def sum_replicas(shards, rank, count):
    def parts_of(array, index):
        split = array.reshape((count, array.shape[0] // count) + array.shape[1:])
        return lax.dynamic_index_in_dim(split, index, 0, keepdims=False)

    def packed(index):
        return jnp.concatenate([parts_of(array, index) for array in shards], axis=0)

    total = packed(rank)
    for mask in range(1, count):
        total = total + swap(packed(rank ^ mask).astype(bf16), "rep", count, mask).astype(f32)
    low = total.astype(bf16)
    pieces = jnp.stack([low] + [swap(low, "rep", count, mask) for mask in range(1, count)])
    ordered = [lax.dynamic_index_in_dim(pieces, rank ^ place, 0, keepdims=False) for place in range(count)]
    results = []
    start = 0
    for array in shards:
        size = array.shape[0] // count
        rows = [piece[start : start + size] for piece in ordered]
        results.append(jnp.concatenate(rows, axis=0).astype(f32))
        start += size
    return results


def gather_small(own, n, me):
    array = own[None]
    bit = 1
    while bit < n:
        other = swap(array, "fsdp", n, bit)
        upper = (me // bit) % 2 == 1
        array = jnp.concatenate([jnp.where(upper, other, array), jnp.where(upper, array, other)], axis=0)
        bit *= 2
    return array


def on_device(n, reps, tokens, cotangent, lengths, live_batches, w_qkv, w_out, w_up, w_down, up_bias, biases, norm_gains):
    seqs, seq, width = tokens.shape
    rows = seqs * seq
    units = w_up.shape[2]
    per = width // n
    me = lax.axis_index("fsdp").astype(jnp.int32)
    rank = lax.axis_index("rep").astype(jnp.int32)
    me_row = me[None]

    places = jnp.arange(seq, dtype=jnp.int32)
    inside = places[None, :] < lengths[:, None]
    alive = jnp.arange(seqs, dtype=jnp.int32) < live_batches[0]
    key_mask = jnp.where(inside, 0.0, big_negative).astype(f32).reshape(rows, 1)
    valid = jnp.where(inside & alive[:, None], 1.0, 0.0).astype(f32).reshape(rows, 1)
    ones = jnp.ones((rows, 1), f32)

    own_small = jnp.concatenate([up_bias.reshape(-1), biases.reshape(-1), norm_gains.reshape(-1)])
    small_all = gather_small(own_small, n, me)
    cut_a = LAYERS * units // n
    cut_b = cut_a + LAYERS * 6 * per
    up_bias_all = small_all[:, :cut_a].reshape(n, LAYERS, units // n).transpose(1, 0, 2).reshape(LAYERS, 1, units)
    bias_all = small_all[:, cut_a:cut_b].reshape(n, LAYERS, 6, per).transpose(1, 2, 0, 3).reshape(LAYERS, 6, width)
    gain_all = small_all[:, cut_b:].reshape(n, LAYERS, 2, per).transpose(1, 2, 0, 3).reshape(LAYERS, 2, width)
    smalls = jnp.concatenate([bias_all, gain_all], axis=1)

    chip_bits = []
    bit = 2
    while bit < n:
        chip_bits.append(bit)
        bit *= 2
    upward = chip_bits + [1]
    downward = chip_bits[::-1] + [1]

    qkv, out, up, down = [], [], [], []
    for layer in range(LAYERS):
        qkv.append(gather_pieces(w_qkv[layer], n, upward))
        out.append(gather_pieces(w_out[layer], n, downward))
        up.append(gather_pieces(w_up[layer], n, downward))
        down.append(gather_pieces(w_down[layer], n, upward))

    current = tokens.reshape(rows, width)
    base = current
    saved = []
    for layer in range(LAYERS):
        last = layer == LAYERS - 1
        q, k, v, ctx, lse, mid, low, n1, r1 = attend_forward(
            me_row, current, smalls[layer], key_mask, qkv[layer], out[layer], seqs
        )
        results = ffn_forward(
            me_row, mid, low, smalls[layer], up_bias_all[layer], valid, up[layer], down[layer], last
        )
        act, slope, n2, r2, current = results[:5]
        saved.append((base, q, k, v, ctx, lse, low, n1, r1, act, slope, n2, r2))
        if not last:
            base = results[5]
    outputs = current.reshape(seqs, seq, width)

    grad = cotangent.reshape(rows, width)
    grad_valid = valid
    shard_sums = [None] * LAYERS
    small_sums = [None] * LAYERS
    for layer in range(LAYERS - 1, -1, -1):
        base, q, k, v, ctx, lse, low, n1, r1, act, slope, n2, r2 = saved[layer]
        gs1, ga1, sums, up_sum, down_keep, down_send, up_keep, up_send = ffn_backward(
            me_row, grad, grad_valid, n2, r2, low, n1, r1, smalls[layer], act, slope, up[layer], down[layer]
        )
        grad, proj_sums, qkv_keep, qkv_send, out_keep, out_send = attend_backward(
            me_row, ga1, gs1, base, key_mask, q, k, v, ctx, lse, qkv[layer], out[layer], seqs,
            f32 if layer else bf16,
        )
        grad_valid = ones
        d_down = scatter_pieces(down_keep, down_send, n, chip_bits[::-1])
        d_up = scatter_pieces(up_keep, up_send, n, chip_bits)
        d_down, d_up = sum_replicas([d_down, d_up.reshape(-1, width)], rank, reps)
        d_qkv = scatter_pieces(qkv_keep, qkv_send, n, chip_bits[::-1])
        d_out = scatter_pieces(out_keep, out_send, n, chip_bits)
        d_qkv, d_out = sum_replicas([d_qkv.reshape(-1, width), d_out], rank, reps)
        d_up = d_up.reshape(units // width, per, width).transpose(1, 0, 2).reshape(per, units)
        d_qkv = d_qkv.reshape(3, per, width).transpose(1, 0, 2).reshape(per, 3 * width)
        shard_sums[layer] = (d_qkv, d_out, d_up, d_down)
        bias_sums = jnp.stack([proj_sums[0], proj_sums[1], sums[5], sums[2], sums[4], sums[1]])
        gain_sums = jnp.stack([sums[3], sums[0]])
        small_sums[layer] = (up_sum.reshape(n, units // n), bias_sums, gain_sums)
    grad_tokens = grad.reshape(seqs, seq, width)

    ups = jnp.stack([small_sums[layer][0] for layer in range(LAYERS)], axis=1).reshape(n, -1)
    bias_rows = jnp.stack([small_sums[layer][1] for layer in range(LAYERS)])
    bias_rows = bias_rows.reshape(LAYERS * 6, n, per).transpose(1, 0, 2).reshape(n, -1)
    gain_rows = jnp.stack([small_sums[layer][2] for layer in range(LAYERS)])
    gain_rows = gain_rows.reshape(LAYERS * 2, n, per).transpose(1, 0, 2).reshape(n, -1)
    small_total = jnp.concatenate([ups, bias_rows, gain_rows], axis=1)
    bit = 1
    while bit < n:
        small_total = small_total + swap(small_total, "fsdp", n, bit)
        bit *= 2
    mine = lax.dynamic_index_in_dim(small_total, me, 0, keepdims=True)
    bit = 1
    while bit < reps:
        mine = mine + swap(mine, "rep", reps, bit)
        bit *= 2
    mine = mine[0]
    grad_up_bias = mine[:cut_a].reshape(LAYERS, units // n)
    grad_biases = mine[cut_a:cut_b].reshape(LAYERS, 6, per)
    grad_gains = mine[cut_b:].reshape(LAYERS, 2, per)

    stacked = [jnp.stack([shard_sums[layer][member] for layer in range(LAYERS)]) for member in range(4)]
    return (outputs, grad_tokens, *stacked, grad_up_bias, grad_biases, grad_gains)


def solution(mesh):
    both = ("rep", "fsdp")
    placed = (
        P(both, None, None),
        P(both, None, None),
        P(both),
        P(both),
        P(None, "fsdp", None),
        P(None, "fsdp", None),
        P(None, "fsdp", None),
        P(None, "fsdp", None),
        P(None, "fsdp"),
        P(None, None, "fsdp"),
        P(None, None, "fsdp"),
    )
    return jax.shard_map(
        functools.partial(on_device, mesh.shape["fsdp"], mesh.shape["rep"]),
        mesh=mesh,
        in_specs=placed,
        out_specs=(
            P(both, None, None),
            P(both, None, None),
            P(None, "fsdp", None),
            P(None, "fsdp", None),
            P(None, "fsdp", None),
            P(None, "fsdp", None),
            P(None, "fsdp"),
            P(None, None, "fsdp"),
            P(None, None, "fsdp"),
        ),
        check_vma=False,
    )
```

```python
import functools

import jax
import jax.numpy as jnp
from jax import lax
from jax.experimental import pallas as pl
from jax.experimental.pallas import tpu as pltpu
from jax.sharding import PartitionSpec as P

HEAD = 64
LAYERS = 2
GROUP = 256
ROWS = 256
VMEM_BYTES = 60 * 1024 * 1024

epsilon = 1e-05
big_negative = -1000000000.0
root_half = 0.7071067811865476
inv_root_tau = 0.3989422804014327
f32 = jnp.float32
bf16 = jnp.bfloat16


def dot_nn(a, b):
    return lax.dot_general(a, b, (((1,), (0,)), ((), ())), preferred_element_type=f32)


def dot_nt(a, b):
    return lax.dot_general(a, b, (((1,), (1,)), ((), ())), preferred_element_type=f32)


def whole(shape):
    zeros = (0,) * len(shape)
    return pl.BlockSpec(shape, lambda *_: zeros, pipeline_mode=pl.Buffered(1))


def column_block(rows, width):
    return pl.BlockSpec((rows, width), lambda j, *_: (0, j))


ANY = pl.BlockSpec(memory_space=pl.ANY)


def flip(index, mask):
    bit = 1
    while bit <= mask:
        if mask & bit:
            index = index + bit - 2 * bit * ((index // bit) % 2)
        bit *= 2
    return index


def greet(n, bits):
    me = lax.axis_index("fsdp")
    barrier = pltpu.get_barrier_semaphore()
    for bit in bits:
        pl.semaphore_signal(barrier, inc=1, device_id={"fsdp": flip(me, bit)}, device_id_type=pl.DeviceIdType.MESH)
    pl.semaphore_wait(barrier, len(bits))


class Gather:
    def __init__(self, own, full, order, send_sems, recv_sems, local_sem):
        self.own, self.full, self.order = own, full, order
        self.send_sems, self.recv_sems, self.local_sem = send_sems, recv_sems, local_sem
        self.me = lax.axis_index("fsdp")
        self.depth = own.shape[0]

    def rows(self, mask):
        return self.full.at[pl.ds(pl.multiple_of(flip(self.me, mask) * self.depth, 16), self.depth), :]

    def round_masks(self, round_at):
        earlier = self.order[:round_at]
        masks = [0]
        for bit in earlier:
            masks += [mask | bit for mask in masks]
        return [mask | self.order[round_at] for mask in masks]

    def copy(self, mask):
        bit = [bit for bit in self.order if bit & mask][-1]
        held = mask ^ bit
        return pltpu.make_async_remote_copy(
            src_ref=self.own if held == 0 else self.rows(held),
            dst_ref=self.rows(held),
            send_sem=self.send_sems.at[mask],
            recv_sem=self.recv_sems.at[mask],
            device_id={"fsdp": flip(self.me, bit)},
            device_id_type=pl.DeviceIdType.MESH,
        )

    def begin(self, round_at):
        if round_at == 0:
            pltpu.make_async_copy(self.own, self.rows(0), self.local_sem).start()
        self.copy(self.order[round_at]).start()

    def onward(self, round_at):
        masks = self.round_masks(round_at)
        for mask in masks:
            self.copy(mask).wait_recv()
        for bit in self.order[round_at + 1 :]:
            for mask in masks:
                self.copy(mask | bit).start()

    def end(self):
        pltpu.make_async_copy(self.own, self.rows(0), self.local_sem).wait()
        for round_at in range(len(self.order)):
            for mask in self.round_masks(round_at):
                self.copy(mask).wait_send()


def begin_all(n, gathers):
    rounds = len(gathers[0].order)
    greet(n, gathers[0].order)
    for round_at in range(rounds):
        for gather in gathers:
            gather.begin(round_at)


def onward_all(gathers, round_at):
    for gather in gathers:
        gather.onward(round_at)


def end_all(gathers):
    for gather in gathers:
        gather.end()


def make_gathers(n, layer, shards, wholes, orders, sems):
    send_sems, recv_sems, local_sems = sems
    return [
        Gather(own.at[layer], full, order, send_sems.at[at], recv_sems.at[at], local_sems.at[at])
        for at, (own, full, order) in enumerate(zip(shards, wholes, orders))
    ]


def gather_sems(n, count):
    return [
        pltpu.SemaphoreType.DMA((count, n)),
        pltpu.SemaphoreType.DMA((count, n)),
        pltpu.SemaphoreType.DMA((count,)),
    ]


def whole_of(n, shard):
    return jax.ShapeDtypeStruct((shard.shape[1] * n, shard.shape[2]), shard.dtype)


def gather_kernel(n, layer, orders, *refs):
    count = len(orders)
    gathers = make_gathers(n, layer, refs[:count], refs[count : 2 * count], orders, refs[2 * count :])
    begin_all(n, gathers)
    for round_at in range(len(orders[0])):
        onward_all(gathers, round_at)
    end_all(gathers)


def gather_weights(n, layer, shards, orders, collective_id):
    return pl.pallas_call(
        functools.partial(gather_kernel, n, layer, orders),
        out_shape=tuple(whole_of(n, shard) for shard in shards),
        in_specs=[ANY] * len(shards),
        out_specs=tuple([ANY] * len(shards)),
        scratch_shapes=gather_sems(n, len(shards)),
        compiler_params=pltpu.CompilerParams(collective_id=collective_id, has_side_effects=True),
        name="gather_weights",
    )(*shards)


def norm_forward(total, gain, shift):
    middle = jnp.mean(total, axis=-1, keepdims=True)
    centred = total - middle
    spread = jnp.mean(centred * centred, axis=-1, keepdims=True)
    scaling = lax.rsqrt(spread + epsilon)
    normed = centred * scaling
    return normed * gain + shift, normed, scaling


def norm_backward(grad, normed, scaling, gain):
    scaled = grad * gain
    first = jnp.mean(scaled, axis=-1, keepdims=True)
    second = jnp.mean(scaled * normed, axis=-1, keepdims=True)
    return scaling * (scaled - first - normed * second)


def head_mask(shape, head):
    lanes = lax.broadcasted_iota(jnp.int32, shape, 1)
    return (lanes >= head * HEAD) & (lanes < (head + 1) * HEAD)


def attend_forward_kernel(n, seqs, layer, orders, x_ref, small_ref, mask_ref, qkv_ref, out_ref, *refs):
    count = len(orders)
    shards, refs = refs[:count], refs[count:]
    q_ref, k_ref, v_ref, ctx_ref, lse_ref, mid_ref, low_ref, n1_ref, r1_ref = refs[:9]
    wholes, refs = refs[9 : 9 + count], refs[9 + count :]
    base, w_qkv, w_out, acc, sems = refs[:5]
    gathers = make_gathers(n, layer, shards, wholes, orders, refs[5:])
    step, steps = pl.program_id(0), pl.num_programs(0)
    rows, width = x_ref.shape
    seq = rows // seqs
    heads = GROUP // HEAD
    qkv_copy = pltpu.make_async_copy(qkv_ref, w_qkv, sems.at[0])
    out_copy = pltpu.make_async_copy(out_ref, w_out, sems.at[1])

    @pl.when(step == 0)
    def _():
        qkv_copy.start()
        out_copy.start()
        begin_all(n, gathers)
        base[...] = x_ref[...].astype(bf16)
        qkv_copy.wait()
        out_copy.wait()

    columns = pl.multiple_of(step * GROUP, GROUP)
    q_bias = small_ref[0:1, pl.ds(columns, GROUP)]
    v_bias = small_ref[1:2, pl.ds(columns, GROUP)]

    def project(block, carry):
        at = pl.ds(pl.multiple_of(block * ROWS, ROWS), ROWS)
        low = base[at, :]
        q = dot_nn(low, w_qkv[:, pl.ds(columns, GROUP)])
        q_ref[at, :] = ((q + q_bias) * HEAD ** (-0.5)).astype(bf16)
        k = dot_nn(low, w_qkv[:, pl.ds(pl.multiple_of(width + columns, GROUP), GROUP)])
        k_ref[at, :] = k.astype(bf16)
        v = dot_nn(low, w_qkv[:, pl.ds(pl.multiple_of(2 * width + columns, GROUP), GROUP)])
        v_ref[at, :] = (v + v_bias).astype(bf16)
        return carry

    lax.fori_loop(0, rows // ROWS, project, 0)

    def attend(s, carry):
        at = pl.ds(pl.multiple_of(s * seq, seq), seq)
        q, k = q_ref[at, :], k_ref[at, :]
        v_turned = v_ref[at, :].T
        key_mask = mask_ref[at, :]
        parts = []
        for head in range(heads):
            q_head = jnp.where(head_mask(q.shape, head), q, jnp.zeros_like(q))
            scores = dot_nt(k, q_head) + key_mask
            peak = jnp.max(scores, axis=0, keepdims=True)
            raised = jnp.exp(scores - peak)
            total = jnp.sum(raised, axis=0, keepdims=True)
            mixed = dot_nn(v_turned[head * HEAD : (head + 1) * HEAD, :], raised.astype(bf16))
            parts.append((mixed / total).astype(bf16))
            lse_ref[0, pl.ds(s * heads + head, 1), :] = peak + jnp.log(total)
        ctx_ref[at, :] = jnp.concatenate(parts, axis=0).T
        return carry

    lax.fori_loop(0, seqs, attend, 0)

    @pl.when(step == 1)
    def _():
        onward_all(gathers, 0)

    def mix(block, carry):
        at = pl.ds(pl.multiple_of(block * ROWS, ROWS), ROWS)
        term = dot_nn(ctx_ref[at, :], w_out[pl.ds(columns, GROUP), :])

        @pl.when(step == 0)
        def _():
            acc[at, :] = term

        @pl.when(step > 0)
        def _():
            acc[at, :] += term

        @pl.when(step == steps - 1)
        def _():
            total = x_ref[at, :].astype(f32) + acc[at, :] + small_ref[2:3, :]
            mid, normed, scaling = norm_forward(total, small_ref[6:7, :], small_ref[4:5, :])
            mid_ref[at, :] = mid
            low_ref[at, :] = mid.astype(bf16)
            n1_ref[at, :] = normed.astype(bf16)
            r1_ref[at, :] = scaling

        return carry

    lax.fori_loop(0, rows // ROWS, mix, 0)

    @pl.when(step == steps - 1)
    def _():
        for round_at in range(1, len(orders[0])):
            onward_all(gathers, round_at)
        end_all(gathers)


def attend_forward(n, x, small, key_mask, w_qkv, w_out, seqs, layer, shards, orders, collective_id):
    rows, width = x.shape
    steps = width // GROUP
    seq = rows // seqs
    wide = jax.ShapeDtypeStruct((rows, width), bf16)
    heads = GROUP // HEAD
    return pl.pallas_call(
        functools.partial(attend_forward_kernel, n, seqs, layer, orders),
        out_shape=(
            wide,
            wide,
            wide,
            wide,
            jax.ShapeDtypeStruct((steps, seqs * heads, seq), f32),
            jax.ShapeDtypeStruct((rows, width), f32),
            wide,
            wide,
            jax.ShapeDtypeStruct((rows, 1), f32),
        )
        + tuple(whole_of(n, shard) for shard in shards),
        grid_spec=pltpu.PrefetchScalarGridSpec(
            num_scalar_prefetch=0,
            grid=(steps,),
            in_specs=[whole((rows, width)), whole(small.shape), whole((rows, 1))] + [ANY] * (2 + len(shards)),
            out_specs=[column_block(rows, GROUP)] * 4
            + [
                pl.BlockSpec((1, seqs * heads, seq), lambda j, *_: (j, 0, 0)),
                whole((rows, width)),
                whole((rows, width)),
                whole((rows, width)),
                whole((rows, 1)),
            ]
            + [ANY] * len(shards),
            scratch_shapes=[
                pltpu.VMEM((rows, width), bf16),
                pltpu.VMEM((width, 3 * width), bf16),
                pltpu.VMEM((width, width), bf16),
                pltpu.VMEM((rows, width), f32),
                pltpu.SemaphoreType.DMA((2,)),
            ]
            + gather_sems(n, len(shards)),
        ),
        compiler_params=pltpu.CompilerParams(
            dimension_semantics=("arbitrary",),
            vmem_limit_bytes=VMEM_BYTES,
            collective_id=collective_id,
            has_side_effects=True,
        ),
        cost_estimate=cost(8 * rows * width * width + 16 * rows * seq * width, 20 * rows * width),
        name="attend_forward",
    )(x, small, key_mask, w_qkv, w_out, *shards)


def ffn_forward_kernel(n, last, layer, orders, mid_ref, low_ref, small_ref, up_bias_ref, valid_ref, up_ref, down_ref, *refs):
    count = len(orders)
    shards, refs = refs[:count], refs[count:]
    act_ref, slope_ref, n2_ref, r2_ref, hid_ref = refs[:5]
    refs = refs[5:]
    if not last:
        hid_low_ref, refs = refs[0], refs[1:]
    wholes, refs = refs[:count], refs[count:]
    w_up, w_down, acc, sems = refs[:4]
    gathers = make_gathers(n, layer, shards, wholes, orders, refs[4:]) if count else []
    step, steps = pl.program_id(0), pl.num_programs(0)
    rows, width = mid_ref.shape
    chunk = act_ref.shape[1]
    up_copy = pltpu.make_async_copy(up_ref, w_up, sems.at[0])
    down_copy = pltpu.make_async_copy(down_ref, w_down, sems.at[1])

    @pl.when(step == 0)
    def _():
        up_copy.start()
        down_copy.start()
        if gathers:
            begin_all(n, gathers)
        up_copy.wait()
        down_copy.wait()

    if gathers:

        @pl.when(step == 1)
        def _():
            onward_all(gathers, 0)

        @pl.when(step == 3)
        def _():
            onward_all(gathers, 1)

    columns = pl.multiple_of(step * chunk, chunk)
    tile = 256

    def block_step(block, carry):
        at = pl.ds(pl.multiple_of(block * ROWS, ROWS), ROWS)
        low = low_ref[at, :]
        for part in range(chunk // tile):
            inside = slice(part * tile, (part + 1) * tile)
            at_units = pl.ds(pl.multiple_of(columns + part * tile, tile), tile)
            pre = dot_nn(low, w_up[:, at_units]) + up_bias_ref[:, inside]
            share = 0.5 * (1.0 + lax.erf(pre * root_half))
            act_ref[at, inside] = (pre * share).astype(bf16)
            density = inv_root_tau * jnp.exp(-0.5 * pre * pre)
            slope_ref[at, inside] = (share + pre * density).astype(bf16)
        term = dot_nn(act_ref[at, :], w_down[pl.ds(columns, chunk), :])

        @pl.when(step == 0)
        def _():
            acc[at, :] = term

        @pl.when(step > 0)
        def _():
            acc[at, :] += term

        @pl.when(step == steps - 1)
        def _():
            total = mid_ref[at, :] + acc[at, :] + small_ref[3:4, :]
            hidden, normed, scaling = norm_forward(total, small_ref[7:8, :], small_ref[5:6, :])
            n2_ref[at, :] = normed.astype(bf16)
            r2_ref[at, :] = scaling
            if last:
                hid_ref[at, :] = (hidden * valid_ref[at, :]).astype(bf16)
            else:
                hid_ref[at, :] = hidden
                hid_low_ref[at, :] = hidden.astype(bf16)

        return carry

    lax.fori_loop(0, rows // ROWS, block_step, 0)

    if gathers:

        @pl.when(step == steps - 1)
        def _():
            for round_at in range(2, len(orders[0])):
                onward_all(gathers, round_at)
            end_all(gathers)


def ffn_forward(n, mid, low, small, up_bias, valid, w_up, w_down, last, layer, shards, orders, collective_id):
    rows, width = mid.shape
    units = up_bias.shape[1]
    chunk = width
    steps = units // chunk
    out_shape = [
        jax.ShapeDtypeStruct((rows, units), bf16),
        jax.ShapeDtypeStruct((rows, units), bf16),
        jax.ShapeDtypeStruct((rows, width), bf16),
        jax.ShapeDtypeStruct((rows, 1), f32),
        jax.ShapeDtypeStruct((rows, width), bf16 if last else f32),
    ]
    out_specs = [column_block(rows, chunk)] * 2 + [
        whole((rows, width)),
        whole((rows, 1)),
        whole((rows, width)),
    ]
    if not last:
        out_shape.append(jax.ShapeDtypeStruct((rows, width), bf16))
        out_specs.append(whole((rows, width)))
    out_shape += [whole_of(n, shard) for shard in shards]
    out_specs += [ANY] * len(shards)
    if shards:
        params = pltpu.CompilerParams(
            dimension_semantics=("arbitrary",),
            vmem_limit_bytes=VMEM_BYTES,
            collective_id=collective_id,
            has_side_effects=True,
        )
    else:
        params = pltpu.CompilerParams(dimension_semantics=("arbitrary",), vmem_limit_bytes=VMEM_BYTES)
    return pl.pallas_call(
        functools.partial(ffn_forward_kernel, n, last, layer, orders),
        out_shape=tuple(out_shape),
        grid_spec=pltpu.PrefetchScalarGridSpec(
            num_scalar_prefetch=0,
            grid=(steps,),
            in_specs=[
                whole((rows, width)),
                whole((rows, width)),
                whole(small.shape),
                column_block(1, chunk),
                whole((rows, 1)),
            ]
            + [ANY] * (2 + len(shards)),
            out_specs=out_specs,
            scratch_shapes=[
                pltpu.VMEM((width, units), bf16),
                pltpu.VMEM((units, width), bf16),
                pltpu.VMEM((rows, width), f32),
                pltpu.SemaphoreType.DMA((2,)),
            ]
            + (gather_sems(n, len(shards)) if shards else []),
        ),
        compiler_params=params,
        cost_estimate=cost(8 * rows * width * units, 8 * rows * units),
        name="ffn_forward",
    )(mid, low, small, up_bias, valid, w_up, w_down, *shards)


def shard_copies(n, me, source_of, keep_of, send_of, sems):
    def each(start):
        for owner in range(n):
            mask = me ^ owner
            place = mask // 2

            @pl.when(mask % 2 == 0)
            def _():
                copy = pltpu.make_async_copy(source_of(owner), keep_of(place), sems.at[owner])
                copy.start() if start else copy.wait()

            @pl.when(mask % 2 == 1)
            def _():
                copy = pltpu.make_async_copy(source_of(owner), send_of(place), sems.at[owner])
                copy.start() if start else copy.wait()

    return each


def ffn_backward_kernel(n, me_ref, g_ref, valid_ref, n2_ref, r2_ref, low_ref, n1_ref, r1_ref, small_ref, act_ref, slope_ref, *refs):
    up_ref, down_ref = refs[:2]
    gs1_ref, ga1_ref, sums_ref, up_sum_ref, down_keep, down_send, up_keep, up_send = refs[2:10]
    w_up, w_down, gs2, gffn, gpre, acc, low_turned, d_down, d_up, sems, out_sems = refs[10:]
    step, steps = pl.program_id(0), pl.num_programs(0)
    me = me_ref[0]
    rows, width = gs2.shape
    chunk = act_ref.shape[1]
    per_down = down_keep.shape[1]
    per_up = up_keep.shape[2]
    tile = 256
    up_copies = [pltpu.make_async_copy(up_ref, w_up, sems.at[0])]
    down_copies = [pltpu.make_async_copy(down_ref, w_down, sems.at[1])]

    @pl.when(step == 0)
    def _():
        for copy in down_copies:
            copy.start()
        for copy in up_copies:
            copy.start()
        sums_ref[...] = jnp.zeros_like(sums_ref)

        def prepare(block, carry):
            at = pl.ds(pl.multiple_of(block * ROWS, ROWS), ROWS)
            grad = g_ref[at, :].astype(f32) * valid_ref[at, :]
            normed = n2_ref[at, :].astype(f32)
            summed = norm_backward(grad, normed, r2_ref[at, :], small_ref[7:8, :])
            gs2[at, :] = summed
            low = summed.astype(bf16)
            gffn[at, :] = low
            sums_ref[0:1, :] += jnp.sum(grad * normed, axis=0, keepdims=True)
            sums_ref[1:2, :] += jnp.sum(grad, axis=0, keepdims=True)
            sums_ref[2:3, :] += jnp.sum(low.astype(f32), axis=0, keepdims=True)
            low_turned[:, at] = low_ref[at, :].T
            return carry

        lax.fori_loop(0, rows // ROWS, prepare, 0)
        for copy in down_copies:
            copy.wait()
        for copy in up_copies:
            copy.wait()

    columns = pl.multiple_of(step * chunk, chunk)
    up_sum_ref[...] = jnp.zeros_like(up_sum_ref)

    def through(block, carry):
        at = pl.ds(pl.multiple_of(block * ROWS, ROWS), ROWS)
        grad = gffn[at, :]
        for part in range(chunk // tile):
            inside = slice(part * tile, (part + 1) * tile)
            at_units = pl.ds(pl.multiple_of(columns + part * tile, tile), tile)
            grad_act = dot_nt(grad, w_down[at_units, :])
            low = (grad_act * slope_ref[at, inside].astype(f32)).astype(bf16)
            gpre[at, inside] = low
            up_sum_ref[:, inside] += jnp.sum(low.astype(f32), axis=0, keepdims=True)
        term = dot_nt(gpre[at, :], w_up[:, pl.ds(columns, chunk)])

        @pl.when(step == 0)
        def _():
            acc[at, :] = term

        @pl.when(step > 0)
        def _():
            acc[at, :] += term

        return carry

    lax.fori_loop(0, rows // ROWS, through, 0)

    def down_out(which):
        def run(start):
            for local in range(chunk // per_down):
                owner = which * (chunk // per_down) + local
                mask = me ^ owner
                source = d_down.at[pl.ds(local * per_down, per_down), :]
                place = mask // 2

                @pl.when(mask % 2 == 0)
                def _():
                    copy = pltpu.make_async_copy(source, down_keep.at[place], out_sems.at[0, local])
                    copy.start() if start else copy.wait()

                @pl.when(mask % 2 == 1)
                def _():
                    copy = pltpu.make_async_copy(source, down_send.at[place], out_sems.at[0, local])
                    copy.start() if start else copy.wait()

        return run

    def up_out(which):
        return shard_copies(
            n,
            me,
            lambda owner: d_up.at[pl.ds(owner * per_up, per_up), :],
            lambda place: up_keep.at[place, which],
            lambda place: up_send.at[place, which],
            out_sems.at[1],
        )

    @pl.when(step > 0)
    def _():
        down_out(step - 1)(False)

    def down_part(part, carry):
        at = pl.ds(pl.multiple_of(part * tile, tile), tile)
        turned = act_ref[:, at].T
        d_down[at, :] = dot_nn(turned, gffn[...]).astype(bf16)
        return carry

    lax.fori_loop(0, chunk // tile, down_part, 0)
    down_out(step)(True)

    @pl.when(step > 0)
    def _():
        up_out(step - 1)(False)

    def up_part(part, carry):
        at = pl.ds(pl.multiple_of(part * tile, tile), tile)
        d_up[at, :] = dot_nn(low_turned[at, :], gpre[...]).astype(bf16)
        return carry

    lax.fori_loop(0, width // tile, up_part, 0)
    up_out(step)(True)

    @pl.when(step == steps - 1)
    def _():
        def finish(block, carry):
            at = pl.ds(pl.multiple_of(block * ROWS, ROWS), ROWS)
            grad = gs2[at, :] + acc[at, :]
            normed = n1_ref[at, :].astype(f32)
            summed = norm_backward(grad, normed, r1_ref[at, :], small_ref[6:7, :])
            gs1_ref[at, :] = summed
            low = summed.astype(bf16)
            ga1_ref[at, :] = low
            sums_ref[3:4, :] += jnp.sum(grad * normed, axis=0, keepdims=True)
            sums_ref[4:5, :] += jnp.sum(grad, axis=0, keepdims=True)
            sums_ref[5:6, :] += jnp.sum(low.astype(f32), axis=0, keepdims=True)
            return carry

        lax.fori_loop(0, rows // ROWS, finish, 0)
        down_out(step)(False)
        up_out(step)(False)


def ffn_backward(me, grad, valid, n2, r2, low, n1, r1, small, act, slope, w_up, w_down, n):
    rows, width = grad.shape
    units = act.shape[1]
    chunk = width
    steps = units // chunk
    chips = n // 2
    down_half = jax.ShapeDtypeStruct((chips, units // n, width), bf16)
    up_half = jax.ShapeDtypeStruct((chips, steps, width // n, chunk), bf16)
    return pl.pallas_call(
        functools.partial(ffn_backward_kernel, n),
        out_shape=(
            jax.ShapeDtypeStruct((rows, width), f32),
            jax.ShapeDtypeStruct((rows, width), bf16),
            jax.ShapeDtypeStruct((8, width), f32),
            jax.ShapeDtypeStruct((1, units), f32),
            down_half,
            down_half,
            up_half,
            up_half,
        ),
        grid_spec=pltpu.PrefetchScalarGridSpec(
            num_scalar_prefetch=1,
            grid=(steps,),
            in_specs=[
                whole((rows, width)),
                whole((rows, 1)),
                whole((rows, width)),
                whole((rows, 1)),
                whole((rows, width)),
                whole((rows, width)),
                whole((rows, 1)),
                whole(small.shape),
                column_block(rows, chunk),
                column_block(rows, chunk),
            ]
            + [ANY] * 2,
            out_specs=[
                whole((rows, width)),
                whole((rows, width)),
                whole((8, width)),
                column_block(1, chunk),
            ]
            + [ANY] * 4,
            scratch_shapes=[
                pltpu.VMEM((width, units), bf16),
                pltpu.VMEM((units, width), bf16),
                pltpu.VMEM((rows, width), f32),
                pltpu.VMEM((rows, width), bf16),
                pltpu.VMEM((rows, chunk), bf16),
                pltpu.VMEM((rows, width), f32),
                pltpu.VMEM((width, rows), bf16),
                pltpu.VMEM((chunk, width), bf16),
                pltpu.VMEM((width, chunk), bf16),
                pltpu.SemaphoreType.DMA((2,)),
                pltpu.SemaphoreType.DMA((2, n)),
            ],
        ),
        compiler_params=pltpu.CompilerParams(
            dimension_semantics=("arbitrary",), vmem_limit_bytes=VMEM_BYTES
        ),
        cost_estimate=cost(10 * rows * width * units, 8 * rows * units),
        name="ffn_backward",
    )(me, grad, valid, n2, r2, low, n1, r1, small, act, slope, w_up, w_down)


def attend_backward_kernel(n, seqs, me_ref, ga_ref, gs_ref, base_ref, mask_ref, q_ref, k_ref, v_ref, ctx_ref, lse_ref, *refs):
    qkv_ref, out_ref = refs[:2]
    gh_ref, sums_ref, qkv_keep, qkv_send, out_keep, out_send = refs[2:8]
    w_qkv, w_out, acc, base_turned, gctx, gproj, d_qkv, d_out, p_all, ds_all, sems, out_sems = refs[8:]
    step, steps = pl.program_id(0), pl.num_programs(0)
    me = me_ref[0]
    rows, width = ga_ref.shape
    seq = rows // seqs
    heads = GROUP // HEAD
    per = width // n
    tile = 256
    qkv_copies = [pltpu.make_async_copy(qkv_ref, w_qkv, sems.at[0])]
    out_copies = [pltpu.make_async_copy(out_ref, w_out, sems.at[1])]

    @pl.when(step == 0)
    def _():
        for copy in out_copies:
            copy.start()
        for copy in qkv_copies:
            copy.start()

        def turn(block, carry):
            at = pl.ds(pl.multiple_of(block * ROWS, ROWS), ROWS)
            base_turned[:, at] = base_ref[at, :].T
            return carry

        lax.fori_loop(0, rows // ROWS, turn, 0)
        for copy in out_copies:
            copy.wait()
        for copy in qkv_copies:
            copy.wait()

    columns = pl.multiple_of(step * GROUP, GROUP)

    def through(block, carry):
        at = pl.ds(pl.multiple_of(block * ROWS, ROWS), ROWS)
        gctx[at, :] = dot_nt(ga_ref[at, :], w_out[pl.ds(columns, GROUP), :]).astype(bf16)
        return carry

    lax.fori_loop(0, rows // ROWS, through, 0)
    d_out[pl.ds(columns, GROUP), :] = dot_nn(ctx_ref[...].T, ga_ref[...]).astype(bf16)

    def attend(s, carry):
        at = pl.ds(pl.multiple_of(s * seq, seq), seq)
        q, k, v, grad = q_ref[at, :], k_ref[at, :], v_ref[at, :], gctx[at, :]
        k_turned = k.T
        key_mask = mask_ref[at, :]
        parts, q_heads, g_heads = [], [], []
        for head in range(heads):
            inside = head_mask(q.shape, head)
            q_head = jnp.where(inside, q, jnp.zeros_like(q))
            g_head = jnp.where(inside, grad, jnp.zeros_like(grad))
            scores = dot_nt(k, q_head) + key_mask
            attention = jnp.exp(scores - lse_ref[0, pl.ds(s * heads + head, 1), :])
            weighted = attention * dot_nt(v, g_head)
            inner = jnp.sum(weighted, axis=0, keepdims=True)
            grad_scores = (weighted - attention * inner).astype(bf16)
            here = slice(head * seq, (head + 1) * seq)
            p_all[:, here] = attention.astype(bf16)
            ds_all[:, here] = grad_scores
            turned = dot_nn(k_turned[head * HEAD : (head + 1) * HEAD, :], grad_scores)
            parts.append(turned.astype(bf16) * HEAD ** (-0.5))
            q_heads.append(q_head)
            g_heads.append(g_head)
        gproj[at, 0:GROUP] = jnp.concatenate(parts, axis=0).T
        gproj[at, GROUP : 2 * GROUP] = dot_nn(ds_all[...], jnp.concatenate(q_heads, axis=0)).astype(bf16)
        gproj[at, 2 * GROUP : 3 * GROUP] = dot_nn(p_all[...], jnp.concatenate(g_heads, axis=0)).astype(bf16)
        return carry

    lax.fori_loop(0, seqs, attend, 0)
    sums_ref[...] = jnp.zeros_like(sums_ref)

    def onward(block, carry):
        at = pl.ds(pl.multiple_of(block * ROWS, ROWS), ROWS)
        term = dot_nt(gproj[at, 0:GROUP], w_qkv[:, pl.ds(columns, GROUP)])
        term += dot_nt(gproj[at, GROUP : 2 * GROUP], w_qkv[:, pl.ds(pl.multiple_of(width + columns, GROUP), GROUP)])
        term += dot_nt(gproj[at, 2 * GROUP : 3 * GROUP], w_qkv[:, pl.ds(pl.multiple_of(2 * width + columns, GROUP), GROUP)])
        sums_ref[0:1, :] += jnp.sum(gproj[at, 0:GROUP].astype(f32), axis=0, keepdims=True)
        sums_ref[1:2, :] += jnp.sum(gproj[at, 2 * GROUP : 3 * GROUP].astype(f32), axis=0, keepdims=True)

        @pl.when(step == 0)
        def _():
            acc[at, :] = gs_ref[at, :] + term

        @pl.when(step > 0)
        def _():
            acc[at, :] += term

        @pl.when(step == steps - 1)
        def _():
            gh_ref[at, :] = acc[at, :].astype(gh_ref.dtype)

        return carry

    lax.fori_loop(0, rows // ROWS, onward, 0)

    def qkv_out(which, start):
        for part in range(3):
            at = pl.ds(pl.multiple_of(which * GROUP, GROUP), GROUP)
            shard_copies(
                n,
                me,
                lambda owner: d_qkv.at[pl.ds(owner * per, per), pl.ds(part * GROUP, GROUP)],
                lambda place: qkv_keep.at[place, part, :, at],
                lambda place: qkv_send.at[place, part, :, at],
                out_sems.at[part],
            )(start)

    @pl.when(step > 0)
    def _():
        qkv_out(step - 1, False)

    def weight_part(part, carry):
        at = pl.ds(pl.multiple_of(part * tile, tile), tile)
        d_qkv[at, :] = dot_nn(base_turned[at, :], gproj[...]).astype(bf16)
        return carry

    lax.fori_loop(0, width // tile, weight_part, 0)
    qkv_out(step, True)

    @pl.when(step == steps - 1)
    def _():
        out_copy = shard_copies(
            n,
            me,
            lambda owner: d_out.at[pl.ds(owner * per, per), :],
            lambda place: out_keep.at[place],
            lambda place: out_send.at[place],
            out_sems.at[3],
        )
        out_copy(True)
        qkv_out(step, False)
        out_copy(False)


def attend_backward(me, ga, gs, base, key_mask, q, k, v, ctx, lse, w_qkv, w_out, seqs, out_type, n):
    rows, width = ga.shape
    steps = width // GROUP
    seq = rows // seqs
    heads = GROUP // HEAD
    chips = n // 2
    qkv_half = jax.ShapeDtypeStruct((chips, 3, width // n, width), bf16)
    out_half = jax.ShapeDtypeStruct((chips, width // n, width), bf16)
    return pl.pallas_call(
        functools.partial(attend_backward_kernel, n, seqs),
        out_shape=(
            jax.ShapeDtypeStruct((rows, width), out_type),
            jax.ShapeDtypeStruct((8, width), f32),
            qkv_half,
            qkv_half,
            out_half,
            out_half,
        ),
        grid_spec=pltpu.PrefetchScalarGridSpec(
            num_scalar_prefetch=1,
            grid=(steps,),
            in_specs=[whole((rows, width))] * 3
            + [whole((rows, 1))]
            + [column_block(rows, GROUP)] * 4
            + [pl.BlockSpec((1, seqs * heads, seq), lambda j, *_: (j, 0, 0))]
            + [ANY] * 2,
            out_specs=[whole((rows, width)), column_block(8, GROUP)] + [ANY] * 4,
            scratch_shapes=[
                pltpu.VMEM((width, 3 * width), bf16),
                pltpu.VMEM((width, width), bf16),
                pltpu.VMEM((rows, width), f32),
                pltpu.VMEM((width, rows), bf16),
                pltpu.VMEM((rows, GROUP), bf16),
                pltpu.VMEM((rows, 3 * GROUP), bf16),
                pltpu.VMEM((width, 3 * GROUP), bf16),
                pltpu.VMEM((width, width), bf16),
                pltpu.VMEM((seq, heads * seq), bf16),
                pltpu.VMEM((seq, heads * seq), bf16),
                pltpu.SemaphoreType.DMA((2,)),
                pltpu.SemaphoreType.DMA((4, n)),
            ],
        ),
        compiler_params=pltpu.CompilerParams(
            dimension_semantics=("arbitrary",), vmem_limit_bytes=VMEM_BYTES
        ),
        cost_estimate=cost(16 * rows * width * width + 40 * rows * seq * width, 20 * rows * width),
        name="attend_backward",
    )(me, ga, gs, base, key_mask, q, k, v, ctx, lse, w_qkv, w_out)


def cost(flops, moved):
    return pl.CostEstimate(flops=int(flops), bytes_accessed=int(moved), transcendentals=0)


def swap(array, axis, count, mask):
    return lax.ppermute(array, axis, [(i, i ^ mask) for i in range(count)])


def scatter_pieces(keep, send, n, bits):
    other = swap(send, "fsdp", n, 1)
    terms = {place: [keep[place], other[place]] for place in range(n // 2)}

    def total(items):
        return sum(item.astype(f32) for item in items)

    for bit in bits:
        half = bit // 2
        leaving = [place for place in sorted(terms) if place & half]
        packed = jnp.stack([total(terms[place]).astype(bf16) for place in leaving])
        arrived = swap(packed, "fsdp", n, bit)
        for slot, place in enumerate(leaving):
            terms[place ^ half].append(arrived[slot])
            del terms[place]
    return total(terms[0])


def sum_replicas(shards, rank, count):
    def parts_of(array, index):
        split = array.reshape((count, array.shape[0] // count) + array.shape[1:])
        return lax.dynamic_index_in_dim(split, index, 0, keepdims=False)

    def packed(index):
        return jnp.concatenate([parts_of(array, index) for array in shards], axis=0)

    total = packed(rank)
    for mask in range(1, count):
        total = total + swap(packed(rank ^ mask).astype(bf16), "rep", count, mask).astype(f32)
    low = total.astype(bf16)
    pieces = jnp.stack([low] + [swap(low, "rep", count, mask) for mask in range(1, count)])
    ordered = [lax.dynamic_index_in_dim(pieces, rank ^ place, 0, keepdims=False) for place in range(count)]
    results = []
    start = 0
    for array in shards:
        size = array.shape[0] // count
        rows = [piece[start : start + size] for piece in ordered]
        results.append(jnp.concatenate(rows, axis=0).astype(f32))
        start += size
    return results


def gather_small(own, n, me):
    array = own[None]
    bit = 1
    while bit < n:
        other = swap(array, "fsdp", n, bit)
        upper = (me // bit) % 2 == 1
        array = jnp.concatenate([jnp.where(upper, other, array), jnp.where(upper, array, other)], axis=0)
        bit *= 2
    return array


def on_device(n, reps, tokens, cotangent, lengths, live_batches, w_qkv, w_out, w_up, w_down, up_bias, biases, norm_gains):
    seqs, seq, width = tokens.shape
    rows = seqs * seq
    units = w_up.shape[2]
    per = width // n
    me = lax.axis_index("fsdp").astype(jnp.int32)
    rank = lax.axis_index("rep").astype(jnp.int32)
    me_row = me[None]

    places = jnp.arange(seq, dtype=jnp.int32)
    inside = places[None, :] < lengths[:, None]
    alive = jnp.arange(seqs, dtype=jnp.int32) < live_batches[0]
    key_mask = jnp.where(inside, 0.0, big_negative).astype(f32).reshape(rows, 1)
    valid = jnp.where(inside & alive[:, None], 1.0, 0.0).astype(f32).reshape(rows, 1)
    ones = jnp.ones((rows, 1), f32)

    own_small = jnp.concatenate([up_bias.reshape(-1), biases.reshape(-1), norm_gains.reshape(-1)])
    small_all = gather_small(own_small, n, me)
    cut_a = LAYERS * units // n
    cut_b = cut_a + LAYERS * 6 * per
    up_bias_all = small_all[:, :cut_a].reshape(n, LAYERS, units // n).transpose(1, 0, 2).reshape(LAYERS, 1, units)
    bias_all = small_all[:, cut_a:cut_b].reshape(n, LAYERS, 6, per).transpose(1, 2, 0, 3).reshape(LAYERS, 6, width)
    gain_all = small_all[:, cut_b:].reshape(n, LAYERS, 2, per).transpose(1, 2, 0, 3).reshape(LAYERS, 2, width)
    smalls = jnp.concatenate([bias_all, gain_all], axis=1)

    chip_bits = []
    bit = 2
    while bit < n:
        chip_bits.append(bit)
        bit *= 2
    upward = tuple(chip_bits + [1])
    downward = tuple(chip_bits[::-1] + [1])

    attend_orders, ffn_orders = (upward, downward), (downward, upward)
    qkv, out, up, down = [None] * LAYERS, [None] * LAYERS, [None] * LAYERS, [None] * LAYERS
    qkv[0], out[0] = gather_weights(n, 0, (w_qkv, w_out), attend_orders, 0)

    current = tokens.reshape(rows, width)
    base = current
    saved = []
    for layer in range(LAYERS):
        last = layer == LAYERS - 1
        q, k, v, ctx, lse, mid, low, n1, r1, up[layer], down[layer] = attend_forward(
            n, current, smalls[layer], key_mask, qkv[layer], out[layer], seqs,
            layer, (w_up, w_down), ffn_orders, 1 + 2 * layer,
        )
        results = ffn_forward(
            n, mid, low, smalls[layer], up_bias_all[layer], valid, up[layer], down[layer], last,
            layer + 1, () if last else (w_qkv, w_out), () if last else attend_orders, 2 + 2 * layer,
        )
        act, slope, n2, r2, current = results[:5]
        saved.append((base, q, k, v, ctx, lse, low, n1, r1, act, slope, n2, r2))
        if not last:
            base, qkv[layer + 1], out[layer + 1] = results[5:]
    outputs = current.reshape(seqs, seq, width)

    grad = cotangent.reshape(rows, width)
    grad_valid = valid
    shard_sums = [None] * LAYERS
    small_sums = [None] * LAYERS
    for layer in range(LAYERS - 1, -1, -1):
        base, q, k, v, ctx, lse, low, n1, r1, act, slope, n2, r2 = saved[layer]
        gs1, ga1, sums, up_sum, down_keep, down_send, up_keep, up_send = ffn_backward(
            me_row, grad, grad_valid, n2, r2, low, n1, r1, smalls[layer], act, slope, up[layer], down[layer], n
        )
        grad, proj_sums, qkv_keep, qkv_send, out_keep, out_send = attend_backward(
            me_row, ga1, gs1, base, key_mask, q, k, v, ctx, lse, qkv[layer], out[layer], seqs,
            f32 if layer else bf16, n,
        )
        grad_valid = ones
        d_down = scatter_pieces(down_keep, down_send, n, chip_bits[::-1])
        d_up = scatter_pieces(up_keep, up_send, n, chip_bits)
        d_down, d_up = sum_replicas([d_down, d_up.reshape(-1, width)], rank, reps)
        d_qkv = scatter_pieces(qkv_keep, qkv_send, n, chip_bits[::-1])
        d_out = scatter_pieces(out_keep, out_send, n, chip_bits)
        d_qkv, d_out = sum_replicas([d_qkv.reshape(-1, width), d_out], rank, reps)
        d_up = d_up.reshape(units // width, per, width).transpose(1, 0, 2).reshape(per, units)
        d_qkv = d_qkv.reshape(3, per, width).transpose(1, 0, 2).reshape(per, 3 * width)
        shard_sums[layer] = (d_qkv, d_out, d_up, d_down)
        bias_sums = jnp.stack([proj_sums[0], proj_sums[1], sums[5], sums[2], sums[4], sums[1]])
        gain_sums = jnp.stack([sums[3], sums[0]])
        small_sums[layer] = (up_sum.reshape(n, units // n), bias_sums, gain_sums)
    grad_tokens = grad.reshape(seqs, seq, width)

    ups = jnp.stack([small_sums[layer][0] for layer in range(LAYERS)], axis=1).reshape(n, -1)
    bias_rows = jnp.stack([small_sums[layer][1] for layer in range(LAYERS)])
    bias_rows = bias_rows.reshape(LAYERS * 6, n, per).transpose(1, 0, 2).reshape(n, -1)
    gain_rows = jnp.stack([small_sums[layer][2] for layer in range(LAYERS)])
    gain_rows = gain_rows.reshape(LAYERS * 2, n, per).transpose(1, 0, 2).reshape(n, -1)
    small_total = jnp.concatenate([ups, bias_rows, gain_rows], axis=1)
    bit = 1
    while bit < n:
        small_total = small_total + swap(small_total, "fsdp", n, bit)
        bit *= 2
    mine = lax.dynamic_index_in_dim(small_total, me, 0, keepdims=True)
    bit = 1
    while bit < reps:
        mine = mine + swap(mine, "rep", reps, bit)
        bit *= 2
    mine = mine[0]
    grad_up_bias = mine[:cut_a].reshape(LAYERS, units // n)
    grad_biases = mine[cut_a:cut_b].reshape(LAYERS, 6, per)
    grad_gains = mine[cut_b:].reshape(LAYERS, 2, per)

    stacked = [jnp.stack([shard_sums[layer][member] for layer in range(LAYERS)]) for member in range(4)]
    return (outputs, grad_tokens, *stacked, grad_up_bias, grad_biases, grad_gains)


def solution(mesh):
    both = ("rep", "fsdp")
    placed = (
        P(both, None, None),
        P(both, None, None),
        P(both),
        P(both),
        P(None, "fsdp", None),
        P(None, "fsdp", None),
        P(None, "fsdp", None),
        P(None, "fsdp", None),
        P(None, "fsdp"),
        P(None, None, "fsdp"),
        P(None, None, "fsdp"),
    )
    return jax.shard_map(
        functools.partial(on_device, mesh.shape["fsdp"], mesh.shape["rep"]),
        mesh=mesh,
        in_specs=placed,
        out_specs=(
            P(both, None, None),
            P(both, None, None),
            P(None, "fsdp", None),
            P(None, "fsdp", None),
            P(None, "fsdp", None),
            P(None, "fsdp", None),
            P(None, "fsdp"),
            P(None, None, "fsdp"),
            P(None, None, "fsdp"),
        ),
        check_vma=False,
    )
```

```python
import functools

import jax
import jax.numpy as jnp
from jax import lax
from jax.experimental import pallas as pl
from jax.experimental.pallas import tpu as pltpu
from jax.sharding import PartitionSpec as P

HEAD = 64
LAYERS = 2
GROUP = 256
ROWS = 256
VMEM_BYTES = 60 * 1024 * 1024

epsilon = 1e-05
big_negative = -1000000000.0
root_half = 0.7071067811865476
inv_root_tau = 0.3989422804014327
f32 = jnp.float32
bf16 = jnp.bfloat16


def dot_nn(a, b):
    return lax.dot_general(a, b, (((1,), (0,)), ((), ())), preferred_element_type=f32)


def dot_nt(a, b):
    return lax.dot_general(a, b, (((1,), (1,)), ((), ())), preferred_element_type=f32)


def whole(shape):
    zeros = (0,) * len(shape)
    return pl.BlockSpec(shape, lambda *_: zeros, pipeline_mode=pl.Buffered(1))


def column_block(rows, width):
    return pl.BlockSpec((rows, width), lambda j, *_: (0, j))


ANY = pl.BlockSpec(memory_space=pl.ANY)


def flip(index, mask):
    bit = 1
    while bit <= mask:
        if mask & bit:
            index = index + bit - 2 * bit * ((index // bit) % 2)
        bit *= 2
    return index


def exclusive_or(a, b, count):
    total, bit = 0, 1
    while bit < count:
        total = total + bit * ((a // bit + b // bit) % 2)
        bit *= 2
    return total


def greet(n, bits):
    me = lax.axis_index("fsdp")
    barrier = pltpu.get_barrier_semaphore()
    for bit in bits:
        pl.semaphore_signal(barrier, inc=1, device_id={"fsdp": flip(me, bit)}, device_id_type=pl.DeviceIdType.MESH)
    pl.semaphore_wait(barrier, len(bits))


class Gather:
    def __init__(self, own, full, order, send_sems, recv_sems, local_sem):
        self.own, self.full, self.order = own, full, order
        self.send_sems, self.recv_sems, self.local_sem = send_sems, recv_sems, local_sem
        self.me = lax.axis_index("fsdp")
        self.depth = own.shape[0]

    def rows(self, mask):
        return self.full.at[pl.ds(pl.multiple_of(flip(self.me, mask) * self.depth, 16), self.depth), :]

    def round_masks(self, round_at):
        earlier = self.order[:round_at]
        masks = [0]
        for bit in earlier:
            masks += [mask | bit for mask in masks]
        return [mask | self.order[round_at] for mask in masks]

    def copy(self, mask):
        bit = [bit for bit in self.order if bit & mask][-1]
        held = mask ^ bit
        return pltpu.make_async_remote_copy(
            src_ref=self.own if held == 0 else self.rows(held),
            dst_ref=self.rows(held),
            send_sem=self.send_sems.at[mask],
            recv_sem=self.recv_sems.at[mask],
            device_id={"fsdp": flip(self.me, bit)},
            device_id_type=pl.DeviceIdType.MESH,
        )

    def begin(self, round_at):
        if round_at == 0:
            pltpu.make_async_copy(self.own, self.rows(0), self.local_sem).start()
        self.copy(self.order[round_at]).start()

    def onward(self, round_at):
        masks = self.round_masks(round_at)
        for mask in masks:
            self.copy(mask).wait_recv()
        for bit in self.order[round_at + 1 :]:
            for mask in masks:
                self.copy(mask | bit).start()

    def end(self):
        pltpu.make_async_copy(self.own, self.rows(0), self.local_sem).wait()
        for round_at in range(len(self.order)):
            for mask in self.round_masks(round_at):
                self.copy(mask).wait_send()


def begin_all(n, gathers):
    rounds = len(gathers[0].order)
    greet(n, gathers[0].order)
    for round_at in range(rounds):
        for gather in gathers:
            gather.begin(round_at)


def onward_all(gathers, round_at):
    for gather in gathers:
        gather.onward(round_at)


def end_all(gathers):
    for gather in gathers:
        gather.end()


def make_gathers(n, layer, shards, wholes, orders, sems):
    send_sems, recv_sems, local_sems = sems
    return [
        Gather(own.at[layer], full, order, send_sems.at[at], recv_sems.at[at], local_sems.at[at])
        for at, (own, full, order) in enumerate(zip(shards, wholes, orders))
    ]


def gather_sems(n, count):
    return [
        pltpu.SemaphoreType.DMA((count, n)),
        pltpu.SemaphoreType.DMA((count, n)),
        pltpu.SemaphoreType.DMA((count,)),
    ]


def whole_of(n, shard):
    return jax.ShapeDtypeStruct((shard.shape[1] * n, shard.shape[2]), shard.dtype)


def gather_kernel(n, layer, orders, *refs):
    count = len(orders)
    gathers = make_gathers(n, layer, refs[:count], refs[count : 2 * count], orders, refs[2 * count :])
    begin_all(n, gathers)
    for round_at in range(len(orders[0])):
        onward_all(gathers, round_at)
    end_all(gathers)


def gather_weights(n, layer, shards, orders, collective_id):
    return pl.pallas_call(
        functools.partial(gather_kernel, n, layer, orders),
        out_shape=tuple(whole_of(n, shard) for shard in shards),
        in_specs=[ANY] * len(shards),
        out_specs=tuple([ANY] * len(shards)),
        scratch_shapes=gather_sems(n, len(shards)),
        compiler_params=pltpu.CompilerParams(collective_id=collective_id, has_side_effects=True),
        name="gather_weights",
    )(*shards)


BLOCK = 96


def add_rows(rows, target, sources):
    def step(block, carry):
        at = pl.ds(pl.multiple_of(block * BLOCK, BLOCK), BLOCK)
        total = None
        for ref, lead in sources:
            value = ref[(*lead, at)].astype(f32)
            total = value if total is None else total + value
        ref, lead = target
        ref[(*lead, at)] = total.astype(ref.dtype)
        return carry

    lax.fori_loop(0, rows // BLOCK, step, 0)


class Reduce:
    def __init__(self, halves, scratch, bits):
        self.keep, self.send = halves[:2], halves[2:]
        self.held, self.arrived = scratch[:2]
        hops = len(bits)
        self.hop_in = scratch[2 : 2 + hops]
        self.sems, self.hop_send, self.hop_recv = scratch[2 + hops : 5 + hops]
        self.orders = (bits[::-1], bits)
        self.chips, self.rows = self.held.shape[1:3]
        self.me = lax.axis_index("fsdp")

    def load(self, stream):
        return pltpu.make_async_copy(self.keep[stream], self.held.at[stream], self.sems.at[0, stream])

    def core_copy(self, stream):
        return pltpu.make_async_remote_copy(
            src_ref=self.send[stream],
            dst_ref=self.arrived.at[stream],
            send_sem=self.sems.at[1, stream],
            recv_sem=self.sems.at[2, stream],
            device_id={"fsdp": flip(self.me, 1)},
            device_id_type=pl.DeviceIdType.MESH,
        )

    def begin(self):
        for stream in range(2):
            self.core_copy(stream).start()
            self.load(stream).start()

    def leaving(self, stream, hop):
        gone = [bit // 2 for bit in self.orders[stream][:hop]]
        half = self.orders[stream][hop] // 2
        return half, [p for p in range(self.chips) if p & half and not any(p & g for g in gone)]

    def terms(self, stream, place, hops):
        found = [(self.held, (stream, place)), (self.arrived, (stream, place))]
        for hop in range(hops):
            half, places = self.leaving(stream, hop)
            found.append((self.hop_in[hop], (stream, places.index(place | half))))
        return found

    def hop_copy(self, stream, hop, slot, place):
        return pltpu.make_async_remote_copy(
            src_ref=self.held.at[stream, place],
            dst_ref=self.hop_in[hop].at[stream, slot],
            send_sem=self.hop_send.at[stream, hop, slot],
            recv_sem=self.hop_recv.at[stream, hop, slot],
            device_id={"fsdp": flip(self.me, self.orders[stream][hop])},
            device_id_type=pl.DeviceIdType.MESH,
        )

    def wait_before(self, stream, hop):
        if hop == 0:
            self.load(stream).wait()
            self.core_copy(stream).wait_recv()
        else:
            _, places = self.leaving(stream, hop - 1)
            for slot, place in enumerate(places):
                self.hop_copy(stream, hop - 1, slot, place).wait_recv()

    def hop(self, at):
        for stream in range(2):
            self.wait_before(stream, at)
            _, places = self.leaving(stream, at)
            for place in places:
                add_rows(self.rows, (self.held, (stream, place)), self.terms(stream, place, at))
            for slot, place in enumerate(places):
                self.hop_copy(stream, at, slot, place).start()

    def finish(self, result):
        hops = len(self.hop_in)
        for stream in range(2):
            self.wait_before(stream, hops)
            add_rows(self.rows, (result, (stream,)), self.terms(stream, 0, hops))
        for stream in range(2):
            self.core_copy(stream).wait_send()
            for hop in range(hops):
                _, places = self.leaving(stream, hop)
                for slot, place in enumerate(places):
                    self.hop_copy(stream, hop, slot, place).wait_send()


def reduce_scratch(chips, rows, width, hops):
    return (
        [pltpu.VMEM((2, chips, rows, width), bf16)] * 2
        + [pltpu.VMEM((2, chips >> (hop + 1), rows, width), bf16) for hop in range(hops)]
        + [pltpu.SemaphoreType.DMA((3, 2))]
        + [pltpu.SemaphoreType.DMA((2, hops, chips // 2))] * 2
    )


class Spread:
    def __init__(self, count, scratch):
        self.total, self.outgoing, self.incoming, self.whole, self.load_sems, self.sems = scratch
        self.bits = []
        bit = 1
        while bit < count:
            self.bits.append(bit)
            bit *= 2
        self.rank = lax.axis_index("rep")
        self.rows = self.total.shape[1]

    def load(self, stream, source):
        return pltpu.make_async_copy(source.at[stream], self.total.at[stream, pl.ds(0, source.shape[1])], self.load_sems.at[stream])

    def side(self, bit):
        return (self.rank // bit) % 2

    def span(self, stage):
        start, size = 0, self.rows
        for bit in self.bits[:stage]:
            size //= 2
            start = start + self.side(bit) * size
        return start, size

    def down_copy(self, stream, stage):
        size = self.rows >> (stage + 1)
        at = pl.ds(self.rows - (self.rows >> stage), size)
        return pltpu.make_async_remote_copy(
            src_ref=self.outgoing.at[stream, at],
            dst_ref=self.incoming.at[stream, at],
            send_sem=self.sems.at[0, stream, stage],
            recv_sem=self.sems.at[1, stream, stage],
            device_id={"rep": flip(self.rank, self.bits[stage])},
            device_id_type=pl.DeviceIdType.MESH,
        )

    def up_copy(self, stream, stage):
        start, size = self.span(stage + 1)
        at = pl.ds(pl.multiple_of(start, 16), size)
        return pltpu.make_async_remote_copy(
            src_ref=self.whole.at[stream, at],
            dst_ref=self.whole.at[stream, at],
            send_sem=self.sems.at[2, stream, stage],
            recv_sem=self.sems.at[3, stream, stage],
            device_id={"rep": flip(self.rank, self.bits[stage])},
            device_id_type=pl.DeviceIdType.MESH,
        )

    def act(self, stream, tick):
        stages = len(self.bits)
        if 0 < tick <= stages:
            stage = tick - 1
            self.down_copy(stream, stage).wait_recv()
            start, size = self.span(tick)
            base = self.rows - (self.rows >> stage)
            at = pl.ds(pl.multiple_of(start, 16), size)
            self.total[stream, at] += self.incoming[stream, pl.ds(base, size)].astype(f32)
        if tick < stages:
            bit = self.bits[tick]
            start, size = self.span(tick)
            size //= 2
            base = self.rows - (self.rows >> tick)
            at = pl.ds(pl.multiple_of(start + (1 - self.side(bit)) * size, 16), size)
            self.outgoing[stream, pl.ds(base, size)] = self.total[stream, at].astype(bf16)
            self.down_copy(stream, tick).start()
        elif tick == stages:
            start, size = self.span(stages)
            at = pl.ds(pl.multiple_of(start, 16), size)
            self.whole[stream, at] = self.total[stream, at].astype(bf16)
            self.up_copy(stream, stages - 1).start()
        else:
            stage = 2 * stages - tick
            self.up_copy(stream, stage).wait_recv()
            if stage:
                self.up_copy(stream, stage - 1).start()

    @property
    def ticks(self):
        return 2 * len(self.bits) + 2

    def tick(self, tick):
        for stream in range(2):
            if 0 <= tick - stream <= 2 * len(self.bits):
                self.act(stream, tick - stream)

    def end(self):
        for stream in range(2):
            for stage in range(len(self.bits)):
                self.down_copy(stream, stage).wait_send()
                self.up_copy(stream, stage).wait_send()


def padded(rows, count):
    return -(-rows // (16 * count)) * 16 * count


def spread_scratch(rows, width, count):
    rows = padded(rows, count)
    stages = count.bit_length() - 1
    return [
        pltpu.VMEM((2, rows, width), f32),
        pltpu.VMEM((2, rows, width), bf16),
        pltpu.VMEM((2, rows, width), bf16),
        pltpu.VMEM((2, rows, width), bf16),
        pltpu.SemaphoreType.DMA((2,)),
        pltpu.SemaphoreType.DMA((4, 2, stages)),
    ]


def greet_both(n, reps, fsdp_bits, rep_bits):
    me, rank = lax.axis_index("fsdp"), lax.axis_index("rep")
    barrier = pltpu.get_barrier_semaphore()
    for bit in fsdp_bits:
        pl.semaphore_signal(barrier, inc=1, device_id={"fsdp": flip(me, bit)}, device_id_type=pl.DeviceIdType.MESH)
    for bit in rep_bits:
        pl.semaphore_signal(barrier, inc=1, device_id={"rep": flip(rank, bit)}, device_id_type=pl.DeviceIdType.MESH)
    pl.semaphore_wait(barrier, len(fsdp_bits) + len(rep_bits))


def bits_below(count, first=1):
    bits = []
    while first < count:
        bits.append(first)
        first *= 2
    return bits


def norm_forward(total, gain, shift):
    middle = jnp.mean(total, axis=-1, keepdims=True)
    centred = total - middle
    spread = jnp.mean(centred * centred, axis=-1, keepdims=True)
    scaling = lax.rsqrt(spread + epsilon)
    normed = centred * scaling
    return normed * gain + shift, normed, scaling


def norm_backward(grad, normed, scaling, gain):
    scaled = grad * gain
    first = jnp.mean(scaled, axis=-1, keepdims=True)
    second = jnp.mean(scaled * normed, axis=-1, keepdims=True)
    return scaling * (scaled - first - normed * second)


def head_mask(shape, head):
    lanes = lax.broadcasted_iota(jnp.int32, shape, 1)
    return (lanes >= head * HEAD) & (lanes < (head + 1) * HEAD)


def attend_forward_kernel(n, seqs, layer, orders, x_ref, small_ref, mask_ref, qkv_ref, out_ref, *refs):
    count = len(orders)
    shards, refs = refs[:count], refs[count:]
    q_ref, k_ref, v_ref, ctx_ref, lse_ref, mid_ref, low_ref, n1_ref, r1_ref = refs[:9]
    wholes, refs = refs[9 : 9 + count], refs[9 + count :]
    base, w_qkv, w_out, acc, sems = refs[:5]
    gathers = make_gathers(n, layer, shards, wholes, orders, refs[5:])
    step, steps = pl.program_id(0), pl.num_programs(0)
    rows, width = x_ref.shape
    seq = rows // seqs
    heads = GROUP // HEAD
    qkv_copy = pltpu.make_async_copy(qkv_ref, w_qkv, sems.at[0])
    out_copy = pltpu.make_async_copy(out_ref, w_out, sems.at[1])

    @pl.when(step == 0)
    def _():
        qkv_copy.start()
        out_copy.start()
        begin_all(n, gathers)
        base[...] = x_ref[...].astype(bf16)
        qkv_copy.wait()
        out_copy.wait()

    columns = pl.multiple_of(step * GROUP, GROUP)
    q_bias = small_ref[0:1, pl.ds(columns, GROUP)]
    v_bias = small_ref[1:2, pl.ds(columns, GROUP)]

    def project(block, carry):
        at = pl.ds(pl.multiple_of(block * ROWS, ROWS), ROWS)
        low = base[at, :]
        q = dot_nn(low, w_qkv[:, pl.ds(columns, GROUP)])
        q_ref[at, :] = ((q + q_bias) * HEAD ** (-0.5)).astype(bf16)
        k = dot_nn(low, w_qkv[:, pl.ds(pl.multiple_of(width + columns, GROUP), GROUP)])
        k_ref[at, :] = k.astype(bf16)
        v = dot_nn(low, w_qkv[:, pl.ds(pl.multiple_of(2 * width + columns, GROUP), GROUP)])
        v_ref[at, :] = (v + v_bias).astype(bf16)
        return carry

    lax.fori_loop(0, rows // ROWS, project, 0)

    def attend(s, carry):
        at = pl.ds(pl.multiple_of(s * seq, seq), seq)
        q, k = q_ref[at, :], k_ref[at, :]
        v_turned = v_ref[at, :].T
        key_mask = mask_ref[at, :]
        parts = []
        for head in range(heads):
            q_head = jnp.where(head_mask(q.shape, head), q, jnp.zeros_like(q))
            scores = dot_nt(k, q_head) + key_mask
            peak = jnp.max(scores, axis=0, keepdims=True)
            raised = jnp.exp(scores - peak)
            total = jnp.sum(raised, axis=0, keepdims=True)
            mixed = dot_nn(v_turned[head * HEAD : (head + 1) * HEAD, :], raised.astype(bf16))
            parts.append((mixed / total).astype(bf16))
            lse_ref[0, pl.ds(s * heads + head, 1), :] = peak + jnp.log(total)
        ctx_ref[at, :] = jnp.concatenate(parts, axis=0).T
        return carry

    lax.fori_loop(0, seqs, attend, 0)

    @pl.when(step == 1)
    def _():
        onward_all(gathers, 0)

    def mix(block, carry):
        at = pl.ds(pl.multiple_of(block * ROWS, ROWS), ROWS)
        term = dot_nn(ctx_ref[at, :], w_out[pl.ds(columns, GROUP), :])

        @pl.when(step == 0)
        def _():
            acc[at, :] = term

        @pl.when(step > 0)
        def _():
            acc[at, :] += term

        @pl.when(step == steps - 1)
        def _():
            total = x_ref[at, :].astype(f32) + acc[at, :] + small_ref[2:3, :]
            mid, normed, scaling = norm_forward(total, small_ref[6:7, :], small_ref[4:5, :])
            mid_ref[at, :] = mid
            low_ref[at, :] = mid.astype(bf16)
            n1_ref[at, :] = normed.astype(bf16)
            r1_ref[at, :] = scaling

        return carry

    lax.fori_loop(0, rows // ROWS, mix, 0)

    @pl.when(step == steps - 1)
    def _():
        for round_at in range(1, len(orders[0])):
            onward_all(gathers, round_at)
        end_all(gathers)


def attend_forward(n, x, small, key_mask, w_qkv, w_out, seqs, layer, shards, orders, collective_id):
    rows, width = x.shape
    steps = width // GROUP
    seq = rows // seqs
    wide = jax.ShapeDtypeStruct((rows, width), bf16)
    heads = GROUP // HEAD
    return pl.pallas_call(
        functools.partial(attend_forward_kernel, n, seqs, layer, orders),
        out_shape=(
            wide,
            wide,
            wide,
            wide,
            jax.ShapeDtypeStruct((steps, seqs * heads, seq), f32),
            jax.ShapeDtypeStruct((rows, width), f32),
            wide,
            wide,
            jax.ShapeDtypeStruct((rows, 1), f32),
        )
        + tuple(whole_of(n, shard) for shard in shards),
        grid_spec=pltpu.PrefetchScalarGridSpec(
            num_scalar_prefetch=0,
            grid=(steps,),
            in_specs=[whole((rows, width)), whole(small.shape), whole((rows, 1))] + [ANY] * (2 + len(shards)),
            out_specs=[column_block(rows, GROUP)] * 4
            + [
                pl.BlockSpec((1, seqs * heads, seq), lambda j, *_: (j, 0, 0)),
                whole((rows, width)),
                whole((rows, width)),
                whole((rows, width)),
                whole((rows, 1)),
            ]
            + [ANY] * len(shards),
            scratch_shapes=[
                pltpu.VMEM((rows, width), bf16),
                pltpu.VMEM((width, 3 * width), bf16),
                pltpu.VMEM((width, width), bf16),
                pltpu.VMEM((rows, width), f32),
                pltpu.SemaphoreType.DMA((2,)),
            ]
            + gather_sems(n, len(shards)),
        ),
        compiler_params=pltpu.CompilerParams(
            dimension_semantics=("arbitrary",),
            vmem_limit_bytes=VMEM_BYTES,
            collective_id=collective_id,
            has_side_effects=True,
        ),
        cost_estimate=cost(8 * rows * width * width + 16 * rows * seq * width, 20 * rows * width),
        name="attend_forward",
    )(x, small, key_mask, w_qkv, w_out, *shards)


def ffn_forward_kernel(n, last, layer, orders, mid_ref, low_ref, small_ref, up_bias_ref, valid_ref, up_ref, down_ref, *refs):
    count = len(orders)
    shards, refs = refs[:count], refs[count:]
    act_ref, slope_ref, n2_ref, r2_ref, hid_ref = refs[:5]
    refs = refs[5:]
    if not last:
        hid_low_ref, refs = refs[0], refs[1:]
    wholes, refs = refs[:count], refs[count:]
    w_up, w_down, acc, sems = refs[:4]
    gathers = make_gathers(n, layer, shards, wholes, orders, refs[4:]) if count else []
    step, steps = pl.program_id(0), pl.num_programs(0)
    rows, width = mid_ref.shape
    chunk = act_ref.shape[1]
    up_copy = pltpu.make_async_copy(up_ref, w_up, sems.at[0])
    down_copy = pltpu.make_async_copy(down_ref, w_down, sems.at[1])

    @pl.when(step == 0)
    def _():
        up_copy.start()
        down_copy.start()
        if gathers:
            begin_all(n, gathers)
        up_copy.wait()
        down_copy.wait()

    if gathers:

        @pl.when(step == 1)
        def _():
            onward_all(gathers, 0)

        @pl.when(step == 3)
        def _():
            onward_all(gathers, 1)

    columns = pl.multiple_of(step * chunk, chunk)
    tile = 256

    def block_step(block, carry):
        at = pl.ds(pl.multiple_of(block * ROWS, ROWS), ROWS)
        low = low_ref[at, :]
        for part in range(chunk // tile):
            inside = slice(part * tile, (part + 1) * tile)
            at_units = pl.ds(pl.multiple_of(columns + part * tile, tile), tile)
            pre = dot_nn(low, w_up[:, at_units]) + up_bias_ref[:, inside]
            share = 0.5 * (1.0 + lax.erf(pre * root_half))
            act_ref[at, inside] = (pre * share).astype(bf16)
            density = inv_root_tau * jnp.exp(-0.5 * pre * pre)
            slope_ref[at, inside] = (share + pre * density).astype(bf16)
        term = dot_nn(act_ref[at, :], w_down[pl.ds(columns, chunk), :])

        @pl.when(step == 0)
        def _():
            acc[at, :] = term

        @pl.when(step > 0)
        def _():
            acc[at, :] += term

        @pl.when(step == steps - 1)
        def _():
            total = mid_ref[at, :] + acc[at, :] + small_ref[3:4, :]
            hidden, normed, scaling = norm_forward(total, small_ref[7:8, :], small_ref[5:6, :])
            n2_ref[at, :] = normed.astype(bf16)
            r2_ref[at, :] = scaling
            if last:
                hid_ref[at, :] = (hidden * valid_ref[at, :]).astype(bf16)
            else:
                hid_ref[at, :] = hidden
                hid_low_ref[at, :] = hidden.astype(bf16)

        return carry

    lax.fori_loop(0, rows // ROWS, block_step, 0)

    if gathers:

        @pl.when(step == steps - 1)
        def _():
            for round_at in range(2, len(orders[0])):
                onward_all(gathers, round_at)
            end_all(gathers)


def ffn_forward(n, mid, low, small, up_bias, valid, w_up, w_down, last, layer, shards, orders, collective_id):
    rows, width = mid.shape
    units = up_bias.shape[1]
    chunk = width
    steps = units // chunk
    out_shape = [
        jax.ShapeDtypeStruct((rows, units), bf16),
        jax.ShapeDtypeStruct((rows, units), bf16),
        jax.ShapeDtypeStruct((rows, width), bf16),
        jax.ShapeDtypeStruct((rows, 1), f32),
        jax.ShapeDtypeStruct((rows, width), bf16 if last else f32),
    ]
    out_specs = [column_block(rows, chunk)] * 2 + [
        whole((rows, width)),
        whole((rows, 1)),
        whole((rows, width)),
    ]
    if not last:
        out_shape.append(jax.ShapeDtypeStruct((rows, width), bf16))
        out_specs.append(whole((rows, width)))
    out_shape += [whole_of(n, shard) for shard in shards]
    out_specs += [ANY] * len(shards)
    if shards:
        params = pltpu.CompilerParams(
            dimension_semantics=("arbitrary",),
            vmem_limit_bytes=VMEM_BYTES,
            collective_id=collective_id,
            has_side_effects=True,
        )
    else:
        params = pltpu.CompilerParams(dimension_semantics=("arbitrary",), vmem_limit_bytes=VMEM_BYTES)
    return pl.pallas_call(
        functools.partial(ffn_forward_kernel, n, last, layer, orders),
        out_shape=tuple(out_shape),
        grid_spec=pltpu.PrefetchScalarGridSpec(
            num_scalar_prefetch=0,
            grid=(steps,),
            in_specs=[
                whole((rows, width)),
                whole((rows, width)),
                whole(small.shape),
                column_block(1, chunk),
                whole((rows, 1)),
            ]
            + [ANY] * (2 + len(shards)),
            out_specs=out_specs,
            scratch_shapes=[
                pltpu.VMEM((width, units), bf16),
                pltpu.VMEM((units, width), bf16),
                pltpu.VMEM((rows, width), f32),
                pltpu.SemaphoreType.DMA((2,)),
            ]
            + (gather_sems(n, len(shards)) if shards else []),
        ),
        compiler_params=params,
        cost_estimate=cost(8 * rows * width * units, 8 * rows * units),
        name="ffn_forward",
    )(mid, low, small, up_bias, valid, w_up, w_down, *shards)


def shard_copies(n, me, source_of, keep_of, send_of, sems):
    def each(start):
        for owner in range(n):
            mask = flip(me, owner)
            place = mask // 2

            @pl.when(mask % 2 == 0)
            def _():
                copy = pltpu.make_async_copy(source_of(owner), keep_of(place), sems.at[owner])
                copy.start() if start else copy.wait()

            @pl.when(mask % 2 == 1)
            def _():
                copy = pltpu.make_async_copy(source_of(owner), send_of(place), sems.at[owner])
                copy.start() if start else copy.wait()

    return each


def ffn_backward_kernel(n, reps, carry, g_ref, valid_ref, n2_ref, r2_ref, low_ref, n1_ref, r1_ref, small_ref, act_ref, slope_ref, *refs):
    up_ref, down_ref, refs = refs[0], refs[1], refs[2:]
    if carry:
        halves, spread_from, refs = refs[:4], refs[4], refs[5:]
    gs1_ref, ga1_ref, sums_ref, up_sum_ref, down_keep, down_send, up_keep, up_send = refs[:8]
    refs = refs[8:]
    if carry:
        reduced_ref, spread_ref, refs = refs[0], refs[1], refs[2:]
    w_up, w_down, gs2, gffn, gpre, acc, low_turned, d_down, d_up, sems, out_sems = refs[:11]
    if carry:
        hops = len(bits_below(n, 2))
        reduce = Reduce(halves, refs[11 : 16 + hops], bits_below(n, 2))
        spread = Spread(reps, refs[16 + hops : 22 + hops])
        spread_sem = refs[22 + hops]
    step, steps = pl.program_id(0), pl.num_programs(0)
    me = lax.axis_index("fsdp")
    rows, width = gs2.shape
    last_step = steps - 1
    if carry:
        out_copy = pltpu.make_async_copy(spread.whole, spread_ref, spread_sem)

        @pl.when(step == 0)
        def _():
            greet_both(n, reps, bits_below(n), bits_below(reps))
            reduce.begin()
            for stream in range(2):
                spread.load(stream, spread_from).start()
            for stream in range(2):
                spread.load(stream, spread_from).wait()
            spread.tick(0)

        @pl.when(step == 1)
        def _():
            reduce.hop(0)
            spread.tick(1)

        @pl.when(step == 2)
        def _():
            spread.tick(3)
            for hop in range(1, hops):
                reduce.hop(hop)

        @pl.when(step == 3)
        def _():
            for tick in range(5, spread.ticks):
                spread.tick(tick)
            out_copy.start()
            reduce.finish(reduced_ref)
    chunk = act_ref.shape[1]
    per_down = down_keep.shape[1]
    per_up = up_keep.shape[2]
    tile = 256
    up_copies = [pltpu.make_async_copy(up_ref, w_up, sems.at[0])]
    down_copies = [pltpu.make_async_copy(down_ref, w_down, sems.at[1])]

    @pl.when(step == 0)
    def _():
        for copy in down_copies:
            copy.start()
        for copy in up_copies:
            copy.start()
        sums_ref[...] = jnp.zeros_like(sums_ref)

        def prepare(block, carry):
            at = pl.ds(pl.multiple_of(block * ROWS, ROWS), ROWS)
            grad = g_ref[at, :].astype(f32) * valid_ref[at, :]
            normed = n2_ref[at, :].astype(f32)
            summed = norm_backward(grad, normed, r2_ref[at, :], small_ref[7:8, :])
            gs2[at, :] = summed
            low = summed.astype(bf16)
            gffn[at, :] = low
            sums_ref[0:1, :] += jnp.sum(grad * normed, axis=0, keepdims=True)
            sums_ref[1:2, :] += jnp.sum(grad, axis=0, keepdims=True)
            sums_ref[2:3, :] += jnp.sum(low.astype(f32), axis=0, keepdims=True)
            low_turned[:, at] = low_ref[at, :].T
            return carry

        lax.fori_loop(0, rows // ROWS, prepare, 0)
        for copy in down_copies:
            copy.wait()
        for copy in up_copies:
            copy.wait()

    columns = pl.multiple_of(step * chunk, chunk)
    up_sum_ref[...] = jnp.zeros_like(up_sum_ref)

    def through(block, carry):
        at = pl.ds(pl.multiple_of(block * ROWS, ROWS), ROWS)
        grad = gffn[at, :]
        for part in range(chunk // tile):
            inside = slice(part * tile, (part + 1) * tile)
            at_units = pl.ds(pl.multiple_of(columns + part * tile, tile), tile)
            grad_act = dot_nt(grad, w_down[at_units, :])
            low = (grad_act * slope_ref[at, inside].astype(f32)).astype(bf16)
            gpre[at, inside] = low
            up_sum_ref[:, inside] += jnp.sum(low.astype(f32), axis=0, keepdims=True)
        term = dot_nt(gpre[at, :], w_up[:, pl.ds(columns, chunk)])

        @pl.when(step == 0)
        def _():
            acc[at, :] = term

        @pl.when(step > 0)
        def _():
            acc[at, :] += term

        return carry

    lax.fori_loop(0, rows // ROWS, through, 0)
    if carry:

        @pl.when(step == 1)
        def _():
            spread.tick(2)

        @pl.when(step == 2)
        def _():
            spread.tick(4)

    def down_out(which):
        def run(start):
            for local in range(chunk // per_down):
                owner = which * (chunk // per_down) + local
                mask = exclusive_or(me, owner, n)
                source = d_down.at[pl.ds(local * per_down, per_down), :]
                place = mask // 2

                @pl.when(mask % 2 == 0)
                def _():
                    copy = pltpu.make_async_copy(source, down_keep.at[place], out_sems.at[0, local])
                    copy.start() if start else copy.wait()

                @pl.when(mask % 2 == 1)
                def _():
                    copy = pltpu.make_async_copy(source, down_send.at[place], out_sems.at[0, local])
                    copy.start() if start else copy.wait()

        return run

    def up_out(which):
        return shard_copies(
            n,
            me,
            lambda owner: d_up.at[pl.ds(owner * per_up, per_up), :],
            lambda place: up_keep.at[place, which],
            lambda place: up_send.at[place, which],
            out_sems.at[1],
        )

    @pl.when(step > 0)
    def _():
        down_out(step - 1)(False)

    def down_part(part, carry):
        at = pl.ds(pl.multiple_of(part * tile, tile), tile)
        turned = act_ref[:, at].T
        d_down[at, :] = dot_nn(turned, gffn[...]).astype(bf16)
        return carry

    lax.fori_loop(0, chunk // tile, down_part, 0)
    down_out(step)(True)

    @pl.when(step > 0)
    def _():
        up_out(step - 1)(False)

    def up_part(part, carry):
        at = pl.ds(pl.multiple_of(part * tile, tile), tile)
        d_up[at, :] = dot_nn(low_turned[at, :], gpre[...]).astype(bf16)
        return carry

    lax.fori_loop(0, width // tile, up_part, 0)
    up_out(step)(True)

    @pl.when(step == steps - 1)
    def _():
        def finish(block, carry):
            at = pl.ds(pl.multiple_of(block * ROWS, ROWS), ROWS)
            grad = gs2[at, :] + acc[at, :]
            normed = n1_ref[at, :].astype(f32)
            summed = norm_backward(grad, normed, r1_ref[at, :], small_ref[6:7, :])
            gs1_ref[at, :] = summed
            low = summed.astype(bf16)
            ga1_ref[at, :] = low
            sums_ref[3:4, :] += jnp.sum(grad * normed, axis=0, keepdims=True)
            sums_ref[4:5, :] += jnp.sum(grad, axis=0, keepdims=True)
            sums_ref[5:6, :] += jnp.sum(low.astype(f32), axis=0, keepdims=True)
            return carry

        lax.fori_loop(0, rows // ROWS, finish, 0)
        down_out(step)(False)
        up_out(step)(False)
        if carry:
            out_copy.wait()
            spread.end()


def remote_params(collective_id):
    return pltpu.CompilerParams(
        dimension_semantics=("arbitrary",),
        vmem_limit_bytes=VMEM_BYTES,
        collective_id=collective_id,
        has_side_effects=True,
    )


def ffn_backward(n, reps, grad, valid, n2, r2, low, n1, r1, small, act, slope, w_up, w_down, carry, collective_id):
    rows, width = grad.shape
    units = act.shape[1]
    chunk = width
    steps = units // chunk
    chips = n // 2
    hops = len(bits_below(n, 2))
    extra_out, extra_specs, extra_scratch = [], [], []
    if carry:
        reduced = (2,) + carry[0].shape[1:]
        spread_rows = carry[4].shape[1]
        extra_out = [
            jax.ShapeDtypeStruct(reduced, f32),
            jax.ShapeDtypeStruct((2, padded(spread_rows, reps), width), bf16),
        ]
        extra_specs = [whole(reduced), ANY]
        extra_scratch = reduce_scratch(chips, carry[0].shape[1], width, hops)
        extra_scratch += spread_scratch(spread_rows, width, reps) + [pltpu.SemaphoreType.DMA]
    down_half = jax.ShapeDtypeStruct((chips, units // n, width), bf16)
    up_half = jax.ShapeDtypeStruct((chips, steps, width // n, chunk), bf16)
    return pl.pallas_call(
        functools.partial(ffn_backward_kernel, n, reps, bool(carry)),
        out_shape=(
            jax.ShapeDtypeStruct((rows, width), f32),
            jax.ShapeDtypeStruct((rows, width), bf16),
            jax.ShapeDtypeStruct((8, width), f32),
            jax.ShapeDtypeStruct((1, units), f32),
            down_half,
            down_half,
            up_half,
            up_half,
            *extra_out,
        ),
        grid_spec=pltpu.PrefetchScalarGridSpec(
            num_scalar_prefetch=0,
            grid=(steps,),
            in_specs=[
                whole((rows, width)),
                whole((rows, 1)),
                whole((rows, width)),
                whole((rows, 1)),
                whole((rows, width)),
                whole((rows, width)),
                whole((rows, 1)),
                whole(small.shape),
                column_block(rows, chunk),
                column_block(rows, chunk),
            ]
            + [ANY] * (2 + len(carry)),
            out_specs=[
                whole((rows, width)),
                whole((rows, width)),
                whole((8, width)),
                column_block(1, chunk),
            ]
            + [ANY] * 4
            + extra_specs,
            scratch_shapes=[
                pltpu.VMEM((width, units), bf16),
                pltpu.VMEM((units, width), bf16),
                pltpu.VMEM((rows, width), f32),
                pltpu.VMEM((rows, width), bf16),
                pltpu.VMEM((rows, chunk), bf16),
                pltpu.VMEM((rows, width), f32),
                pltpu.VMEM((width, rows), bf16),
                pltpu.VMEM((chunk, width), bf16),
                pltpu.VMEM((width, chunk), bf16),
                pltpu.SemaphoreType.DMA((2,)),
                pltpu.SemaphoreType.DMA((2, n)),
            ]
            + extra_scratch,
        ),
        compiler_params=remote_params(collective_id)
        if carry
        else pltpu.CompilerParams(dimension_semantics=("arbitrary",), vmem_limit_bytes=VMEM_BYTES),
        cost_estimate=cost(10 * rows * width * units, 8 * rows * units),
        name="ffn_backward",
    )(grad, valid, n2, r2, low, n1, r1, small, act, slope, w_up, w_down, *carry)


def attend_backward_kernel(n, reps, seqs, spreads, ga_ref, gs_ref, base_ref, mask_ref, q_ref, k_ref, v_ref, ctx_ref, lse_ref, *refs):
    qkv_ref, out_ref, halves, refs = refs[0], refs[1], refs[2:6], refs[6:]
    if spreads:
        spread_from, refs = refs[0], refs[1:]
    gh_ref, sums_ref, a_keep, b_keep, a_send, b_send, reduced_ref = refs[:7]
    refs = refs[7:]
    if spreads:
        spread_ref, refs = refs[0], refs[1:]
    w_qkv, w_out, acc, base_turned, gctx, gproj, d_qkv, d_out, p_all, ds_all, sems, out_sems = refs[:12]
    hops = len(bits_below(n, 2))
    reduce = Reduce(halves, refs[12 : 17 + hops], bits_below(n, 2))
    step, steps = pl.program_id(0), pl.num_programs(0)
    me = lax.axis_index("fsdp")
    if spreads:
        spread = Spread(reps, refs[17 + hops : 23 + hops])
        spread_copy = pltpu.make_async_copy(spread.whole, spread_ref, refs[23 + hops])

    @pl.when(step == 0)
    def _():
        greet_both(n, reps, bits_below(n), bits_below(reps) if spreads else [])
        reduce.begin()
        if spreads:
            for stream in range(2):
                spread.load(stream, spread_from).start()
            for stream in range(2):
                spread.load(stream, spread_from).wait()
            spread.tick(0)

    if spreads:

        @pl.when(step == 1)
        def _():
            spread.tick(2)

        @pl.when(step == 2)
        def _():
            spread.tick(4)
    rows, width = ga_ref.shape
    seq = rows // seqs
    heads = GROUP // HEAD
    per = width // n
    tile = 256
    qkv_copies = [pltpu.make_async_copy(qkv_ref, w_qkv, sems.at[0])]
    out_copies = [pltpu.make_async_copy(out_ref, w_out, sems.at[1])]

    @pl.when(step == 0)
    def _():
        for copy in out_copies:
            copy.start()
        for copy in qkv_copies:
            copy.start()

        def turn(block, carry):
            at = pl.ds(pl.multiple_of(block * ROWS, ROWS), ROWS)
            base_turned[:, at] = base_ref[at, :].T
            return carry

        lax.fori_loop(0, rows // ROWS, turn, 0)
        for copy in out_copies:
            copy.wait()
        for copy in qkv_copies:
            copy.wait()

    columns = pl.multiple_of(step * GROUP, GROUP)

    def through(block, carry):
        at = pl.ds(pl.multiple_of(block * ROWS, ROWS), ROWS)
        gctx[at, :] = dot_nt(ga_ref[at, :], w_out[pl.ds(columns, GROUP), :]).astype(bf16)
        return carry

    lax.fori_loop(0, rows // ROWS, through, 0)
    d_out[pl.ds(columns, GROUP), :] = dot_nn(ctx_ref[...].T, ga_ref[...]).astype(bf16)

    @pl.when(step == 2)
    def _():
        for hop in range(1, hops):
            reduce.hop(hop)

    def attend(s, carry):
        at = pl.ds(pl.multiple_of(s * seq, seq), seq)
        q, k, v, grad = q_ref[at, :], k_ref[at, :], v_ref[at, :], gctx[at, :]
        k_turned = k.T
        key_mask = mask_ref[at, :]
        parts, q_heads, g_heads = [], [], []
        for head in range(heads):
            inside = head_mask(q.shape, head)
            q_head = jnp.where(inside, q, jnp.zeros_like(q))
            g_head = jnp.where(inside, grad, jnp.zeros_like(grad))
            scores = dot_nt(k, q_head) + key_mask
            attention = jnp.exp(scores - lse_ref[0, pl.ds(s * heads + head, 1), :])
            weighted = attention * dot_nt(v, g_head)
            inner = jnp.sum(weighted, axis=0, keepdims=True)
            grad_scores = (weighted - attention * inner).astype(bf16)
            here = slice(head * seq, (head + 1) * seq)
            p_all[:, here] = attention.astype(bf16)
            ds_all[:, here] = grad_scores
            turned = dot_nn(k_turned[head * HEAD : (head + 1) * HEAD, :], grad_scores)
            parts.append(turned.astype(bf16) * HEAD ** (-0.5))
            q_heads.append(q_head)
            g_heads.append(g_head)
        gproj[at, 0:GROUP] = jnp.concatenate(parts, axis=0).T
        gproj[at, GROUP : 2 * GROUP] = dot_nn(ds_all[...], jnp.concatenate(q_heads, axis=0)).astype(bf16)
        gproj[at, 2 * GROUP : 3 * GROUP] = dot_nn(p_all[...], jnp.concatenate(g_heads, axis=0)).astype(bf16)
        return carry

    lax.fori_loop(0, seqs, attend, 0)
    sums_ref[...] = jnp.zeros_like(sums_ref)

    @pl.when(step == 0)
    def _():
        reduce.hop(0)
        if spreads:
            spread.tick(1)

    @pl.when(step == 1)
    def _():
        if spreads:
            spread.tick(3)

    @pl.when(step == 2)
    def _():
        if spreads:
            for tick in range(5, spread.ticks):
                spread.tick(tick)
            spread_copy.start()

    def onward(block, carry):
        at = pl.ds(pl.multiple_of(block * ROWS, ROWS), ROWS)
        term = dot_nt(gproj[at, 0:GROUP], w_qkv[:, pl.ds(columns, GROUP)])
        term += dot_nt(gproj[at, GROUP : 2 * GROUP], w_qkv[:, pl.ds(pl.multiple_of(width + columns, GROUP), GROUP)])
        term += dot_nt(gproj[at, 2 * GROUP : 3 * GROUP], w_qkv[:, pl.ds(pl.multiple_of(2 * width + columns, GROUP), GROUP)])
        sums_ref[0:1, :] += jnp.sum(gproj[at, 0:GROUP].astype(f32), axis=0, keepdims=True)
        sums_ref[1:2, :] += jnp.sum(gproj[at, 2 * GROUP : 3 * GROUP].astype(f32), axis=0, keepdims=True)

        @pl.when(step == 0)
        def _():
            acc[at, :] = gs_ref[at, :] + term

        @pl.when(step > 0)
        def _():
            acc[at, :] += term

        @pl.when(step == steps - 1)
        def _():
            gh_ref[at, :] = acc[at, :].astype(gh_ref.dtype)

        return carry

    lax.fori_loop(0, rows // ROWS, onward, 0)

    def place_of(part, a_half, b_half):
        return a_half if part < 2 else b_half

    def rows_of(part):
        return pl.ds((part % 2) * per, per)

    def qkv_out(which, start):
        for part in range(3):
            at = pl.ds(pl.multiple_of(which * GROUP, GROUP), GROUP)
            shard_copies(
                n,
                me,
                lambda owner: d_qkv.at[pl.ds(owner * per, per), pl.ds(part * GROUP, GROUP)],
                lambda place: place_of(part, a_keep, b_keep).at[place, rows_of(part), at],
                lambda place: place_of(part, a_send, b_send).at[place, rows_of(part), at],
                out_sems.at[part],
            )(start)

    @pl.when(step > 0)
    def _():
        qkv_out(step - 1, False)

    def weight_part(part, carry):
        at = pl.ds(pl.multiple_of(part * tile, tile), tile)
        d_qkv[at, :] = dot_nn(base_turned[at, :], gproj[...]).astype(bf16)
        return carry

    lax.fori_loop(0, width // tile, weight_part, 0)
    qkv_out(step, True)

    @pl.when(step == steps - 1)
    def _():
        out_copy = shard_copies(
            n,
            me,
            lambda owner: d_out.at[pl.ds(owner * per, per), :],
            lambda place: b_keep.at[place, rows_of(3)],
            lambda place: b_send.at[place, rows_of(3)],
            out_sems.at[3],
        )
        out_copy(True)
        qkv_out(step, False)
        out_copy(False)
        reduce.finish(reduced_ref)
        if spreads:
            spread_copy.wait()
            spread.end()


def attend_backward(n, reps, ga, gs, base, key_mask, q, k, v, ctx, lse, w_qkv, w_out, seqs, out_type, carry, collective_id):
    rows, width = ga.shape
    steps = width // GROUP
    seq = rows // seqs
    heads = GROUP // HEAD
    chips = n // 2
    half = jax.ShapeDtypeStruct((chips, 2 * width // n, width), bf16)
    hops = len(bits_below(n, 2))
    reduced = (2,) + carry[0].shape[1:]
    extra_out, extra_specs = [], []
    extra_scratch = reduce_scratch(chips, carry[0].shape[1], width, hops)
    if len(carry) > 4:
        spread_rows = carry[4].shape[1]
        extra_out = [jax.ShapeDtypeStruct((2, padded(spread_rows, reps), width), bf16)]
        extra_specs = [ANY]
        extra_scratch += spread_scratch(spread_rows, width, reps) + [pltpu.SemaphoreType.DMA]
    return pl.pallas_call(
        functools.partial(attend_backward_kernel, n, reps, seqs, len(carry) > 4),
        out_shape=(
            jax.ShapeDtypeStruct((rows, width), out_type),
            jax.ShapeDtypeStruct((8, width), f32),
            half,
            half,
            half,
            half,
            jax.ShapeDtypeStruct(reduced, f32),
            *extra_out,
        ),
        grid_spec=pltpu.PrefetchScalarGridSpec(
            num_scalar_prefetch=0,
            grid=(steps,),
            in_specs=[whole((rows, width))] * 3
            + [whole((rows, 1))]
            + [column_block(rows, GROUP)] * 4
            + [pl.BlockSpec((1, seqs * heads, seq), lambda j, *_: (j, 0, 0))]
            + [ANY] * (2 + len(carry)),
            out_specs=[whole((rows, width)), column_block(8, GROUP)] + [ANY] * 4 + [whole(reduced)] + extra_specs,
            scratch_shapes=[
                pltpu.VMEM((width, 3 * width), bf16),
                pltpu.VMEM((width, width), bf16),
                pltpu.VMEM((rows, width), f32),
                pltpu.VMEM((width, rows), bf16),
                pltpu.VMEM((rows, GROUP), bf16),
                pltpu.VMEM((rows, 3 * GROUP), bf16),
                pltpu.VMEM((width, 3 * GROUP), bf16),
                pltpu.VMEM((width, width), bf16),
                pltpu.VMEM((seq, heads * seq), bf16),
                pltpu.VMEM((seq, heads * seq), bf16),
                pltpu.SemaphoreType.DMA((2,)),
                pltpu.SemaphoreType.DMA((4, n)),
            ]
            + extra_scratch,
        ),
        compiler_params=remote_params(collective_id),
        cost_estimate=cost(16 * rows * width * width + 40 * rows * seq * width, 20 * rows * width),
        name="attend_backward",
    )(ga, gs, base, key_mask, q, k, v, ctx, lse, w_qkv, w_out, *carry)


def cost(flops, moved):
    return pl.CostEstimate(flops=int(flops), bytes_accessed=int(moved), transcendentals=0)


def last_sums_kernel(n, reps, a_keep, b_keep, a_send, b_send, spread_from, small_ref, spread_ref, attend_ref, total_ref, *scratch):
    bits, rep_bits = bits_below(n, 2), bits_below(reps)
    hops = len(bits)
    reduce = Reduce((a_keep, b_keep, a_send, b_send), scratch[: 5 + hops], bits)
    first = Spread(reps, scratch[5 + hops : 11 + hops])
    second = Spread(reps, scratch[11 + hops : 17 + hops])
    reduced, small_out, small_in, small_sems, sems = scratch[17 + hops :]
    axes = [("fsdp", bit) for bit in bits_below(n)] + [("rep", bit) for bit in rep_bits]

    def small_copy(at):
        axis, bit = axes[at]
        return pltpu.make_async_remote_copy(
            src_ref=small_out.at[at],
            dst_ref=small_in.at[at],
            send_sem=small_sems.at[0, at],
            recv_sem=small_sems.at[1, at],
            device_id={axis: flip(lax.axis_index(axis), bit)},
            device_id_type=pl.DeviceIdType.MESH,
        )

    def small_step(at):
        small_copy(at).wait_recv()
        if at + 1 < len(axes):
            small_out[at + 1] = small_out[at] + small_in[at]
            small_copy(at + 1).start()
        else:
            total_ref[...] = small_out[at] + small_in[at]

    greet_both(n, reps, bits_below(n), rep_bits)
    reduce.begin()
    for stream in range(2):
        first.load(stream, spread_from).start()
    small_out[0] = small_ref[...]
    small_copy(0).start()
    for stream in range(2):
        first.load(stream, spread_from).wait()
    first.tick(0)
    reduce.hop(0)
    small_step(0)
    first.tick(1)
    small_step(1)
    first.tick(2)
    for hop in range(1, hops):
        reduce.hop(hop)
    small_step(2)
    first.tick(3)
    reduce.finish(reduced)
    rows = reduced.shape[1]
    for stream in range(2):
        second.total[stream, pl.ds(0, rows)] = reduced[stream]
    second.tick(0)
    for at in range(3, len(axes)):
        small_step(at)
    for tick in range(4, first.ticks):
        first.tick(tick)
        second.tick(tick - 3)
    first_copy = pltpu.make_async_copy(first.whole, spread_ref, sems.at[0])
    first_copy.start()
    for tick in range(first.ticks - 3, second.ticks):
        second.tick(tick)
    second_copy = pltpu.make_async_copy(second.whole, attend_ref, sems.at[1])
    second_copy.start()
    first.end()
    second.end()
    for at in range(len(axes)):
        small_copy(at).wait_send()
    first_copy.wait()
    second_copy.wait()


def last_sums(n, reps, halves, spread_rows, small, collective_id):
    chips, rows, width = halves[0].shape
    hops = len(bits_below(n, 2))
    count = len(bits_below(n)) + len(bits_below(reps))
    vmem = pl.BlockSpec(memory_space=pltpu.VMEM)
    return pl.pallas_call(
        functools.partial(last_sums_kernel, n, reps),
        out_shape=(
            jax.ShapeDtypeStruct((2, padded(spread_rows.shape[1], reps), width), bf16),
            jax.ShapeDtypeStruct((2, padded(rows, reps), width), bf16),
            jax.ShapeDtypeStruct(small.shape, f32),
        ),
        in_specs=[ANY] * 5 + [vmem],
        out_specs=(ANY, ANY, vmem),
        scratch_shapes=reduce_scratch(chips, rows, width, hops)
        + spread_scratch(spread_rows.shape[1], width, reps)
        + spread_scratch(rows, width, reps)
        + [
            pltpu.VMEM((2, rows, width), f32),
            pltpu.VMEM((count, *small.shape), f32),
            pltpu.VMEM((count, *small.shape), f32),
            pltpu.SemaphoreType.DMA((2, count)),
            pltpu.SemaphoreType.DMA((2,)),
        ],
        compiler_params=pltpu.CompilerParams(
            vmem_limit_bytes=VMEM_BYTES, collective_id=collective_id, has_side_effects=True
        ),
        name="last_sums",
    )(*halves, spread_rows, small)


def swap(array, axis, count, mask):
    return lax.ppermute(array, axis, [(i, i ^ mask) for i in range(count)])


def gather_small(own, n, me):
    array = own[None]
    bit = 1
    while bit < n:
        other = swap(array, "fsdp", n, bit)
        upper = (me // bit) % 2 == 1
        array = jnp.concatenate([jnp.where(upper, other, array), jnp.where(upper, array, other)], axis=0)
        bit *= 2
    return array


def on_device(n, reps, tokens, cotangent, lengths, live_batches, w_qkv, w_out, w_up, w_down, up_bias, biases, norm_gains):
    seqs, seq, width = tokens.shape
    rows = seqs * seq
    units = w_up.shape[2]
    per = width // n
    me = lax.axis_index("fsdp").astype(jnp.int32)

    places = jnp.arange(seq, dtype=jnp.int32)
    inside = places[None, :] < lengths[:, None]
    alive = jnp.arange(seqs, dtype=jnp.int32) < live_batches[0]
    key_mask = jnp.where(inside, 0.0, big_negative).astype(f32).reshape(rows, 1)
    valid = jnp.where(inside & alive[:, None], 1.0, 0.0).astype(f32).reshape(rows, 1)
    ones = jnp.ones((rows, 1), f32)

    own_small = jnp.concatenate([up_bias.reshape(-1), biases.reshape(-1), norm_gains.reshape(-1)])
    small_all = gather_small(own_small, n, me)
    cut_a = LAYERS * units // n
    cut_b = cut_a + LAYERS * 6 * per
    up_bias_all = small_all[:, :cut_a].reshape(n, LAYERS, units // n).transpose(1, 0, 2).reshape(LAYERS, 1, units)
    bias_all = small_all[:, cut_a:cut_b].reshape(n, LAYERS, 6, per).transpose(1, 2, 0, 3).reshape(LAYERS, 6, width)
    gain_all = small_all[:, cut_b:].reshape(n, LAYERS, 2, per).transpose(1, 2, 0, 3).reshape(LAYERS, 2, width)
    smalls = jnp.concatenate([bias_all, gain_all], axis=1)

    chip_bits = []
    bit = 2
    while bit < n:
        chip_bits.append(bit)
        bit *= 2
    upward = tuple(chip_bits + [1])
    downward = tuple(chip_bits[::-1] + [1])

    attend_orders, ffn_orders = (upward, downward), (downward, upward)
    qkv, out, up, down = [None] * LAYERS, [None] * LAYERS, [None] * LAYERS, [None] * LAYERS
    qkv[0], out[0] = gather_weights(n, 0, (w_qkv, w_out), attend_orders, 0)

    current = tokens.reshape(rows, width)
    base = current
    saved = []
    for layer in range(LAYERS):
        last = layer == LAYERS - 1
        q, k, v, ctx, lse, mid, low, n1, r1, up[layer], down[layer] = attend_forward(
            n, current, smalls[layer], key_mask, qkv[layer], out[layer], seqs,
            layer, (w_up, w_down), ffn_orders, 1 + 2 * layer,
        )
        results = ffn_forward(
            n, mid, low, smalls[layer], up_bias_all[layer], valid, up[layer], down[layer], last,
            layer + 1, () if last else (w_qkv, w_out), () if last else attend_orders, 2 + 2 * layer,
        )
        act, slope, n2, r2, current = results[:5]
        saved.append((base, q, k, v, ctx, lse, low, n1, r1, act, slope, n2, r2))
        if not last:
            base, qkv[layer + 1], out[layer + 1] = results[5:]
    outputs = current.reshape(seqs, seq, width)

    grad = cotangent.reshape(rows, width)
    grad_valid = valid
    small_rows = [None] * LAYERS
    attend_halves, attend_reduced, ffn_done, attend_done = None, None, [None] * LAYERS, [None] * LAYERS
    ffn_reduced = None
    for layer in range(LAYERS - 1, -1, -1):
        first = layer == LAYERS - 1
        base, q, k, v, ctx, lse, low, n1, r1, act, slope, n2, r2 = saved[layer]
        results = ffn_backward(
            n, reps, grad, grad_valid, n2, r2, low, n1, r1, smalls[layer], act, slope, up[layer], down[layer],
            () if first else (*attend_halves, ffn_reduced), 10 + layer,
        )
        gs1, ga1, sums, up_sum, down_keep, down_send, up_keep, up_send = results[:8]
        if not first:
            attend_reduced, ffn_done[layer + 1] = results[8:]
        ffn_halves = (
            down_keep,
            up_keep.reshape(n // 2, -1, width),
            down_send,
            up_send.reshape(n // 2, -1, width),
        )
        results = attend_backward(
            n, reps, ga1, gs1, base, key_mask, q, k, v, ctx, lse, qkv[layer], out[layer], seqs,
            f32 if layer else bf16, ffn_halves + (() if first else (attend_reduced,)), 20 + layer,
        )
        grad, proj_sums = results[:2]
        attend_halves, ffn_reduced = results[2:6], results[6]
        if not first:
            attend_done[layer + 1] = results[7]
        grad_valid = ones
        small_rows[layer] = jnp.concatenate(
            [sums[:6], proj_sums[:2], up_sum.reshape(units // width, width), jnp.zeros((8 - units // width, width), f32)]
        )
    grad_tokens = grad.reshape(seqs, seq, width)
    ffn_done[0], attend_done[0], small_total = last_sums(
        n, reps, attend_halves, ffn_reduced, jnp.concatenate(small_rows), 30
    )

    ffn_rows, attend_rows = units // n, 2 * per
    both_ffn = jnp.stack([done[:, :ffn_rows] for done in ffn_done])
    both_attend = jnp.stack([done[:, :attend_rows] for done in attend_done])
    grad_down = both_ffn[:, 0].astype(f32)
    grad_up = both_ffn[:, 1].reshape(LAYERS, units // width, per, width).transpose(0, 2, 1, 3)
    grad_up = grad_up.reshape(LAYERS, per, units).astype(f32)
    parts = both_attend.reshape(LAYERS, 4, per, width)
    grad_qkv = parts[:, :3].transpose(0, 2, 1, 3).reshape(LAYERS, per, 3 * width).astype(f32)
    grad_out = parts[:, 3].astype(f32)

    small_total = small_total.reshape(LAYERS, 16, width)
    mine = lax.dynamic_slice_in_dim(small_total[:, :8], me * per, per, axis=2)
    grad_biases = jnp.stack([mine[:, at] for at in (6, 7, 5, 2, 4, 1)], axis=1)
    grad_gains = jnp.stack([mine[:, at] for at in (3, 0)], axis=1)
    up_rows = small_total[:, 8 : 8 + units // width].reshape(LAYERS, units)
    grad_up_bias = lax.dynamic_slice_in_dim(up_rows, me * (units // n), units // n, axis=1)
    return (outputs, grad_tokens, grad_qkv, grad_out, grad_up, grad_down, grad_up_bias, grad_biases, grad_gains)


def solution(mesh):
    both = ("rep", "fsdp")
    placed = (
        P(both, None, None),
        P(both, None, None),
        P(both),
        P(both),
        P(None, "fsdp", None),
        P(None, "fsdp", None),
        P(None, "fsdp", None),
        P(None, "fsdp", None),
        P(None, "fsdp"),
        P(None, None, "fsdp"),
        P(None, None, "fsdp"),
    )
    return jax.shard_map(
        functools.partial(on_device, mesh.shape["fsdp"], mesh.shape["rep"]),
        mesh=mesh,
        in_specs=placed,
        out_specs=(
            P(both, None, None),
            P(both, None, None),
            P(None, "fsdp", None),
            P(None, "fsdp", None),
            P(None, "fsdp", None),
            P(None, "fsdp", None),
            P(None, "fsdp"),
            P(None, None, "fsdp"),
            P(None, None, "fsdp"),
        ),
        check_vma=False,
    )
```

```python
import functools

import jax
import jax.numpy as jnp
from jax import lax
from jax.experimental import pallas as pl
from jax.experimental.pallas import tpu as pltpu
from jax.sharding import PartitionSpec as P

HEAD = 64
LAYERS = 2
GROUP = 256
ROWS = 256
VMEM_BYTES = 60 * 1024 * 1024
UP_PARTS = 4
EARLY = 2

epsilon = 1e-05
big_negative = -1000000000.0
root_half = 0.7071067811865476
inv_root_tau = 0.3989422804014327
f32 = jnp.float32
bf16 = jnp.bfloat16


def dot_nn(a, b):
    return lax.dot_general(a, b, (((1,), (0,)), ((), ())), preferred_element_type=f32)


def dot_nt(a, b):
    return lax.dot_general(a, b, (((1,), (1,)), ((), ())), preferred_element_type=f32)


def whole(shape):
    zeros = (0,) * len(shape)
    return pl.BlockSpec(shape, lambda *_: zeros, pipeline_mode=pl.Buffered(1))


def column_block(rows, width):
    return pl.BlockSpec((rows, width), lambda j, *_: (0, j))


ANY = pl.BlockSpec(memory_space=pl.ANY)


def flip(index, mask):
    bit = 1
    while bit <= mask:
        if mask & bit:
            index = index + bit - 2 * bit * ((index // bit) % 2)
        bit *= 2
    return index


def exclusive_or(a, b, count):
    total, bit = 0, 1
    while bit < count:
        total = total + bit * ((a // bit + b // bit) % 2)
        bit *= 2
    return total


def greet(n, bits):
    me = lax.axis_index("fsdp")
    barrier = pltpu.get_barrier_semaphore()
    for bit in bits:
        pl.semaphore_signal(barrier, inc=1, device_id={"fsdp": flip(me, bit)}, device_id_type=pl.DeviceIdType.MESH)
    pl.semaphore_wait(barrier, len(bits))


class Gather:
    def __init__(self, own, full, order, send_sems, recv_sems, local_sem):
        self.own, self.full, self.order = own, full, order
        self.send_sems, self.recv_sems, self.local_sem = send_sems, recv_sems, local_sem
        self.me = lax.axis_index("fsdp")
        self.depth = own.shape[0]

    def rows(self, mask):
        return self.full.at[pl.ds(pl.multiple_of(flip(self.me, mask) * self.depth, 16), self.depth), :]

    def round_masks(self, round_at):
        earlier = self.order[:round_at]
        masks = [0]
        for bit in earlier:
            masks += [mask | bit for mask in masks]
        return [mask | self.order[round_at] for mask in masks]

    def copy(self, mask):
        bit = [bit for bit in self.order if bit & mask][-1]
        held = mask ^ bit
        return pltpu.make_async_remote_copy(
            src_ref=self.own if held == 0 else self.rows(held),
            dst_ref=self.rows(held),
            send_sem=self.send_sems.at[mask],
            recv_sem=self.recv_sems.at[mask],
            device_id={"fsdp": flip(self.me, bit)},
            device_id_type=pl.DeviceIdType.MESH,
        )

    def begin(self, round_at):
        if round_at == 0:
            pltpu.make_async_copy(self.own, self.rows(0), self.local_sem).start()
        self.copy(self.order[round_at]).start()

    def onward(self, round_at):
        masks = self.round_masks(round_at)
        for mask in masks:
            self.copy(mask).wait_recv()
        for bit in self.order[round_at + 1 :]:
            for mask in masks:
                self.copy(mask | bit).start()

    def end(self):
        pltpu.make_async_copy(self.own, self.rows(0), self.local_sem).wait()
        for round_at in range(len(self.order)):
            for mask in self.round_masks(round_at):
                self.copy(mask).wait_send()


def begin_all(n, gathers):
    rounds = len(gathers[0].order)
    greet(n, gathers[0].order)
    for round_at in range(rounds):
        for gather in gathers:
            gather.begin(round_at)


def onward_all(gathers, round_at):
    for gather in gathers:
        gather.onward(round_at)


def end_all(gathers):
    for gather in gathers:
        gather.end()


def make_gathers(layer, parts, shards, wholes, sems):
    send_sems, recv_sems, local_sems = sems
    gathers = []
    for at, ((which, column, width, order), full) in enumerate(zip(parts, wholes)):
        own = shards[which].at[layer, :, pl.ds(column, width)]
        gathers.append(Gather(own, full, order, send_sems.at[at], recv_sems.at[at], local_sems.at[at]))
    return gathers


def parts_of(which, shard, count, orders, first=0):
    step = shard.shape[2] // count
    return [(which, at * step, step, orders[at % 2]) for at in range(first, count)]


def gather_sems(n, count):
    return [
        pltpu.SemaphoreType.DMA((count, n)),
        pltpu.SemaphoreType.DMA((count, n)),
        pltpu.SemaphoreType.DMA((count,)),
    ]


def wholes_of(n, shards, parts):
    return tuple(
        jax.ShapeDtypeStruct((shards[which].shape[1] * n, width), shards[which].dtype) for which, _, width, _ in parts
    )


def gather_kernel(n, layer, parts, shard_count, *refs):
    shards, wholes = refs[:shard_count], refs[shard_count : shard_count + len(parts)]
    gathers = make_gathers(layer, parts, shards, wholes, refs[shard_count + len(parts) :])
    begin_all(n, gathers)
    for round_at in range(len(gathers[0].order)):
        onward_all(gathers, round_at)
    end_all(gathers)


def gather_weights(n, layer, shards, parts, collective_id):
    return pl.pallas_call(
        functools.partial(gather_kernel, n, layer, parts, len(shards)),
        out_shape=wholes_of(n, shards, parts),
        in_specs=[ANY] * len(shards),
        out_specs=tuple([ANY] * len(parts)),
        scratch_shapes=gather_sems(n, len(parts)),
        compiler_params=pltpu.CompilerParams(collective_id=collective_id, has_side_effects=True),
        name="gather_weights",
    )(*shards)


def part_copies(sources, target, sems, first=0):
    copies, column = [], 0
    for at, source in enumerate(sources):
        width = source.shape[1]
        copies.append(pltpu.make_async_copy(source, target.at[:, pl.ds(column, width)], sems.at[first + at]))
        column += width
    return copies


def both_copies(sources, count, targets, sems):
    return part_copies(sources[:count], targets[0], sems), part_copies(sources[count:], targets[1], sems, count)


BLOCK = 96


def add_rows(rows, target, sources):
    def step(block, carry):
        at = pl.ds(pl.multiple_of(block * BLOCK, BLOCK), BLOCK)
        total = None
        for ref, lead in sources:
            value = ref[(*lead, at)].astype(f32)
            total = value if total is None else total + value
        ref, lead = target
        ref[(*lead, at)] = total.astype(ref.dtype)
        return carry

    lax.fori_loop(0, rows // BLOCK, step, 0)


class Reduce:
    def __init__(self, halves, scratch, bits):
        self.keep, self.send = halves[:2], halves[2:]
        self.held, self.arrived = scratch[:2]
        hops = len(bits)
        self.hop_in = scratch[2 : 2 + hops]
        self.sems, self.hop_send, self.hop_recv = scratch[2 + hops : 5 + hops]
        self.orders = (bits[::-1], bits)
        self.chips, self.rows = self.held.shape[1:3]
        self.me = lax.axis_index("fsdp")

    def load(self, stream):
        return pltpu.make_async_copy(self.keep[stream], self.held.at[stream], self.sems.at[0, stream])

    def core_copy(self, stream):
        return pltpu.make_async_remote_copy(
            src_ref=self.send[stream],
            dst_ref=self.arrived.at[stream],
            send_sem=self.sems.at[1, stream],
            recv_sem=self.sems.at[2, stream],
            device_id={"fsdp": flip(self.me, 1)},
            device_id_type=pl.DeviceIdType.MESH,
        )

    def begin(self):
        for stream in range(2):
            self.core_copy(stream).start()
            self.load(stream).start()

    def leaving(self, stream, hop):
        gone = [bit // 2 for bit in self.orders[stream][:hop]]
        half = self.orders[stream][hop] // 2
        return half, [p for p in range(self.chips) if p & half and not any(p & g for g in gone)]

    def terms(self, stream, place, hops):
        found = [(self.held, (stream, place)), (self.arrived, (stream, place))]
        for hop in range(hops):
            half, places = self.leaving(stream, hop)
            found.append((self.hop_in[hop], (stream, places.index(place | half))))
        return found

    def hop_copy(self, stream, hop, slot, place):
        return pltpu.make_async_remote_copy(
            src_ref=self.held.at[stream, place],
            dst_ref=self.hop_in[hop].at[stream, slot],
            send_sem=self.hop_send.at[stream, hop, slot],
            recv_sem=self.hop_recv.at[stream, hop, slot],
            device_id={"fsdp": flip(self.me, self.orders[stream][hop])},
            device_id_type=pl.DeviceIdType.MESH,
        )

    def wait_before(self, stream, hop):
        if hop == 0:
            self.load(stream).wait()
            self.core_copy(stream).wait_recv()
        else:
            _, places = self.leaving(stream, hop - 1)
            for slot, place in enumerate(places):
                self.hop_copy(stream, hop - 1, slot, place).wait_recv()

    def hop(self, at):
        for stream in range(2):
            self.wait_before(stream, at)
            _, places = self.leaving(stream, at)
            for place in places:
                add_rows(self.rows, (self.held, (stream, place)), self.terms(stream, place, at))
            for slot, place in enumerate(places):
                self.hop_copy(stream, at, slot, place).start()

    def finish(self, result):
        hops = len(self.hop_in)
        for stream in range(2):
            self.wait_before(stream, hops)
            add_rows(self.rows, (result, (stream,)), self.terms(stream, 0, hops))
        for stream in range(2):
            self.core_copy(stream).wait_send()
            for hop in range(hops):
                _, places = self.leaving(stream, hop)
                for slot, place in enumerate(places):
                    self.hop_copy(stream, hop, slot, place).wait_send()


def reduce_scratch(chips, rows, width, hops):
    return (
        [pltpu.VMEM((2, chips, rows, width), bf16)] * 2
        + [pltpu.VMEM((2, chips >> (hop + 1), rows, width), bf16) for hop in range(hops)]
        + [pltpu.SemaphoreType.DMA((3, 2))]
        + [pltpu.SemaphoreType.DMA((2, hops, chips // 2))] * 2
    )


class Spread:
    def __init__(self, count, scratch, first=0):
        self.first = first
        self.total, self.outgoing, self.incoming, self.whole, self.load_sems, self.sems = scratch
        self.bits = []
        bit = 1
        while bit < count:
            self.bits.append(bit)
            bit *= 2
        self.rank = lax.axis_index("rep")
        self.streams, self.rows = self.total.shape[:2]

    def load(self, stream, source):
        target = self.total.at[stream, pl.ds(0, source.shape[1])]
        return pltpu.make_async_copy(source.at[self.first + stream], target, self.load_sems.at[stream])

    def begin(self, source):
        for stream in range(self.streams):
            self.load(stream, source).start()

    def loaded(self, source):
        for stream in range(self.streams):
            self.load(stream, source).wait()
        self.tick(0)

    def side(self, bit):
        return (self.rank // bit) % 2

    def span(self, stage):
        start, size = 0, self.rows
        for bit in self.bits[:stage]:
            size //= 2
            start = start + self.side(bit) * size
        return start, size

    def down_copy(self, stream, stage):
        size = self.rows >> (stage + 1)
        at = pl.ds(self.rows - (self.rows >> stage), size)
        return pltpu.make_async_remote_copy(
            src_ref=self.outgoing.at[stream, at],
            dst_ref=self.incoming.at[stream, at],
            send_sem=self.sems.at[0, stream, stage],
            recv_sem=self.sems.at[1, stream, stage],
            device_id={"rep": flip(self.rank, self.bits[stage])},
            device_id_type=pl.DeviceIdType.MESH,
        )

    def up_copy(self, stream, stage):
        start, size = self.span(stage + 1)
        at = pl.ds(pl.multiple_of(start, 16), size)
        return pltpu.make_async_remote_copy(
            src_ref=self.whole.at[stream, at],
            dst_ref=self.whole.at[stream, at],
            send_sem=self.sems.at[2, stream, stage],
            recv_sem=self.sems.at[3, stream, stage],
            device_id={"rep": flip(self.rank, self.bits[stage])},
            device_id_type=pl.DeviceIdType.MESH,
        )

    def act(self, stream, tick):
        stages = len(self.bits)
        if 0 < tick <= stages:
            stage = tick - 1
            self.down_copy(stream, stage).wait_recv()
            start, size = self.span(tick)
            base = self.rows - (self.rows >> stage)
            at = pl.ds(pl.multiple_of(start, 16), size)
            self.total[stream, at] += self.incoming[stream, pl.ds(base, size)].astype(f32)
        if tick < stages:
            bit = self.bits[tick]
            start, size = self.span(tick)
            size //= 2
            base = self.rows - (self.rows >> tick)
            at = pl.ds(pl.multiple_of(start + (1 - self.side(bit)) * size, 16), size)
            self.outgoing[stream, pl.ds(base, size)] = self.total[stream, at].astype(bf16)
            self.down_copy(stream, tick).start()
        elif tick == stages:
            start, size = self.span(stages)
            at = pl.ds(pl.multiple_of(start, 16), size)
            self.whole[stream, at] = self.total[stream, at].astype(bf16)
            self.up_copy(stream, stages - 1).start()
        else:
            stage = 2 * stages - tick
            self.up_copy(stream, stage).wait_recv()
            if stage:
                self.up_copy(stream, stage - 1).start()

    @property
    def ticks(self):
        return 2 * len(self.bits) + self.streams

    def tick(self, tick):
        for stream in range(self.streams):
            if 0 <= tick - stream <= 2 * len(self.bits):
                self.act(stream, tick - stream)

    def end(self):
        for stream in range(self.streams):
            for stage in range(len(self.bits)):
                self.down_copy(stream, stage).wait_send()
                self.up_copy(stream, stage).wait_send()


CHAIN = 4
PIECES = 2


class Chain(Spread):
    def __init__(self, count, scratch, first=0):
        super().__init__(count, scratch, first)
        self.inner = (self.rank == 1) | (self.rank == 2)
        self.chunks = self.streams * PIECES

    def place(self, chunk):
        size = self.rows // PIECES
        return chunk // PIECES, pl.ds((chunk % PIECES) * size, size)

    def copy(self, leg, chunk):
        stream, at = self.place(chunk)
        source = self.whole if leg == 2 else self.outgoing
        target = self.whole.at[stream, at] if leg == 2 else self.incoming.at[leg * self.streams + stream, at]
        return pltpu.make_async_remote_copy(
            src_ref=source.at[stream, at],
            dst_ref=target,
            send_sem=self.sems.at[2 * leg, chunk],
            recv_sem=self.sems.at[2 * leg + 1, chunk],
            device_id={"rep": flip(self.rank, 3 if leg == 1 else 1)},
            device_id_type=pl.DeviceIdType.MESH,
        )

    def act(self, chunk, tick):
        stream, at = self.place(chunk)

        if tick == 0:

            @pl.when(jnp.logical_not(self.inner))
            def _():
                self.outgoing[stream, at] = self.total[stream, at].astype(bf16)
                self.copy(0, chunk).start()

        elif tick == 3:

            @pl.when(jnp.logical_not(self.inner))
            def _():
                self.copy(2, chunk).wait_recv()

        else:

            @pl.when(self.inner)
            def _():
                self.copy(tick - 1, chunk).wait_recv()
                arrived = self.incoming[(tick - 1) * self.streams + stream, at].astype(f32)
                if tick == 1:
                    self.outgoing[stream, at] = (self.total[stream, at] + arrived).astype(bf16)
                else:
                    self.whole[stream, at] = (self.outgoing[stream, at].astype(f32) + arrived).astype(bf16)
                self.copy(tick, chunk).start()

    @property
    def ticks(self):
        return self.chunks + 3

    def tick(self, tick):
        for chunk in range(self.chunks):
            if tick == 0:
                self.act(chunk, 0)
            elif 1 <= tick - chunk <= 3:
                self.act(chunk, tick - chunk)

    def end(self):
        for chunk in range(self.chunks):

            @pl.when(self.inner)
            def _():
                self.copy(1, chunk).wait_send()
                self.copy(2, chunk).wait_send()

            @pl.when(jnp.logical_not(self.inner))
            def _():
                self.copy(0, chunk).wait_send()


def make_spread(count, scratch, first=0):
    return (Chain if count == CHAIN else Spread)(count, scratch, first)


def rep_masks(count):
    return [1, 3] if count == CHAIN else bits_below(count)


def padded(rows, count):
    return -(-rows // (16 * count)) * 16 * count


def spread_scratch(rows, width, count, streams=2):
    rows = padded(rows, count)
    stages = count.bit_length() - 1
    return [
        pltpu.VMEM((streams, rows, width), f32),
        pltpu.VMEM((streams, rows, width), bf16),
        pltpu.VMEM((2 * streams if count == CHAIN else streams, rows, width), bf16),
        pltpu.VMEM((streams, rows, width), bf16),
        pltpu.SemaphoreType.DMA((streams,)),
        pltpu.SemaphoreType.DMA((6, streams * PIECES) if count == CHAIN else (4, streams, stages)),
    ]


def greet_both(n, reps, fsdp_bits, rep_bits):
    me, rank = lax.axis_index("fsdp"), lax.axis_index("rep")
    barrier = pltpu.get_barrier_semaphore()
    for bit in fsdp_bits:
        pl.semaphore_signal(barrier, inc=1, device_id={"fsdp": flip(me, bit)}, device_id_type=pl.DeviceIdType.MESH)
    for bit in rep_bits:
        pl.semaphore_signal(barrier, inc=1, device_id={"rep": flip(rank, bit)}, device_id_type=pl.DeviceIdType.MESH)
    pl.semaphore_wait(barrier, len(fsdp_bits) + len(rep_bits))


def bits_below(count, first=1):
    bits = []
    while first < count:
        bits.append(first)
        first *= 2
    return bits


def norm_forward(total, gain, shift):
    middle = jnp.mean(total, axis=-1, keepdims=True)
    centred = total - middle
    spread = jnp.mean(centred * centred, axis=-1, keepdims=True)
    scaling = lax.rsqrt(spread + epsilon)
    normed = centred * scaling
    return normed * gain + shift, normed, scaling


def norm_backward(grad, normed, scaling, gain):
    scaled = grad * gain
    first = jnp.mean(scaled, axis=-1, keepdims=True)
    second = jnp.mean(scaled * normed, axis=-1, keepdims=True)
    return scaling * (scaled - first - normed * second)


def head_mask(shape, head):
    lanes = lax.broadcasted_iota(jnp.int32, shape, 1)
    return (lanes >= head * HEAD) & (lanes < (head + 1) * HEAD)


def attend_forward_kernel(n, seqs, layer, counts, parts, x_ref, small_ref, mask_ref, *refs):
    first, given, taken = counts
    sources, shards, refs = refs[:given], refs[given : given + taken], refs[given + taken :]
    count = len(parts)
    q_ref, k_ref, v_ref, ctx_ref, lse_ref, mid_ref, low_ref, n1_ref, r1_ref = refs[:9]
    wholes, refs = refs[9 : 9 + count], refs[9 + count :]
    base, w_qkv, w_out, acc, sems = refs[:5]
    gathers = make_gathers(layer, parts, shards, wholes, refs[5:])
    step, steps = pl.program_id(0), pl.num_programs(0)
    rows, width = x_ref.shape
    seq = rows // seqs
    heads = GROUP // HEAD
    copies = sum(both_copies(sources, first, (w_qkv, w_out), sems), [])

    @pl.when(step == 0)
    def _():
        for copy in copies:
            copy.start()
        begin_all(n, gathers)
        base[...] = x_ref[...].astype(bf16)
        acc[...] = x_ref[...].astype(f32) + small_ref[2:3, :]
        for copy in copies:
            copy.wait()

    columns = pl.multiple_of(step * GROUP, GROUP)
    q_bias = small_ref[0:1, pl.ds(columns, GROUP)]
    v_bias = small_ref[1:2, pl.ds(columns, GROUP)]

    def project(block, carry):
        at = pl.ds(pl.multiple_of(block * ROWS, ROWS), ROWS)
        low = base[at, :]
        q = dot_nn(low, w_qkv[:, pl.ds(columns, GROUP)])
        q_ref[at, :] = ((q + q_bias) * HEAD ** (-0.5)).astype(bf16)
        k = dot_nn(low, w_qkv[:, pl.ds(pl.multiple_of(width + columns, GROUP), GROUP)])
        k_ref[at, :] = k.astype(bf16)
        v = dot_nn(low, w_qkv[:, pl.ds(pl.multiple_of(2 * width + columns, GROUP), GROUP)])
        v_ref[at, :] = (v + v_bias).astype(bf16)
        return carry

    lax.fori_loop(0, rows // ROWS, project, 0)

    def attend(s, carry):
        at = pl.ds(pl.multiple_of(s * seq, seq), seq)
        q, k = q_ref[at, :], k_ref[at, :]
        v_turned = v_ref[at, :].T
        key_mask = mask_ref[at, :]
        parts = []
        for head in range(heads):
            q_head = jnp.where(head_mask(q.shape, head), q, jnp.zeros_like(q))
            scores = dot_nt(k, q_head) + key_mask
            peak = jnp.max(scores, axis=0, keepdims=True)
            raised = jnp.exp(scores - peak)
            total = jnp.sum(raised, axis=0, keepdims=True)
            mixed = dot_nn(v_turned[head * HEAD : (head + 1) * HEAD, :], raised.astype(bf16))
            parts.append((mixed / total).astype(bf16))
            lse_ref[0, pl.ds(s * heads + head, 1), :] = peak + jnp.log(total)
        ctx_ref[at, :] = jnp.concatenate(parts, axis=0).T
        return carry

    lax.fori_loop(0, seqs, attend, 0)

    @pl.when(step == 1)
    def _():
        onward_all(gathers, 0)

    def mix(block, carry):
        at = pl.ds(pl.multiple_of(block * ROWS, ROWS), ROWS)
        acc[at, :] += dot_nn(ctx_ref[at, :], w_out[pl.ds(columns, GROUP), :])
        return carry

    lax.fori_loop(0, rows // ROWS, mix, 0)

    @pl.when(step == steps - 1)
    def _():
        def finish(block, carry):
            at = pl.ds(pl.multiple_of(block * ROWS, ROWS), ROWS)
            mid, normed, scaling = norm_forward(acc[at, :], small_ref[6:7, :], small_ref[4:5, :])
            mid_ref[at, :] = mid
            low_ref[at, :] = mid.astype(bf16)
            n1_ref[at, :] = normed.astype(bf16)
            r1_ref[at, :] = scaling
            return carry

        lax.fori_loop(0, rows // ROWS, finish, 0)
        for round_at in range(1, len(gathers[0].order)):
            onward_all(gathers, round_at)
        end_all(gathers)


def attend_forward(n, x, small, key_mask, w_qkv, w_out, seqs, layer, shards, parts, collective_id):
    rows, width = x.shape
    steps = width // GROUP
    seq = rows // seqs
    wide = jax.ShapeDtypeStruct((rows, width), bf16)
    heads = GROUP // HEAD
    return pl.pallas_call(
        functools.partial(
            attend_forward_kernel, n, seqs, layer, (len(w_qkv), len(w_qkv) + len(w_out), len(shards)), parts
        ),
        out_shape=(
            wide,
            wide,
            wide,
            wide,
            jax.ShapeDtypeStruct((steps, seqs * heads, seq), f32),
            jax.ShapeDtypeStruct((rows, width), f32),
            wide,
            wide,
            jax.ShapeDtypeStruct((rows, 1), f32),
        )
        + wholes_of(n, shards, parts),
        grid_spec=pltpu.PrefetchScalarGridSpec(
            num_scalar_prefetch=0,
            grid=(steps,),
            in_specs=[whole((rows, width)), whole(small.shape), whole((rows, 1))]
            + [ANY] * (len(w_qkv) + len(w_out) + len(shards)),
            out_specs=[column_block(rows, GROUP)] * 4
            + [
                pl.BlockSpec((1, seqs * heads, seq), lambda j, *_: (j, 0, 0)),
                whole((rows, width)),
                whole((rows, width)),
                whole((rows, width)),
                whole((rows, 1)),
            ]
            + [ANY] * len(parts),
            scratch_shapes=[
                pltpu.VMEM((rows, width), bf16),
                pltpu.VMEM((width, 3 * width), bf16),
                pltpu.VMEM((width, width), bf16),
                pltpu.VMEM((rows, width), f32),
                pltpu.SemaphoreType.DMA((len(w_qkv) + len(w_out),)),
            ]
            + gather_sems(n, len(parts)),
        ),
        compiler_params=pltpu.CompilerParams(
            dimension_semantics=("arbitrary",),
            vmem_limit_bytes=VMEM_BYTES,
            collective_id=collective_id,
            has_side_effects=True,
        ),
        cost_estimate=cost(8 * rows * width * width + 16 * rows * seq * width, 20 * rows * width),
        name="attend_forward",
    )(x, small, key_mask, *w_qkv, *w_out, *shards)


def ffn_forward_kernel(n, last, layer, counts, parts, mid_ref, low_ref, small_ref, up_bias_ref, valid_ref, *refs):
    first, given, taken = counts
    sources, shards, refs = refs[:given], refs[given : given + taken], refs[given + taken :]
    count = len(parts)
    act_ref, slope_ref, n2_ref, r2_ref, hid_ref = refs[:5]
    refs = refs[5:]
    if not last:
        hid_low_ref, refs = refs[0], refs[1:]
    wholes, refs = refs[:count], refs[count:]
    w_up, w_down, acc, sems = refs[:4]
    gathers = make_gathers(layer, parts, shards, wholes, refs[4:]) if count else []
    step, steps = pl.program_id(0), pl.num_programs(0)
    rows, width = mid_ref.shape
    chunk = act_ref.shape[1]
    copies = sum(both_copies(sources, first, (w_up, w_down), sems), [])

    @pl.when(step == 0)
    def _():
        for copy in copies:
            copy.start()
        if gathers:
            begin_all(n, gathers)
        acc[...] = mid_ref[...] + small_ref[3:4, :]
        for copy in copies:
            copy.wait()

    if gathers:

        @pl.when(step == 2)
        def _():
            onward_all(gathers, 0)

    columns = pl.multiple_of(step * chunk, chunk)
    tile = 256

    def block_step(block, carry):
        at = pl.ds(pl.multiple_of(block * ROWS, ROWS), ROWS)
        low = low_ref[at, :]
        acts = []
        for part in range(chunk // tile):
            inside = slice(part * tile, (part + 1) * tile)
            at_units = pl.ds(pl.multiple_of(columns + part * tile, tile), tile)
            pre = dot_nn(low, w_up[:, at_units]) + up_bias_ref[:, inside]
            share = 0.5 * (1.0 + lax.erf(pre * root_half))
            act = (pre * share).astype(bf16)
            act_ref[at, inside] = act
            acts.append(act)
            density = inv_root_tau * jnp.exp(-0.5 * pre * pre)
            slope_ref[at, inside] = (share + pre * density).astype(bf16)
        acc[at, :] += dot_nn(jnp.concatenate(acts, axis=1), w_down[pl.ds(columns, chunk), :])
        return carry

    lax.fori_loop(0, rows // ROWS, block_step, 0)

    @pl.when(step == steps - 1)
    def _():
        def finish(block, carry):
            at = pl.ds(pl.multiple_of(block * ROWS, ROWS), ROWS)
            hidden, normed, scaling = norm_forward(acc[at, :], small_ref[7:8, :], small_ref[5:6, :])
            n2_ref[at, :] = normed.astype(bf16)
            r2_ref[at, :] = scaling
            if last:
                hid_ref[at, :] = (hidden * valid_ref[at, :]).astype(bf16)
            else:
                hid_ref[at, :] = hidden
                hid_low_ref[at, :] = hidden.astype(bf16)
            return carry

        lax.fori_loop(0, rows // ROWS, finish, 0)

    if gathers:

        @pl.when(step == steps - 1)
        def _():
            for round_at in range(1, len(gathers[0].order)):
                onward_all(gathers, round_at)
            end_all(gathers)


def ffn_forward(n, mid, low, small, up_bias, valid, w_up, w_down, last, layer, shards, parts, collective_id):
    rows, width = mid.shape
    units = up_bias.shape[1]
    chunk = width
    steps = units // chunk
    out_shape = [
        jax.ShapeDtypeStruct((rows, units), bf16),
        jax.ShapeDtypeStruct((rows, units), bf16),
        jax.ShapeDtypeStruct((rows, width), bf16),
        jax.ShapeDtypeStruct((rows, 1), f32),
        jax.ShapeDtypeStruct((rows, width), bf16 if last else f32),
    ]
    out_specs = [column_block(rows, chunk)] * 2 + [
        whole((rows, width)),
        whole((rows, 1)),
        whole((rows, width)),
    ]
    if not last:
        out_shape.append(jax.ShapeDtypeStruct((rows, width), bf16))
        out_specs.append(whole((rows, width)))
    out_shape += wholes_of(n, shards, parts)
    out_specs += [ANY] * len(parts)
    if parts:
        params = pltpu.CompilerParams(
            dimension_semantics=("arbitrary",),
            vmem_limit_bytes=VMEM_BYTES,
            collective_id=collective_id,
            has_side_effects=True,
        )
    else:
        params = pltpu.CompilerParams(dimension_semantics=("arbitrary",), vmem_limit_bytes=VMEM_BYTES)
    return pl.pallas_call(
        functools.partial(
            ffn_forward_kernel, n, last, layer, (len(w_up), len(w_up) + len(w_down), len(shards)), parts
        ),
        out_shape=tuple(out_shape),
        grid_spec=pltpu.PrefetchScalarGridSpec(
            num_scalar_prefetch=0,
            grid=(steps,),
            in_specs=[
                whole((rows, width)),
                whole((rows, width)),
                whole(small.shape),
                column_block(1, chunk),
                whole((rows, 1)),
            ]
            + [ANY] * (len(w_up) + len(w_down) + len(shards)),
            out_specs=out_specs,
            scratch_shapes=[
                pltpu.VMEM((width, units), bf16),
                pltpu.VMEM((units, width), bf16),
                pltpu.VMEM((rows, width), f32),
                pltpu.SemaphoreType.DMA((len(w_up) + len(w_down),)),
            ]
            + (gather_sems(n, len(parts)) if parts else []),
        ),
        compiler_params=params,
        cost_estimate=cost(8 * rows * width * units, 8 * rows * units),
        name="ffn_forward",
    )(mid, low, small, up_bias, valid, *w_up, *w_down, *shards)


def shard_copies(n, me, source_of, keep_of, send_of, sems):
    def each(start):
        for owner in range(n):
            mask = flip(me, owner)
            place = mask // 2

            @pl.when(mask % 2 == 0)
            def _():
                copy = pltpu.make_async_copy(source_of(owner), keep_of(place), sems.at[owner])
                copy.start() if start else copy.wait()

            @pl.when(mask % 2 == 1)
            def _():
                copy = pltpu.make_async_copy(source_of(owner), send_of(place), sems.at[owner])
                copy.start() if start else copy.wait()

    return each


def ffn_backward_kernel(n, reps, counts, carry, g_ref, valid_ref, n2_ref, r2_ref, low_ref, n1_ref, r1_ref, small_ref, act_ref, slope_ref, *refs):
    sources, refs = refs[: counts[1]], refs[counts[1] :]
    if carry:
        halves, spread_from, refs = refs[:4], refs[4], refs[5:]
    gs1_ref, ga1_ref, sums_ref, up_sum_ref, down_keep, down_send, up_keep, up_send = refs[:8]
    refs = refs[8:]
    if carry:
        reduced_ref, spread_ref, refs = refs[0], refs[1], refs[2:]
    w_up, w_down, gffn, gpre, acc, low_turned, d_down, d_up, sems, out_sems = refs[:10]
    if carry:
        hops = len(bits_below(n, 2))
        reduce = Reduce(halves, refs[10 : 15 + hops], bits_below(n, 2))
        spread = make_spread(reps, refs[15 + hops : 21 + hops])
        spread_sem = refs[21 + hops]
    step, steps = pl.program_id(0), pl.num_programs(0)
    me = lax.axis_index("fsdp")
    rows, width = acc.shape
    last_step = steps - 1
    if carry:
        out_copy = pltpu.make_async_copy(spread.whole, spread_ref, spread_sem)

        @pl.when(step == 0)
        def _():
            greet_both(n, reps, bits_below(n), rep_masks(reps))
            spread.begin(spread_from)
            reduce.begin()
            spread.loaded(spread_from)

        @pl.when(step == 1)
        def _():
            spread.tick(1)

        @pl.when(step == 2)
        def _():
            spread.tick(2)
            for hop in range(1, hops):
                reduce.hop(hop)

        @pl.when(step == 3)
        def _():
            reduce.finish(reduced_ref)
    chunk = act_ref.shape[1]
    per_down = down_keep.shape[1]
    per_up = up_keep.shape[2]
    tile = 256
    up_copies, down_copies = both_copies(sources, counts[0], (w_up, w_down), sems)

    @pl.when(step == 0)
    def _():
        for copy in down_copies:
            copy.start()
        for copy in up_copies:
            copy.start()
        sums_ref[...] = jnp.zeros_like(sums_ref)

        def prepare(block, carry):
            at = pl.ds(pl.multiple_of(block * ROWS, ROWS), ROWS)
            grad = g_ref[at, :].astype(f32) * valid_ref[at, :]
            normed = n2_ref[at, :].astype(f32)
            summed = norm_backward(grad, normed, r2_ref[at, :], small_ref[7:8, :])
            acc[at, :] = summed
            low = summed.astype(bf16)
            gffn[at, :] = low
            sums_ref[0:1, :] += jnp.sum(grad * normed, axis=0, keepdims=True)
            sums_ref[1:2, :] += jnp.sum(grad, axis=0, keepdims=True)
            sums_ref[2:3, :] += jnp.sum(low.astype(f32), axis=0, keepdims=True)
            low_turned[:, at] = low_ref[at, :].T
            return carry

        lax.fori_loop(0, rows // ROWS, prepare, 0)
        for copy in down_copies:
            copy.wait()
        for copy in up_copies:
            copy.wait()

    columns = pl.multiple_of(step * chunk, chunk)
    up_sum_ref[...] = jnp.zeros_like(up_sum_ref)

    def through(block, carry):
        at = pl.ds(pl.multiple_of(block * ROWS, ROWS), ROWS)
        grad = gffn[at, :]
        lows = []
        for part in range(chunk // tile):
            inside = slice(part * tile, (part + 1) * tile)
            at_units = pl.ds(pl.multiple_of(columns + part * tile, tile), tile)
            grad_act = dot_nt(grad, w_down[at_units, :])
            low = (grad_act * slope_ref[at, inside].astype(f32)).astype(bf16)
            gpre[at, inside] = low
            lows.append(low)
            up_sum_ref[:, inside] += jnp.sum(low.astype(f32), axis=0, keepdims=True)
        acc[at, :] += dot_nt(jnp.concatenate(lows, axis=1), w_up[:, pl.ds(columns, chunk)])
        return carry

    lax.fori_loop(0, rows // ROWS, through, 0)
    if carry:

        @pl.when(step == 0)
        def _():
            reduce.hop(0)

        @pl.when(step == 2)
        def _():
            spread.tick(3)

        @pl.when(step == 3)
        def _():
            for tick in range(4, spread.ticks):
                spread.tick(tick)
            out_copy.start()

    def down_out(which):
        def run(start):
            for local in range(chunk // per_down):
                owner = which * (chunk // per_down) + local
                mask = exclusive_or(me, owner, n)
                source = d_down.at[pl.ds(local * per_down, per_down), :]
                place = mask // 2

                @pl.when(mask % 2 == 0)
                def _():
                    copy = pltpu.make_async_copy(source, down_keep.at[place], out_sems.at[0, local])
                    copy.start() if start else copy.wait()

                @pl.when(mask % 2 == 1)
                def _():
                    copy = pltpu.make_async_copy(source, down_send.at[place], out_sems.at[0, local])
                    copy.start() if start else copy.wait()

        return run

    def up_out(which):
        return shard_copies(
            n,
            me,
            lambda owner: d_up.at[pl.ds(owner * per_up, per_up), :],
            lambda place: up_keep.at[place, which],
            lambda place: up_send.at[place, which],
            out_sems.at[1],
        )

    @pl.when(step > 0)
    def _():
        down_out(step - 1)(False)

    def down_part(part, carry):
        at = pl.ds(pl.multiple_of(part * tile, tile), tile)
        turned = act_ref[:, at].T
        d_down[at, :] = dot_nn(turned, gffn[...]).astype(bf16)
        return carry

    lax.fori_loop(0, chunk // tile, down_part, 0)
    down_out(step)(True)

    @pl.when(step > 0)
    def _():
        up_out(step - 1)(False)

    def up_part(part, carry):
        at = pl.ds(pl.multiple_of(part * tile, tile), tile)
        d_up[at, :] = dot_nn(low_turned[at, :], gpre[...]).astype(bf16)
        return carry

    lax.fori_loop(0, width // tile, up_part, 0)
    up_out(step)(True)

    @pl.when(step == steps - 1)
    def _():
        def finish(block, carry):
            at = pl.ds(pl.multiple_of(block * ROWS, ROWS), ROWS)
            grad = acc[at, :]
            normed = n1_ref[at, :].astype(f32)
            summed = norm_backward(grad, normed, r1_ref[at, :], small_ref[6:7, :])
            gs1_ref[at, :] = summed
            low = summed.astype(bf16)
            ga1_ref[at, :] = low
            sums_ref[3:4, :] += jnp.sum(grad * normed, axis=0, keepdims=True)
            sums_ref[4:5, :] += jnp.sum(grad, axis=0, keepdims=True)
            sums_ref[5:6, :] += jnp.sum(low.astype(f32), axis=0, keepdims=True)
            return carry

        lax.fori_loop(0, rows // ROWS, finish, 0)
        down_out(step)(False)
        up_out(step)(False)
        if carry:
            out_copy.wait()
            spread.end()


def remote_params(collective_id):
    return pltpu.CompilerParams(
        dimension_semantics=("arbitrary",),
        vmem_limit_bytes=VMEM_BYTES,
        collective_id=collective_id,
        has_side_effects=True,
    )


def ffn_backward(n, reps, grad, valid, n2, r2, low, n1, r1, small, act, slope, w_up, w_down, carry, collective_id):
    rows, width = grad.shape
    units = act.shape[1]
    chunk = width
    steps = units // chunk
    chips = n // 2
    hops = len(bits_below(n, 2))
    extra_out, extra_specs, extra_scratch = [], [], []
    if carry:
        reduced = (2,) + carry[0].shape[1:]
        spread_rows = carry[4].shape[1]
        extra_out = [
            jax.ShapeDtypeStruct(reduced, f32),
            jax.ShapeDtypeStruct((1, padded(spread_rows, reps), width), bf16),
        ]
        extra_specs = [whole(reduced), ANY]
        extra_scratch = reduce_scratch(chips, carry[0].shape[1], width, hops)
        extra_scratch += spread_scratch(spread_rows, width, reps, 1) + [pltpu.SemaphoreType.DMA]
    down_half = jax.ShapeDtypeStruct((chips, units // n, width), bf16)
    up_half = jax.ShapeDtypeStruct((chips, steps, width // n, chunk), bf16)
    return pl.pallas_call(
        functools.partial(ffn_backward_kernel, n, reps, (len(w_up), len(w_up) + len(w_down)), bool(carry)),
        out_shape=(
            jax.ShapeDtypeStruct((rows, width), f32),
            jax.ShapeDtypeStruct((rows, width), bf16),
            jax.ShapeDtypeStruct((8, width), f32),
            jax.ShapeDtypeStruct((1, units), f32),
            down_half,
            down_half,
            up_half,
            up_half,
            *extra_out,
        ),
        grid_spec=pltpu.PrefetchScalarGridSpec(
            num_scalar_prefetch=0,
            grid=(steps,),
            in_specs=[
                whole((rows, width)),
                whole((rows, 1)),
                whole((rows, width)),
                whole((rows, 1)),
                whole((rows, width)),
                whole((rows, width)),
                whole((rows, 1)),
                whole(small.shape),
                column_block(rows, chunk),
                column_block(rows, chunk),
            ]
            + [ANY] * (len(w_up) + len(w_down) + len(carry)),
            out_specs=[
                whole((rows, width)),
                whole((rows, width)),
                whole((8, width)),
                column_block(1, chunk),
            ]
            + [ANY] * 4
            + extra_specs,
            scratch_shapes=[
                pltpu.VMEM((width, units), bf16),
                pltpu.VMEM((units, width), bf16),
                pltpu.VMEM((rows, width), bf16),
                pltpu.VMEM((rows, chunk), bf16),
                pltpu.VMEM((rows, width), f32),
                pltpu.VMEM((width, rows), bf16),
                pltpu.VMEM((chunk, width), bf16),
                pltpu.VMEM((width, chunk), bf16),
                pltpu.SemaphoreType.DMA((len(w_up) + len(w_down),)),
                pltpu.SemaphoreType.DMA((2, n)),
            ]
            + extra_scratch,
        ),
        compiler_params=remote_params(collective_id)
        if carry
        else pltpu.CompilerParams(dimension_semantics=("arbitrary",), vmem_limit_bytes=VMEM_BYTES),
        cost_estimate=cost(10 * rows * width * units, 8 * rows * units),
        name="ffn_backward",
    )(grad, valid, n2, r2, low, n1, r1, small, act, slope, *w_up, *w_down, *carry)


def attend_backward_kernel(n, reps, seqs, counts, spreads, ga_ref, gs_ref, base_ref, mask_ref, q_ref, k_ref, v_ref, ctx_ref, lse_ref, *refs):
    sources, refs = refs[: counts[1]], refs[counts[1] :]
    halves, refs = refs[:4], refs[4:]
    if spreads:
        spread_from, refs = refs[:2], refs[2:]
    gh_ref, sums_ref, a_keep, b_keep, a_send, b_send, reduced_ref = refs[:7]
    refs = refs[7:]
    if spreads:
        spread_refs, refs = refs[:2], refs[2:]
    w_qkv, w_out, acc, base_turned, gctx, gproj, d_qkv, d_out, p_all, ds_all, sems, out_sems = refs[:12]
    hops = len(bits_below(n, 2))
    reduce = Reduce(halves, refs[12 : 17 + hops], bits_below(n, 2))
    step, steps = pl.program_id(0), pl.num_programs(0)
    me = lax.axis_index("fsdp")
    if spreads:
        rest = refs[17 + hops :]
        spread_list = [make_spread(reps, rest[:6]), make_spread(reps, rest[6:12], 1)]
        spread_copies = [
            pltpu.make_async_copy(spread.whole, ref, rest[12].at[at])
            for at, (spread, ref) in enumerate(zip(spread_list, spread_refs))
        ]

    def spread_tick(tick):
        if spreads:
            for spread, copy in zip(spread_list, spread_copies):
                if tick < spread.ticks:
                    spread.tick(tick)
                if tick == spread.ticks - 1:
                    copy.start()

    @pl.when(step == 0)
    def _():
        greet_both(n, reps, bits_below(n), rep_masks(reps) if spreads else [])
        if spreads:
            for spread, source in zip(spread_list, spread_from):
                spread.begin(source)
        reduce.begin()
        if spreads:
            for spread, source in zip(spread_list, spread_from):
                spread.loaded(source)

    if spreads:

        @pl.when(step == 1)
        def _():
            spread_tick(2)

        @pl.when(step == 2)
        def _():
            spread_tick(4)

    rows, width = ga_ref.shape
    seq = rows // seqs
    heads = GROUP // HEAD
    per = width // n
    tile = 256
    qkv_copies, out_copies = both_copies(sources, counts[0], (w_qkv, w_out), sems)

    @pl.when(step == 0)
    def _():
        for copy in out_copies:
            copy.start()
        for copy in qkv_copies:
            copy.start()

        def turn(block, carry):
            at = pl.ds(pl.multiple_of(block * ROWS, ROWS), ROWS)
            acc[at, :] = gs_ref[at, :]
            base_turned[:, at] = base_ref[at, :].T
            return carry

        lax.fori_loop(0, rows // ROWS, turn, 0)
        for copy in out_copies:
            copy.wait()
        for copy in qkv_copies:
            copy.wait()

    columns = pl.multiple_of(step * GROUP, GROUP)

    def through(block, carry):
        at = pl.ds(pl.multiple_of(block * ROWS, ROWS), ROWS)
        gctx[at, :] = dot_nt(ga_ref[at, :], w_out[pl.ds(columns, GROUP), :]).astype(bf16)
        return carry

    lax.fori_loop(0, rows // ROWS, through, 0)
    d_out[pl.ds(columns, GROUP), :] = dot_nn(ctx_ref[...].T, ga_ref[...]).astype(bf16)

    @pl.when(step == 2)
    def _():
        for hop in range(1, hops):
            reduce.hop(hop)

    def attend(s, carry):
        at = pl.ds(pl.multiple_of(s * seq, seq), seq)
        q, k, v, grad = q_ref[at, :], k_ref[at, :], v_ref[at, :], gctx[at, :]
        k_turned = k.T
        key_mask = mask_ref[at, :]
        parts, q_heads, g_heads = [], [], []
        for head in range(heads):
            inside = head_mask(q.shape, head)
            q_head = jnp.where(inside, q, jnp.zeros_like(q))
            g_head = jnp.where(inside, grad, jnp.zeros_like(grad))
            scores = dot_nt(k, q_head) + key_mask
            attention = jnp.exp(scores - lse_ref[0, pl.ds(s * heads + head, 1), :])
            weighted = attention * dot_nt(v, g_head)
            inner = jnp.sum(weighted, axis=0, keepdims=True)
            grad_scores = (weighted - attention * inner).astype(bf16)
            here = slice(head * seq, (head + 1) * seq)
            p_all[:, here] = attention.astype(bf16)
            ds_all[:, here] = grad_scores
            turned = dot_nn(k_turned[head * HEAD : (head + 1) * HEAD, :], grad_scores)
            parts.append(turned.astype(bf16) * HEAD ** (-0.5))
            q_heads.append(q_head)
            g_heads.append(g_head)
        gproj[at, 0:GROUP] = jnp.concatenate(parts, axis=0).T
        gproj[at, GROUP : 2 * GROUP] = dot_nn(ds_all[...], jnp.concatenate(q_heads, axis=0)).astype(bf16)
        gproj[at, 2 * GROUP : 3 * GROUP] = dot_nn(p_all[...], jnp.concatenate(g_heads, axis=0)).astype(bf16)
        return carry

    lax.fori_loop(0, seqs, attend, 0)
    sums_ref[...] = jnp.zeros_like(sums_ref)

    @pl.when(step == 0)
    def _():
        reduce.hop(0)
        spread_tick(1)

    if spreads:

        @pl.when(step == 1)
        def _():
            spread_tick(3)

        @pl.when(step == 2)
        def _():
            for tick in range(5, spread_list[0].ticks):
                spread_tick(tick)

    def onward(block, carry):
        at = pl.ds(pl.multiple_of(block * ROWS, ROWS), ROWS)
        term = dot_nt(gproj[at, 0:GROUP], w_qkv[:, pl.ds(columns, GROUP)])
        term += dot_nt(gproj[at, GROUP : 2 * GROUP], w_qkv[:, pl.ds(pl.multiple_of(width + columns, GROUP), GROUP)])
        term += dot_nt(gproj[at, 2 * GROUP : 3 * GROUP], w_qkv[:, pl.ds(pl.multiple_of(2 * width + columns, GROUP), GROUP)])
        sums_ref[0:1, :] += jnp.sum(gproj[at, 0:GROUP].astype(f32), axis=0, keepdims=True)
        sums_ref[1:2, :] += jnp.sum(gproj[at, 2 * GROUP : 3 * GROUP].astype(f32), axis=0, keepdims=True)
        acc[at, :] += term
        return carry

    lax.fori_loop(0, rows // ROWS, onward, 0)

    @pl.when(step == steps - 1)
    def _():
        gh_ref[...] = acc[...].astype(gh_ref.dtype)

    def place_of(part, a_half, b_half):
        return a_half if part < 2 else b_half

    def rows_of(part):
        return pl.ds((part % 2) * per, per)

    def qkv_out(which, start):
        for part in range(3):
            at = pl.ds(pl.multiple_of(which * GROUP, GROUP), GROUP)
            shard_copies(
                n,
                me,
                lambda owner: d_qkv.at[pl.ds(owner * per, per), pl.ds(part * GROUP, GROUP)],
                lambda place: place_of(part, a_keep, b_keep).at[place, rows_of(part), at],
                lambda place: place_of(part, a_send, b_send).at[place, rows_of(part), at],
                out_sems.at[part],
            )(start)

    @pl.when(step > 0)
    def _():
        qkv_out(step - 1, False)

    def weight_part(part, carry):
        at = pl.ds(pl.multiple_of(part * tile, tile), tile)
        d_qkv[at, :] = dot_nn(base_turned[at, :], gproj[...]).astype(bf16)
        return carry

    lax.fori_loop(0, width // tile, weight_part, 0)
    qkv_out(step, True)

    @pl.when(step == steps - 1)
    def _():
        out_copy = shard_copies(
            n,
            me,
            lambda owner: d_out.at[pl.ds(owner * per, per), :],
            lambda place: b_keep.at[place, rows_of(3)],
            lambda place: b_send.at[place, rows_of(3)],
            out_sems.at[3],
        )
        out_copy(True)
        qkv_out(step, False)
        out_copy(False)
        reduce.finish(reduced_ref)
        if spreads:
            for spread, copy in zip(spread_list, spread_copies):
                copy.wait()
                spread.end()


def attend_backward(n, reps, ga, gs, base, key_mask, q, k, v, ctx, lse, w_qkv, w_out, seqs, out_type, carry, collective_id):
    rows, width = ga.shape
    steps = width // GROUP
    seq = rows // seqs
    heads = GROUP // HEAD
    chips = n // 2
    half = jax.ShapeDtypeStruct((chips, 2 * width // n, width), bf16)
    hops = len(bits_below(n, 2))
    reduced = (2,) + carry[0].shape[1:]
    extra_out, extra_specs = [], []
    extra_scratch = reduce_scratch(chips, carry[0].shape[1], width, hops)
    if len(carry) > 4:
        for source, streams in zip(carry[4:], (2, 1)):
            extra_out.append(jax.ShapeDtypeStruct((streams, padded(source.shape[1], reps), width), bf16))
            extra_specs.append(ANY)
            extra_scratch += spread_scratch(source.shape[1], width, reps, streams)
        extra_scratch.append(pltpu.SemaphoreType.DMA((2,)))
    return pl.pallas_call(
        functools.partial(
            attend_backward_kernel, n, reps, seqs, (len(w_qkv), len(w_qkv) + len(w_out)), len(carry) > 4
        ),
        out_shape=(
            jax.ShapeDtypeStruct((rows, width), out_type),
            jax.ShapeDtypeStruct((8, width), f32),
            half,
            half,
            half,
            half,
            jax.ShapeDtypeStruct(reduced, f32),
            *extra_out,
        ),
        grid_spec=pltpu.PrefetchScalarGridSpec(
            num_scalar_prefetch=0,
            grid=(steps,),
            in_specs=[whole((rows, width))] * 3
            + [whole((rows, 1))]
            + [column_block(rows, GROUP)] * 4
            + [pl.BlockSpec((1, seqs * heads, seq), lambda j, *_: (j, 0, 0))]
            + [ANY] * (len(w_qkv) + len(w_out) + len(carry)),
            out_specs=[whole((rows, width)), column_block(8, GROUP)] + [ANY] * 4 + [whole(reduced)] + extra_specs,
            scratch_shapes=[
                pltpu.VMEM((width, 3 * width), bf16),
                pltpu.VMEM((width, width), bf16),
                pltpu.VMEM((rows, width), f32),
                pltpu.VMEM((width, rows), bf16),
                pltpu.VMEM((rows, GROUP), bf16),
                pltpu.VMEM((rows, 3 * GROUP), bf16),
                pltpu.VMEM((width, 3 * GROUP), bf16),
                pltpu.VMEM((width, width), bf16),
                pltpu.VMEM((seq, heads * seq), bf16),
                pltpu.VMEM((seq, heads * seq), bf16),
                pltpu.SemaphoreType.DMA((len(w_qkv) + len(w_out),)),
                pltpu.SemaphoreType.DMA((4, n)),
            ]
            + extra_scratch,
        ),
        compiler_params=remote_params(collective_id),
        cost_estimate=cost(16 * rows * width * width + 40 * rows * seq * width, 20 * rows * width),
        name="attend_backward",
    )(ga, gs, base, key_mask, q, k, v, ctx, lse, *w_qkv, *w_out, *carry)


def cost(flops, moved):
    return pl.CostEstimate(flops=int(flops), bytes_accessed=int(moved), transcendentals=0)


def last_sums_kernel(n, reps, a_keep, b_keep, a_send, b_send, spread_from, *refs):
    sums, refs = refs[: 3 * LAYERS], refs[3 * LAYERS :]
    spread_ref, attend_ref, total_ref, *scratch = refs
    bits, rep_bits = bits_below(n, 2), bits_below(reps)
    hops = len(bits)
    reduce = Reduce((a_keep, b_keep, a_send, b_send), scratch[: 5 + hops], bits)
    first = make_spread(reps, scratch[5 + hops : 11 + hops])
    second = make_spread(reps, scratch[11 + hops : 17 + hops])
    reduced, small_out, small_in, small_sems, sems = scratch[17 + hops :]
    axes = [("fsdp", bit) for bit in bits_below(n)] + [("rep", bit) for bit in rep_bits]

    def small_copy(at):
        axis, bit = axes[at]
        return pltpu.make_async_remote_copy(
            src_ref=small_out.at[at],
            dst_ref=small_in.at[at],
            send_sem=small_sems.at[0, at],
            recv_sem=small_sems.at[1, at],
            device_id={axis: flip(lax.axis_index(axis), bit)},
            device_id_type=pl.DeviceIdType.MESH,
        )

    def small_step(at):
        small_copy(at).wait_recv()
        if at + 1 < len(axes):
            small_out[at + 1] = small_out[at] + small_in[at]
            small_copy(at + 1).start()
        else:
            total_ref[...] = small_out[at] + small_in[at]

    greet_both(n, reps, bits_below(n), sorted({*rep_bits, *rep_masks(reps)}))
    first.begin(spread_from)
    width = small_out.shape[2]
    small_out[0] = jnp.zeros(small_out.shape[1:], f32)
    for layer in range(LAYERS):
        ffn_sums, proj_sums, up_sums = sums[3 * layer : 3 * layer + 3]
        small_out[0, 16 * layer : 16 * layer + 6] = ffn_sums[0:6]
        small_out[0, 16 * layer + 6 : 16 * layer + 8] = proj_sums[0:2]
        for at in range(up_sums.shape[1] // width):
            small_out[0, 16 * layer + 8 + at : 16 * layer + 9 + at] = up_sums[:, at * width : (at + 1) * width]
    small_copy(0).start()
    reduce.begin()
    first.loaded(spread_from)
    small_step(0)
    reduce.hop(0)
    small_step(1)
    first.tick(1)
    first.tick(2)
    for hop in range(1, hops):
        reduce.hop(hop)
    for at in range(2, len(bits) + 1):
        small_step(at)
    first.tick(3)
    reduce.finish(reduced)
    rows = reduced.shape[1]
    for stream in range(2):
        second.total[stream, pl.ds(0, rows)] = reduced[stream]
    second.tick(0)
    for tick in range(4, first.ticks):
        first.tick(tick)
        second.tick(tick - 3)
        if len(bits) + tick - 3 < len(axes):
            small_step(len(bits) + tick - 3)
    first_copy = pltpu.make_async_copy(first.whole, spread_ref, sems.at[0])
    first_copy.start()
    for tick in range(first.ticks - 3, second.ticks):
        second.tick(tick)
    for at in range(len(bits) + max(first.ticks - 3, 1), len(axes)):
        small_step(at)
    second_copy = pltpu.make_async_copy(second.whole, attend_ref, sems.at[1])
    second_copy.start()
    first.end()
    second.end()
    for at in range(len(axes)):
        small_copy(at).wait_send()
    first_copy.wait()
    second_copy.wait()


def last_sums(n, reps, halves, spread_rows, sums, collective_id):
    chips, rows, width = halves[0].shape
    hops = len(bits_below(n, 2))
    count = len(bits_below(n)) + len(bits_below(reps))
    vmem = pl.BlockSpec(memory_space=pltpu.VMEM)
    return pl.pallas_call(
        functools.partial(last_sums_kernel, n, reps),
        out_shape=(
            jax.ShapeDtypeStruct((2, padded(spread_rows.shape[1], reps), width), bf16),
            jax.ShapeDtypeStruct((2, padded(rows, reps), width), bf16),
            jax.ShapeDtypeStruct((16 * LAYERS, width), f32),
        ),
        in_specs=[ANY] * 5 + [vmem] * len(sums),
        out_specs=(ANY, ANY, vmem),
        scratch_shapes=reduce_scratch(chips, rows, width, hops)
        + spread_scratch(spread_rows.shape[1], width, reps)
        + spread_scratch(rows, width, reps)
        + [
            pltpu.VMEM((2, rows, width), f32),
            pltpu.VMEM((count, 16 * LAYERS, width), f32),
            pltpu.VMEM((count, 16 * LAYERS, width), f32),
            pltpu.SemaphoreType.DMA((2, count)),
            pltpu.SemaphoreType.DMA((2,)),
        ],
        compiler_params=pltpu.CompilerParams(
            vmem_limit_bytes=VMEM_BYTES, collective_id=collective_id, has_side_effects=True
        ),
        name="last_sums",
    )(*halves, spread_rows, *sums)


def on_device(n, reps, tokens, cotangent, lengths, live_batches, w_qkv, w_out, w_up, w_down, up_bias, biases, norm_gains):
    seqs, seq, width = tokens.shape
    rows = seqs * seq
    units = w_up.shape[2]
    per = width // n
    me = lax.axis_index("fsdp").astype(jnp.int32)

    places = jnp.arange(seq, dtype=jnp.int32)
    inside = places[None, :] < lengths[:, None]
    alive = jnp.arange(seqs, dtype=jnp.int32) < live_batches[0]
    key_mask = jnp.where(inside, 0.0, big_negative).astype(f32).reshape(rows, 1)
    valid = jnp.where(inside & alive[:, None], 1.0, 0.0).astype(f32).reshape(rows, 1)
    ones = jnp.ones((rows, 1), f32)

    chip_bits = bits_below(n, 2)
    orders = (tuple(chip_bits + [1]), tuple(chip_bits[::-1] + [1]))

    qkv, out, up, down = ([[] for _ in range(LAYERS)] for _ in range(4))
    attend_parts = parts_of(0, w_qkv, 2, orders) + parts_of(1, w_out, 2, orders)

    own_small = jnp.concatenate([up_bias.reshape(-1), biases.reshape(-1), norm_gains.reshape(-1)])
    small_count = own_small.shape[0]
    small_rows = -(-small_count // 2048) * 16
    own_small = jnp.pad(own_small, (0, small_rows * 128 - small_count)).reshape(1, small_rows, 128)
    small_parts = [(2, 0, 128, orders[0])]
    gathered = gather_weights(n, 0, (w_qkv, w_out, own_small), small_parts + attend_parts, 0)
    small_all = gathered[0].reshape(n, small_rows * 128)[:, :small_count]
    qkv[0], out[0] = gathered[1:3], gathered[3:5]
    cut_a = LAYERS * units // n
    cut_b = cut_a + LAYERS * 6 * per
    up_bias_all = small_all[:, :cut_a].reshape(n, LAYERS, units // n).transpose(1, 0, 2).reshape(LAYERS, 1, units)
    bias_all = small_all[:, cut_a:cut_b].reshape(n, LAYERS, 6, per).transpose(1, 2, 0, 3).reshape(LAYERS, 6, width)
    gain_all = small_all[:, cut_b:].reshape(n, LAYERS, 2, per).transpose(1, 2, 0, 3).reshape(LAYERS, 2, width)
    smalls = jnp.concatenate([bias_all, gain_all], axis=1)

    current = tokens.reshape(rows, width)
    base = current
    saved = []
    for layer in range(LAYERS):
        last = layer == LAYERS - 1
        begun = EARLY if layer else 0
        parts = parts_of(0, w_up, UP_PARTS, orders, begun) + parts_of(1, w_down, 2, orders)
        results = attend_forward(
            n, current, smalls[layer], key_mask, qkv[layer], out[layer], seqs,
            layer, (w_up, w_down), parts, 1 + 2 * layer,
        )
        q, k, v, ctx, lse, mid, low, n1, r1 = results[:9]
        up[layer] = [*up[layer], *results[9:-2]]
        down[layer] = results[-2:]
        parts = [] if last else attend_parts + parts_of(2, w_up, UP_PARTS, orders)[:EARLY]
        results = ffn_forward(
            n, mid, low, smalls[layer], up_bias_all[layer], valid, up[layer], down[layer], last,
            layer + 1, () if last else (w_qkv, w_out, w_up), parts, 2 + 2 * layer,
        )
        act, slope, n2, r2, current = results[:5]
        saved.append((base, q, k, v, ctx, lse, low, n1, r1, act, slope, n2, r2))
        if not last:
            base = results[5]
            qkv[layer + 1], out[layer + 1], up[layer + 1] = results[6:8], results[8:10], list(results[10:])
    outputs = current.reshape(seqs, seq, width)

    grad = cotangent.reshape(rows, width)
    grad_valid = valid
    sum_rows = [None] * LAYERS
    attend_halves, attend_reduced = None, None
    down_done, up_done, attend_done = [None] * LAYERS, [None] * LAYERS, [None] * LAYERS
    ffn_reduced = None
    for layer in range(LAYERS - 1, -1, -1):
        first = layer == LAYERS - 1
        base, q, k, v, ctx, lse, low, n1, r1, act, slope, n2, r2 = saved[layer]
        results = ffn_backward(
            n, reps, grad, grad_valid, n2, r2, low, n1, r1, smalls[layer], act, slope, up[layer], down[layer],
            () if first else (*attend_halves, ffn_reduced), 10 + layer,
        )
        gs1, ga1, sums, up_sum, down_keep, down_send, up_keep, up_send = results[:8]
        if not first:
            attend_reduced, down_done[layer + 1] = results[8:]
        ffn_halves = (
            down_keep,
            up_keep.reshape(n // 2, -1, width),
            down_send,
            up_send.reshape(n // 2, -1, width),
        )
        results = attend_backward(
            n, reps, ga1, gs1, base, key_mask, q, k, v, ctx, lse, qkv[layer], out[layer], seqs,
            f32 if layer else bf16, ffn_halves + (() if first else (attend_reduced, ffn_reduced)), 20 + layer,
        )
        grad, proj_sums = results[:2]
        attend_halves, ffn_reduced = results[2:6], results[6]
        if not first:
            attend_done[layer + 1], up_done[layer + 1] = results[7:]
        grad_valid = ones
        sum_rows[layer] = (sums, proj_sums, up_sum)
    grad_tokens = grad.reshape(seqs, seq, width)
    ffn_last, attend_done[0], small_total = last_sums(
        n, reps, attend_halves, ffn_reduced, [array for arrays in sum_rows for array in arrays], 30
    )
    down_done[0], up_done[0] = ffn_last[:1], ffn_last[1:]

    ffn_rows, attend_rows = units // n, 2 * per
    both_attend = jnp.stack([done[:, :attend_rows] for done in attend_done])
    grad_down = jnp.stack([done[0, :ffn_rows] for done in down_done]).astype(f32)
    grad_up = jnp.stack([done[0, :ffn_rows] for done in up_done])
    grad_up = grad_up.reshape(LAYERS, units // width, per, width).transpose(0, 2, 1, 3)
    grad_up = grad_up.reshape(LAYERS, per, units).astype(f32)
    parts = both_attend.reshape(LAYERS, 4, per, width)
    grad_qkv = parts[:, :3].transpose(0, 2, 1, 3).reshape(LAYERS, per, 3 * width).astype(f32)
    grad_out = parts[:, 3].astype(f32)

    small_total = small_total.reshape(LAYERS, 16, width)
    mine = lax.dynamic_slice_in_dim(small_total[:, :8], me * per, per, axis=2)
    grad_biases = jnp.stack([mine[:, at] for at in (6, 7, 5, 2, 4, 1)], axis=1)
    grad_gains = jnp.stack([mine[:, at] for at in (3, 0)], axis=1)
    up_rows = small_total[:, 8 : 8 + units // width].reshape(LAYERS, units)
    grad_up_bias = lax.dynamic_slice_in_dim(up_rows, me * (units // n), units // n, axis=1)
    return (outputs, grad_tokens, grad_qkv, grad_out, grad_up, grad_down, grad_up_bias, grad_biases, grad_gains)


def solution(mesh):
    both = ("rep", "fsdp")
    placed = (
        P(both, None, None),
        P(both, None, None),
        P(both),
        P(both),
        P(None, "fsdp", None),
        P(None, "fsdp", None),
        P(None, "fsdp", None),
        P(None, "fsdp", None),
        P(None, "fsdp"),
        P(None, None, "fsdp"),
        P(None, None, "fsdp"),
    )
    return jax.shard_map(
        functools.partial(on_device, mesh.shape["fsdp"], mesh.shape["rep"]),
        mesh=mesh,
        in_specs=placed,
        out_specs=(
            P(both, None, None),
            P(both, None, None),
            P(None, "fsdp", None),
            P(None, "fsdp", None),
            P(None, "fsdp", None),
            P(None, "fsdp", None),
            P(None, "fsdp"),
            P(None, None, "fsdp"),
            P(None, None, "fsdp"),
        ),
        check_vma=False,
    )
```

```python
import functools

import jax
import jax.numpy as jnp
from jax import lax
from jax.experimental import pallas as pl
from jax.experimental.pallas import tpu as pltpu
from jax.sharding import PartitionSpec as P

HEAD = 64
LAYERS = 2
GROUP = 256
ROWS = 256
VMEM_BYTES = 60 * 1024 * 1024
UP_PARTS = 4
EARLY = 2

epsilon = 1e-05
big_negative = -1000000000.0
root_half = 0.7071067811865476
inv_root_tau = 0.3989422804014327
f32 = jnp.float32
bf16 = jnp.bfloat16


def dot_nn(a, b):
    return lax.dot_general(a, b, (((1,), (0,)), ((), ())), preferred_element_type=f32)


def dot_nt(a, b):
    return lax.dot_general(a, b, (((1,), (1,)), ((), ())), preferred_element_type=f32)


def whole(shape):
    zeros = (0,) * len(shape)
    return pl.BlockSpec(shape, lambda *_: zeros, pipeline_mode=pl.Buffered(1))


def layer_of(array, layer):
    return pl.BlockSpec((None, *array.shape[1:]), lambda *_: (layer, 0, 0), pipeline_mode=pl.Buffered(1))


def column_block(rows, width):
    return pl.BlockSpec((rows, width), lambda j, *_: (0, j))


ANY = pl.BlockSpec(memory_space=pl.ANY)


def flip(index, mask):
    bit = 1
    while bit <= mask:
        if mask & bit:
            index = index + bit - 2 * bit * ((index // bit) % 2)
        bit *= 2
    return index


def exclusive_or(a, b, count):
    total, bit = 0, 1
    while bit < count:
        total = total + bit * ((a // bit + b // bit) % 2)
        bit *= 2
    return total


def greet(n, bits):
    me = lax.axis_index("fsdp")
    barrier = pltpu.get_barrier_semaphore()
    for bit in bits:
        pl.semaphore_signal(barrier, inc=1, device_id={"fsdp": flip(me, bit)}, device_id_type=pl.DeviceIdType.MESH)
    pl.semaphore_wait(barrier, len(bits))


class Gather:
    def __init__(self, own, full, order, send_sems, recv_sems, local_sem):
        self.own, self.full, self.order = own, full, order
        self.send_sems, self.recv_sems, self.local_sem = send_sems, recv_sems, local_sem
        self.me = lax.axis_index("fsdp")
        self.depth = own.shape[0]

    def rows(self, mask):
        return self.full.at[pl.ds(pl.multiple_of(flip(self.me, mask) * self.depth, 16), self.depth), :]

    def round_masks(self, round_at):
        earlier = self.order[:round_at]
        masks = [0]
        for bit in earlier:
            masks += [mask | bit for mask in masks]
        return [mask | self.order[round_at] for mask in masks]

    def copy(self, mask):
        bit = [bit for bit in self.order if bit & mask][-1]
        held = mask ^ bit
        return pltpu.make_async_remote_copy(
            src_ref=self.own if held == 0 else self.rows(held),
            dst_ref=self.rows(held),
            send_sem=self.send_sems.at[mask],
            recv_sem=self.recv_sems.at[mask],
            device_id={"fsdp": flip(self.me, bit)},
            device_id_type=pl.DeviceIdType.MESH,
        )

    def begin(self, round_at):
        if round_at == 0:
            pltpu.make_async_copy(self.own, self.rows(0), self.local_sem).start()
        self.copy(self.order[round_at]).start()

    def onward(self, round_at, which=slice(None)):
        masks = self.round_masks(round_at)[which]
        for mask in masks:
            self.copy(mask).wait_recv()
        for bit in self.order[round_at + 1 :]:
            for mask in masks:
                self.copy(mask | bit).start()

    def end(self):
        pltpu.make_async_copy(self.own, self.rows(0), self.local_sem).wait()
        for round_at in range(len(self.order)):
            for mask in self.round_masks(round_at):
                self.copy(mask).wait_send()


def begin_all(n, gathers):
    rounds = len(gathers[0].order)
    greet(n, gathers[0].order)
    for round_at in range(rounds):
        for gather in gathers:
            gather.begin(round_at)


def onward_all(gathers, round_at, which=slice(None)):
    for gather in gathers:
        gather.onward(round_at, which)


def onward_rest(gathers):
    onward_all(gathers, 1, slice(1, None))
    for round_at in range(2, len(gathers[0].order)):
        onward_all(gathers, round_at)


def end_all(gathers):
    for gather in gathers:
        gather.end()


def make_gathers(layer, parts, shards, wholes, sems):
    send_sems, recv_sems, local_sems = sems
    gathers = []
    for at, ((which, column, width, order), full) in enumerate(zip(parts, wholes)):
        own = shards[which].at[layer, :, pl.ds(column, width)]
        gathers.append(Gather(own, full, order, send_sems.at[at], recv_sems.at[at], local_sems.at[at]))
    return gathers


def parts_of(which, shard, count, orders, first=0):
    step = shard.shape[2] // count
    return [(which, at * step, step, orders[at % 2]) for at in range(first, count)]


def gather_sems(n, count):
    return [
        pltpu.SemaphoreType.DMA((count, n)),
        pltpu.SemaphoreType.DMA((count, n)),
        pltpu.SemaphoreType.DMA((count,)),
    ]


def wholes_of(n, shards, parts):
    return tuple(
        jax.ShapeDtypeStruct((shards[which].shape[1] * n, width), shards[which].dtype) for which, _, width, _ in parts
    )


def gather_kernel(n, layer, parts, shard_count, *refs):
    shards, wholes = refs[:shard_count], refs[shard_count : shard_count + len(parts)]
    gathers = make_gathers(layer, parts, shards, wholes, refs[shard_count + len(parts) :])
    begin_all(n, gathers)
    for round_at in range(len(gathers[0].order)):
        onward_all(gathers, round_at)
    end_all(gathers)


def gather_weights(n, layer, shards, parts, collective_id):
    return pl.pallas_call(
        functools.partial(gather_kernel, n, layer, parts, len(shards)),
        out_shape=wholes_of(n, shards, parts),
        in_specs=[ANY] * len(shards),
        out_specs=tuple([ANY] * len(parts)),
        scratch_shapes=gather_sems(n, len(parts)),
        compiler_params=pltpu.CompilerParams(collective_id=collective_id, has_side_effects=True),
        name="gather_weights",
    )(*shards)


def part_copies(sources, target, sems, first=0):
    copies, column = [], 0
    for at, source in enumerate(sources):
        width = source.shape[1]
        copies.append(pltpu.make_async_copy(source, target.at[:, pl.ds(column, width)], sems.at[first + at]))
        column += width
    return copies


def both_copies(sources, count, targets, sems):
    return part_copies(sources[:count], targets[0], sems), part_copies(sources[count:], targets[1], sems, count)


BLOCK = 96


def add_rows(rows, target, sources):
    def step(block, carry):
        at = pl.ds(pl.multiple_of(block * BLOCK, BLOCK), BLOCK)
        total = None
        for ref, lead in sources:
            value = ref[(*lead, at)].astype(f32)
            total = value if total is None else total + value
        ref, lead = target
        ref[(*lead, at)] = total.astype(ref.dtype)
        return carry

    lax.fori_loop(0, rows // BLOCK, step, 0)


class Reduce:
    def __init__(self, halves, scratch, bits):
        self.keep, self.send = halves[:2], halves[2:]
        self.held, self.arrived = scratch[:2]
        hops = len(bits)
        self.hop_in = scratch[2 : 2 + hops]
        self.sems, self.hop_send, self.hop_recv = scratch[2 + hops : 5 + hops]
        self.orders = (bits[::-1], bits)
        self.chips, self.rows = self.held.shape[1:3]
        self.me = lax.axis_index("fsdp")

    def load(self, stream):
        return pltpu.make_async_copy(self.keep[stream], self.held.at[stream], self.sems.at[0, stream])

    def core_copy(self, stream):
        return pltpu.make_async_remote_copy(
            src_ref=self.send[stream],
            dst_ref=self.arrived.at[stream],
            send_sem=self.sems.at[1, stream],
            recv_sem=self.sems.at[2, stream],
            device_id={"fsdp": flip(self.me, 1)},
            device_id_type=pl.DeviceIdType.MESH,
        )

    def begin(self):
        for stream in range(2):
            self.core_copy(stream).start()
            self.load(stream).start()

    def leaving(self, stream, hop):
        gone = [bit // 2 for bit in self.orders[stream][:hop]]
        half = self.orders[stream][hop] // 2
        return half, [p for p in range(self.chips) if p & half and not any(p & g for g in gone)]

    def terms(self, stream, place, hops):
        found = [(self.held, (stream, place)), (self.arrived, (stream, place))]
        for hop in range(hops):
            half, places = self.leaving(stream, hop)
            found.append((self.hop_in[hop], (stream, places.index(place | half))))
        return found

    def hop_copy(self, stream, hop, slot, place):
        return pltpu.make_async_remote_copy(
            src_ref=self.held.at[stream, place],
            dst_ref=self.hop_in[hop].at[stream, slot],
            send_sem=self.hop_send.at[stream, hop, slot],
            recv_sem=self.hop_recv.at[stream, hop, slot],
            device_id={"fsdp": flip(self.me, self.orders[stream][hop])},
            device_id_type=pl.DeviceIdType.MESH,
        )

    def wait_before(self, stream, hop):
        if hop == 0:
            self.load(stream).wait()
            self.core_copy(stream).wait_recv()
        else:
            _, places = self.leaving(stream, hop - 1)
            for slot, place in enumerate(places):
                self.hop_copy(stream, hop - 1, slot, place).wait_recv()

    def hop(self, at):
        for stream in range(2):
            self.wait_before(stream, at)
            _, places = self.leaving(stream, at)
            for place in places:
                add_rows(self.rows, (self.held, (stream, place)), self.terms(stream, place, at))
            for slot, place in enumerate(places):
                self.hop_copy(stream, at, slot, place).start()

    def finish(self, result):
        hops = len(self.hop_in)
        for stream in range(2):
            self.wait_before(stream, hops)
            add_rows(self.rows, (result, (stream,)), self.terms(stream, 0, hops))
        for stream in range(2):
            self.core_copy(stream).wait_send()
            for hop in range(hops):
                _, places = self.leaving(stream, hop)
                for slot, place in enumerate(places):
                    self.hop_copy(stream, hop, slot, place).wait_send()


def reduce_scratch(chips, rows, width, hops):
    return (
        [pltpu.VMEM((2, chips, rows, width), bf16)] * 2
        + [pltpu.VMEM((2, chips >> (hop + 1), rows, width), bf16) for hop in range(hops)]
        + [pltpu.SemaphoreType.DMA((3, 2))]
        + [pltpu.SemaphoreType.DMA((2, hops, chips // 2))] * 2
    )


class Spread:
    def __init__(self, count, scratch, first=0):
        self.first = first
        self.total, self.outgoing, self.incoming, self.whole, self.load_sems, self.sems = scratch
        self.bits = []
        bit = 1
        while bit < count:
            self.bits.append(bit)
            bit *= 2
        self.rank = lax.axis_index("rep")
        self.streams, self.rows = self.total.shape[:2]

    def load(self, stream, source):
        target = self.total.at[stream, pl.ds(0, source.shape[1])]
        return pltpu.make_async_copy(source.at[self.first + stream], target, self.load_sems.at[stream])

    def begin(self, source):
        for stream in range(self.streams):
            self.load(stream, source).start()

    def loaded(self, source):
        for stream in range(self.streams):
            self.load(stream, source).wait()
        self.tick(0)

    def side(self, bit):
        return (self.rank // bit) % 2

    def span(self, stage):
        start, size = 0, self.rows
        for bit in self.bits[:stage]:
            size //= 2
            start = start + self.side(bit) * size
        return start, size

    def down_copy(self, stream, stage):
        size = self.rows >> (stage + 1)
        at = pl.ds(self.rows - (self.rows >> stage), size)
        return pltpu.make_async_remote_copy(
            src_ref=self.outgoing.at[stream, at],
            dst_ref=self.incoming.at[stream, at],
            send_sem=self.sems.at[0, stream, stage],
            recv_sem=self.sems.at[1, stream, stage],
            device_id={"rep": flip(self.rank, self.bits[stage])},
            device_id_type=pl.DeviceIdType.MESH,
        )

    def up_copy(self, stream, stage):
        start, size = self.span(stage + 1)
        at = pl.ds(pl.multiple_of(start, 16), size)
        return pltpu.make_async_remote_copy(
            src_ref=self.whole.at[stream, at],
            dst_ref=self.whole.at[stream, at],
            send_sem=self.sems.at[2, stream, stage],
            recv_sem=self.sems.at[3, stream, stage],
            device_id={"rep": flip(self.rank, self.bits[stage])},
            device_id_type=pl.DeviceIdType.MESH,
        )

    def act(self, stream, tick):
        stages = len(self.bits)
        if 0 < tick <= stages:
            stage = tick - 1
            self.down_copy(stream, stage).wait_recv()
            start, size = self.span(tick)
            base = self.rows - (self.rows >> stage)
            at = pl.ds(pl.multiple_of(start, 16), size)
            self.total[stream, at] += self.incoming[stream, pl.ds(base, size)].astype(f32)
        if tick < stages:
            bit = self.bits[tick]
            start, size = self.span(tick)
            size //= 2
            base = self.rows - (self.rows >> tick)
            at = pl.ds(pl.multiple_of(start + (1 - self.side(bit)) * size, 16), size)
            self.outgoing[stream, pl.ds(base, size)] = self.total[stream, at].astype(bf16)
            self.down_copy(stream, tick).start()
        elif tick == stages:
            start, size = self.span(stages)
            at = pl.ds(pl.multiple_of(start, 16), size)
            self.whole[stream, at] = self.total[stream, at].astype(bf16)
            self.up_copy(stream, stages - 1).start()
        else:
            stage = 2 * stages - tick
            self.up_copy(stream, stage).wait_recv()
            if stage:
                self.up_copy(stream, stage - 1).start()

    @property
    def ticks(self):
        return 2 * len(self.bits) + self.streams

    def tick(self, tick):
        for stream in range(self.streams):
            if 0 <= tick - stream <= 2 * len(self.bits):
                self.act(stream, tick - stream)

    def end(self):
        for stream in range(self.streams):
            for stage in range(len(self.bits)):
                self.down_copy(stream, stage).wait_send()
                self.up_copy(stream, stage).wait_send()


CHAIN = 4
PIECES = 2


class Chain(Spread):
    def __init__(self, count, scratch, first=0, lag=1):
        super().__init__(count, scratch, first)
        self.lag = lag
        self.inner = (self.rank == 1) | (self.rank == 2)
        self.chunks = self.streams * PIECES

    def place(self, chunk):
        size = self.rows // PIECES
        return chunk // PIECES, pl.ds((chunk % PIECES) * size, size)

    def copy(self, leg, chunk):
        stream, at = self.place(chunk)
        source = self.whole if leg == 2 else self.outgoing
        target = self.whole.at[stream, at] if leg == 2 else self.incoming.at[leg * self.streams + stream, at]
        return pltpu.make_async_remote_copy(
            src_ref=source.at[stream, at],
            dst_ref=target,
            send_sem=self.sems.at[2 * leg, chunk],
            recv_sem=self.sems.at[2 * leg + 1, chunk],
            device_id={"rep": flip(self.rank, 3 if leg == 1 else 1)},
            device_id_type=pl.DeviceIdType.MESH,
        )

    def act(self, chunk, tick):
        stream, at = self.place(chunk)

        if tick == 0:

            @pl.when(jnp.logical_not(self.inner))
            def _():
                self.outgoing[stream, at] = self.total[stream, at].astype(bf16)
                self.copy(0, chunk).start()

        elif tick == 3:

            @pl.when(jnp.logical_not(self.inner))
            def _():
                self.copy(2, chunk).wait_recv()

        else:

            @pl.when(self.inner)
            def _():
                self.copy(tick - 1, chunk).wait_recv()
                arrived = self.incoming[(tick - 1) * self.streams + stream, at].astype(f32)
                if tick == 1:
                    self.outgoing[stream, at] = (self.total[stream, at] + arrived).astype(bf16)
                else:
                    self.whole[stream, at] = (self.outgoing[stream, at].astype(f32) + arrived).astype(bf16)
                self.copy(tick, chunk).start()

    @property
    def ticks(self):
        return (self.chunks - 1) * self.lag + 4

    def tick(self, tick):
        if tick == 0:
            for chunk in range(self.chunks):
                self.act(chunk, 0)
            return
        for chunk in range(self.chunks - 1, -1, -1) if self.lag else range(self.chunks):
            if 1 <= tick - chunk * self.lag <= 3:
                self.act(chunk, tick - chunk * self.lag)

    def end(self):
        for chunk in range(self.chunks):

            @pl.when(self.inner)
            def _():
                self.copy(1, chunk).wait_send()
                self.copy(2, chunk).wait_send()

            @pl.when(jnp.logical_not(self.inner))
            def _():
                self.copy(0, chunk).wait_send()


def make_spread(count, scratch, first=0, lag=1):
    return Chain(count, scratch, first, lag) if count == CHAIN else Spread(count, scratch, first)


def rep_masks(count):
    return [1, 3] if count == CHAIN else bits_below(count)


def padded(rows, count):
    return -(-rows // (16 * count)) * 16 * count


def spread_scratch(rows, width, count, streams=2):
    rows = padded(rows, count)
    stages = count.bit_length() - 1
    return [
        pltpu.VMEM((streams, rows, width), f32),
        pltpu.VMEM((streams, rows, width), bf16),
        pltpu.VMEM((2 * streams if count == CHAIN else streams, rows, width), bf16),
        pltpu.VMEM((streams, rows, width), bf16),
        pltpu.SemaphoreType.DMA((streams,)),
        pltpu.SemaphoreType.DMA((6, streams * PIECES) if count == CHAIN else (4, streams, stages)),
    ]


def greet_both(n, reps, fsdp_bits, rep_bits):
    me, rank = lax.axis_index("fsdp"), lax.axis_index("rep")
    barrier = pltpu.get_barrier_semaphore()
    for bit in fsdp_bits:
        pl.semaphore_signal(barrier, inc=1, device_id={"fsdp": flip(me, bit)}, device_id_type=pl.DeviceIdType.MESH)
    for bit in rep_bits:
        pl.semaphore_signal(barrier, inc=1, device_id={"rep": flip(rank, bit)}, device_id_type=pl.DeviceIdType.MESH)
    pl.semaphore_wait(barrier, len(fsdp_bits) + len(rep_bits))


def bits_below(count, first=1):
    bits = []
    while first < count:
        bits.append(first)
        first *= 2
    return bits


def norm_forward(total, gain, shift):
    middle = jnp.mean(total, axis=-1, keepdims=True)
    centred = total - middle
    spread = jnp.mean(centred * centred, axis=-1, keepdims=True)
    scaling = lax.rsqrt(spread + epsilon)
    normed = centred * scaling
    return normed * gain + shift, normed, scaling


def norm_backward(grad, normed, scaling, gain):
    scaled = grad * gain
    first = jnp.mean(scaled, axis=-1, keepdims=True)
    second = jnp.mean(scaled * normed, axis=-1, keepdims=True)
    return scaling * (scaled - first - normed * second)


def head_mask(shape, head):
    lanes = lax.broadcasted_iota(jnp.int32, shape, 1)
    return (lanes >= head * HEAD) & (lanes < (head + 1) * HEAD)


def attend_forward_kernel(n, seqs, layer, counts, parts, x_ref, small_ref, mask_ref, *refs):
    first, given, taken = counts
    sources, shards, refs = refs[:given], refs[given : given + taken], refs[given + taken :]
    count = len(parts)
    q_ref, k_ref, v_ref, ctx_ref, lse_ref, mid_ref, low_ref, n1_ref, r1_ref = refs[:9]
    wholes, refs = refs[9 : 9 + count], refs[9 + count :]
    base, w_qkv, w_out, acc, sems, mid_buffer, low_buffer, n1_buffer, out_sems = refs[:9]
    gathers = make_gathers(layer, parts, shards, wholes, refs[9:])
    out_copies = [
        pltpu.make_async_copy(source, target, out_sems.at[at])
        for at, (source, target) in enumerate(((mid_buffer, mid_ref), (low_buffer, low_ref), (n1_buffer, n1_ref)))
    ]
    step, steps = pl.program_id(0), pl.num_programs(0)
    rows, width = x_ref.shape
    seq = rows // seqs
    heads = GROUP // HEAD
    copies = sum(both_copies(sources, first, (w_qkv, w_out), sems), [])

    @pl.when(step == 0)
    def _():
        for copy in copies:
            copy.start()
        begin_all(n, gathers)

        def prepare(block, carry):
            at = pl.ds(pl.multiple_of(block * ROWS, ROWS), ROWS)
            base[at, :] = x_ref[at, :].astype(bf16)
            acc[at, :] = x_ref[at, :].astype(f32) + small_ref[2:3, :]
            return carry

        lax.fori_loop(0, rows // ROWS, prepare, 0)
        for copy in copies:
            copy.wait()

    columns = pl.multiple_of(step * GROUP, GROUP)
    q_bias = small_ref[0:1, pl.ds(columns, GROUP)]
    v_bias = small_ref[1:2, pl.ds(columns, GROUP)]

    def project(block, carry):
        at = pl.ds(pl.multiple_of(block * ROWS, ROWS), ROWS)
        low = base[at, :]
        q = dot_nn(low, w_qkv[:, pl.ds(columns, GROUP)])
        q_ref[at, :] = ((q + q_bias) * HEAD ** (-0.5)).astype(bf16)
        k = dot_nn(low, w_qkv[:, pl.ds(pl.multiple_of(width + columns, GROUP), GROUP)])
        k_ref[at, :] = k.astype(bf16)
        v = dot_nn(low, w_qkv[:, pl.ds(pl.multiple_of(2 * width + columns, GROUP), GROUP)])
        v_ref[at, :] = (v + v_bias).astype(bf16)
        return carry

    lax.fori_loop(0, rows // ROWS, project, 0)

    def attend(s, carry):
        at = pl.ds(pl.multiple_of(s * seq, seq), seq)
        q, k = q_ref[at, :], k_ref[at, :]
        v_turned = v_ref[at, :].T
        key_mask = mask_ref[at, :]
        parts = []
        for head in range(heads):
            q_head = jnp.where(head_mask(q.shape, head), q, jnp.zeros_like(q))
            scores = dot_nt(k, q_head) + key_mask
            peak = jnp.max(scores, axis=0, keepdims=True)
            raised = jnp.exp(scores - peak)
            total = jnp.sum(raised, axis=0, keepdims=True)
            mixed = dot_nn(v_turned[head * HEAD : (head + 1) * HEAD, :], raised.astype(bf16))
            parts.append((mixed / total).astype(bf16))
            lse_ref[0, pl.ds(s * heads + head, 1), :] = peak + jnp.log(total)
        ctx_ref[at, :] = jnp.concatenate(parts, axis=0).T
        return carry

    lax.fori_loop(0, seqs, attend, 0)

    @pl.when(step == 1)
    def _():
        onward_all(gathers, 0)

    @pl.when(step == steps - 1)
    def _():
        onward_all(gathers, 1, slice(1))

    def mix(block, carry):
        at = pl.ds(pl.multiple_of(block * ROWS, ROWS), ROWS)
        acc[at, :] += dot_nn(ctx_ref[at, :], w_out[pl.ds(columns, GROUP), :])
        return carry

    lax.fori_loop(0, rows // ROWS, mix, 0)

    @pl.when(step == steps - 1)
    def _():
        def finish(block, carry):
            at = pl.ds(pl.multiple_of(block * ROWS, ROWS), ROWS)
            mid, normed, scaling = norm_forward(acc[at, :], small_ref[6:7, :], small_ref[4:5, :])
            mid_buffer[at, :] = mid
            low_buffer[at, :] = mid.astype(bf16)
            n1_buffer[at, :] = normed.astype(bf16)
            r1_ref[at, :] = scaling
            return carry

        lax.fori_loop(0, rows // ROWS, finish, 0)
        for copy in out_copies:
            copy.start()
        onward_rest(gathers)
        end_all(gathers)
        for copy in out_copies:
            copy.wait()


def attend_forward(n, x, small, key_mask, w_qkv, w_out, seqs, layer, shards, parts, collective_id):
    rows, width = x.shape
    steps = width // GROUP
    seq = rows // seqs
    wide = jax.ShapeDtypeStruct((rows, width), bf16)
    heads = GROUP // HEAD
    return pl.pallas_call(
        functools.partial(
            attend_forward_kernel, n, seqs, layer, (len(w_qkv), len(w_qkv) + len(w_out), len(shards)), parts
        ),
        out_shape=(
            wide,
            wide,
            wide,
            wide,
            jax.ShapeDtypeStruct((steps, seqs * heads, seq), f32),
            jax.ShapeDtypeStruct((rows, width), f32),
            wide,
            wide,
            jax.ShapeDtypeStruct((rows, 1), f32),
        )
        + wholes_of(n, shards, parts),
        grid_spec=pltpu.PrefetchScalarGridSpec(
            num_scalar_prefetch=0,
            grid=(steps,),
            in_specs=[whole((rows, width)), layer_of(small, layer), whole((rows, 1))]
            + [ANY] * (len(w_qkv) + len(w_out) + len(shards)),
            out_specs=[column_block(rows, GROUP)] * 4
            + [
                pl.BlockSpec((1, seqs * heads, seq), lambda j, *_: (j, 0, 0)),
                ANY,
                ANY,
                ANY,
                whole((rows, 1)),
            ]
            + [ANY] * len(parts),
            scratch_shapes=[
                pltpu.VMEM((rows, width), bf16),
                pltpu.VMEM((width, 3 * width), bf16),
                pltpu.VMEM((width, width), bf16),
                pltpu.VMEM((rows, width), f32),
                pltpu.SemaphoreType.DMA((len(w_qkv) + len(w_out),)),
                pltpu.VMEM((rows, width), f32),
                pltpu.VMEM((rows, width), bf16),
                pltpu.VMEM((rows, width), bf16),
                pltpu.SemaphoreType.DMA((3,)),
            ]
            + gather_sems(n, len(parts)),
        ),
        compiler_params=pltpu.CompilerParams(
            dimension_semantics=("arbitrary",),
            vmem_limit_bytes=VMEM_BYTES,
            collective_id=collective_id,
            has_side_effects=True,
        ),
        cost_estimate=cost(8 * rows * width * width + 16 * rows * seq * width, 20 * rows * width),
        name="attend_forward",
    )(x, small, key_mask, *w_qkv, *w_out, *shards)


def ffn_forward_kernel(n, last, layer, counts, parts, mid_ref, low_ref, small_ref, up_bias_ref, valid_ref, *refs):
    first, given, taken = counts
    sources, shards, refs = refs[:given], refs[given : given + taken], refs[given + taken :]
    count = len(parts)
    act_ref, slope_ref, n2_ref, r2_ref, hid_ref = refs[:5]
    refs = refs[5:]
    if not last:
        hid_low_ref, refs = refs[0], refs[1:]
    wholes, refs = refs[:count], refs[count:]
    w_up, w_down, acc, sems, n2_buffer, hid_buffer, low_buffer, out_sems = refs[:8]
    gathers = make_gathers(layer, parts, shards, wholes, refs[8:]) if count else []
    out_pairs = [(n2_buffer, n2_ref), (hid_buffer, hid_ref)] + ([] if last else [(low_buffer, hid_low_ref)])
    out_copies = [
        pltpu.make_async_copy(source, target, out_sems.at[at]) for at, (source, target) in enumerate(out_pairs)
    ]
    step, steps = pl.program_id(0), pl.num_programs(0)
    rows, width = mid_ref.shape
    chunk = act_ref.shape[1]
    copies = sum(both_copies(sources, first, (w_up, w_down), sems), [])

    @pl.when(step == 0)
    def _():
        for copy in copies:
            copy.start()
        if gathers:
            begin_all(n, gathers)

        def prepare(block, carry):
            at = pl.ds(pl.multiple_of(block * ROWS, ROWS), ROWS)
            acc[at, :] = mid_ref[at, :] + small_ref[3:4, :]
            return carry

        lax.fori_loop(0, rows // ROWS, prepare, 0)
        for copy in copies:
            copy.wait()

    if gathers:

        @pl.when(step == 2)
        def _():
            onward_all(gathers, 0)

        @pl.when(step == 3)
        def _():
            onward_all(gathers, 1, slice(1))

    columns = pl.multiple_of(step * chunk, chunk)
    tile = 256

    def block_step(block, carry):
        at = pl.ds(pl.multiple_of(block * ROWS, ROWS), ROWS)
        low = low_ref[at, :]
        acts = []
        for part in range(chunk // tile):
            inside = slice(part * tile, (part + 1) * tile)
            at_units = pl.ds(pl.multiple_of(columns + part * tile, tile), tile)
            pre = dot_nn(low, w_up[:, at_units]) + up_bias_ref[:, inside]
            share = 0.5 * (1.0 + lax.erf(pre * root_half))
            act = (pre * share).astype(bf16)
            act_ref[at, inside] = act
            acts.append(act)
            density = inv_root_tau * jnp.exp(-0.5 * pre * pre)
            slope_ref[at, inside] = (share + pre * density).astype(bf16)
        acc[at, :] += dot_nn(jnp.concatenate(acts, axis=1), w_down[pl.ds(columns, chunk), :])
        return carry

    lax.fori_loop(0, rows // ROWS, block_step, 0)

    @pl.when(step == steps - 1)
    def _():
        def finish(block, carry):
            at = pl.ds(pl.multiple_of(block * ROWS, ROWS), ROWS)
            hidden, normed, scaling = norm_forward(acc[at, :], small_ref[7:8, :], small_ref[5:6, :])
            n2_buffer[at, :] = normed.astype(bf16)
            r2_ref[at, :] = scaling
            if last:
                hid_buffer[at, :] = (hidden * valid_ref[at, :]).astype(bf16)
            else:
                hid_buffer[at, :] = hidden
                low_buffer[at, :] = hidden.astype(bf16)
            return carry

        lax.fori_loop(0, rows // ROWS, finish, 0)
        for copy in out_copies:
            copy.start()

    if gathers:

        @pl.when(step == steps - 1)
        def _():
            onward_rest(gathers)
            end_all(gathers)

    @pl.when(step == steps - 1)
    def _():
        for copy in out_copies:
            copy.wait()


def ffn_forward(n, mid, low, small, up_bias, valid, w_up, w_down, last, layer, shards, parts, collective_id):
    rows, width = mid.shape
    units = up_bias.shape[2]
    chunk = width
    steps = units // chunk
    out_shape = [
        jax.ShapeDtypeStruct((rows, units), bf16),
        jax.ShapeDtypeStruct((rows, units), bf16),
        jax.ShapeDtypeStruct((rows, width), bf16),
        jax.ShapeDtypeStruct((rows, 1), f32),
        jax.ShapeDtypeStruct((rows, width), bf16 if last else f32),
    ]
    out_specs = [column_block(rows, chunk)] * 2 + [ANY, whole((rows, 1)), ANY]
    if not last:
        out_shape.append(jax.ShapeDtypeStruct((rows, width), bf16))
        out_specs.append(ANY)
    out_shape += wholes_of(n, shards, parts)
    out_specs += [ANY] * len(parts)
    if parts:
        params = pltpu.CompilerParams(
            dimension_semantics=("arbitrary",),
            vmem_limit_bytes=VMEM_BYTES,
            collective_id=collective_id,
            has_side_effects=True,
        )
    else:
        params = pltpu.CompilerParams(dimension_semantics=("arbitrary",), vmem_limit_bytes=VMEM_BYTES)
    return pl.pallas_call(
        functools.partial(
            ffn_forward_kernel, n, last, layer + 1, (len(w_up), len(w_up) + len(w_down), len(shards)), parts
        ),
        out_shape=tuple(out_shape),
        grid_spec=pltpu.PrefetchScalarGridSpec(
            num_scalar_prefetch=0,
            grid=(steps,),
            in_specs=[
                whole((rows, width)),
                whole((rows, width)),
                layer_of(small, layer),
                pl.BlockSpec((None, 1, chunk), lambda j, *_: (layer, 0, j)),
                whole((rows, 1)),
            ]
            + [ANY] * (len(w_up) + len(w_down) + len(shards)),
            out_specs=out_specs,
            scratch_shapes=[
                pltpu.VMEM((width, units), bf16),
                pltpu.VMEM((units, width), bf16),
                pltpu.VMEM((rows, width), f32),
                pltpu.SemaphoreType.DMA((len(w_up) + len(w_down),)),
                pltpu.VMEM((rows, width), bf16),
                pltpu.VMEM((rows, width), bf16 if last else f32),
                pltpu.VMEM((rows, width), bf16),
                pltpu.SemaphoreType.DMA((3,)),
            ]
            + (gather_sems(n, len(parts)) if parts else []),
        ),
        compiler_params=params,
        cost_estimate=cost(8 * rows * width * units, 8 * rows * units),
        name="ffn_forward",
    )(mid, low, small, up_bias, valid, *w_up, *w_down, *shards)


def shard_copies(n, me, source_of, keep_of, send_of, sems):
    def each(start):
        for owner in range(n):
            mask = flip(me, owner)
            place = mask // 2

            @pl.when(mask % 2 == 0)
            def _():
                copy = pltpu.make_async_copy(source_of(owner), keep_of(place), sems.at[owner])
                copy.start() if start else copy.wait()

            @pl.when(mask % 2 == 1)
            def _():
                copy = pltpu.make_async_copy(source_of(owner), send_of(place), sems.at[owner])
                copy.start() if start else copy.wait()

    return each


def ffn_backward_kernel(n, reps, counts, carry, g_ref, valid_ref, n2_ref, r2_ref, low_ref, n1_ref, r1_ref, small_ref, act_ref, slope_ref, *refs):
    sources, refs = refs[: counts[1]], refs[counts[1] :]
    if carry:
        halves, spread_from, refs = refs[:4], refs[4], refs[5:]
    gs1_ref, ga1_ref, sums_ref, up_sum_ref, down_keep, down_send, up_keep, up_send = refs[:8]
    refs = refs[8:]
    if carry:
        reduced_ref, spread_ref, refs = refs[0], refs[1], refs[2:]
    w_up, w_down, gffn, gpre, acc, low_turned, d_down, d_up, sems, out_sems = refs[:10]
    if carry:
        hops = len(bits_below(n, 2))
        reduce = Reduce(halves, refs[10 : 15 + hops], bits_below(n, 2))
        spread = make_spread(reps, refs[15 + hops : 21 + hops])
        spread_sem = refs[21 + hops]
    carry_in = carry
    step, steps = pl.program_id(0), pl.num_programs(0)
    me = lax.axis_index("fsdp")
    rows, width = acc.shape
    last_step = steps - 1
    if carry:
        out_copy = pltpu.make_async_copy(spread.whole, spread_ref, spread_sem)

        @pl.when(step == 0)
        def _():
            greet_both(n, reps, bits_below(n), rep_masks(reps))
            spread.begin(spread_from)
            reduce.begin()
            spread.loaded(spread_from)

        @pl.when(step == 1)
        def _():
            spread.tick(1)

        @pl.when(step == 2)
        def _():
            spread.tick(2)
            for hop in range(1, hops):
                reduce.hop(hop)

        @pl.when(step == 3)
        def _():
            reduce.finish(reduced_ref)
    chunk = act_ref.shape[1]
    per_down = down_keep.shape[1]
    per_up = up_keep.shape[2]
    tile = 256
    up_copies, down_copies = both_copies(sources, counts[0], (w_up, w_down), sems)

    @pl.when(step == 0)
    def _():
        for copy in down_copies:
            copy.start()
        for copy in up_copies:
            copy.start()
        sums_ref[...] = jnp.zeros_like(sums_ref)

        def prepare(block, carry):
            at = pl.ds(pl.multiple_of(block * ROWS, ROWS), ROWS)
            grad = g_ref[at, :].astype(f32)
            if not carry_in:
                grad = grad * valid_ref[at, :]
            normed = n2_ref[at, :].astype(f32)
            summed = norm_backward(grad, normed, r2_ref[at, :], small_ref[7:8, :])
            acc[at, :] = summed
            low = summed.astype(bf16)
            gffn[at, :] = low
            sums_ref[0:1, :] += jnp.sum(grad * normed, axis=0, keepdims=True)
            sums_ref[1:2, :] += jnp.sum(grad, axis=0, keepdims=True)
            sums_ref[2:3, :] += jnp.sum(low.astype(f32), axis=0, keepdims=True)
            low_turned[:, at] = low_ref[at, :].T
            return carry

        lax.fori_loop(0, rows // ROWS, prepare, 0)
        for copy in down_copies:
            copy.wait()
        for copy in up_copies:
            copy.wait()

    columns = pl.multiple_of(step * chunk, chunk)
    up_sum_ref[...] = jnp.zeros_like(up_sum_ref)

    def through(block, carry):
        at = pl.ds(pl.multiple_of(block * ROWS, ROWS), ROWS)
        grad = gffn[at, :]
        lows = []
        for part in range(chunk // tile):
            inside = slice(part * tile, (part + 1) * tile)
            at_units = pl.ds(pl.multiple_of(columns + part * tile, tile), tile)
            grad_act = dot_nt(grad, w_down[at_units, :])
            low = (grad_act * slope_ref[at, inside].astype(f32)).astype(bf16)
            gpre[at, inside] = low
            lows.append(low)
            up_sum_ref[:, inside] += jnp.sum(low.astype(f32), axis=0, keepdims=True)
        acc[at, :] += dot_nt(jnp.concatenate(lows, axis=1), w_up[:, pl.ds(columns, chunk)])
        return carry

    lax.fori_loop(0, rows // ROWS, through, 0)
    if carry:

        @pl.when(step == 0)
        def _():
            reduce.hop(0)

        @pl.when(step == 2)
        def _():
            spread.tick(3)

        @pl.when(step == 3)
        def _():
            for tick in range(4, spread.ticks):
                spread.tick(tick)
            out_copy.start()

    def down_out(which):
        def run(start):
            for local in range(chunk // per_down):
                owner = which * (chunk // per_down) + local
                mask = exclusive_or(me, owner, n)
                source = d_down.at[pl.ds(local * per_down, per_down), :]
                place = mask // 2

                @pl.when(mask % 2 == 0)
                def _():
                    copy = pltpu.make_async_copy(source, down_keep.at[place], out_sems.at[0, local])
                    copy.start() if start else copy.wait()

                @pl.when(mask % 2 == 1)
                def _():
                    copy = pltpu.make_async_copy(source, down_send.at[place], out_sems.at[0, local])
                    copy.start() if start else copy.wait()

        return run

    def up_out(which):
        return shard_copies(
            n,
            me,
            lambda owner: d_up.at[pl.ds(owner * per_up, per_up), :],
            lambda place: up_keep.at[place, which],
            lambda place: up_send.at[place, which],
            out_sems.at[1],
        )

    @pl.when(step > 0)
    def _():
        down_out(step - 1)(False)

    def down_part(part, carry):
        at = pl.ds(pl.multiple_of(part * tile, tile), tile)
        turned = act_ref[:, at].T
        d_down[at, :] = dot_nn(turned, gffn[...]).astype(bf16)
        return carry

    lax.fori_loop(0, chunk // tile, down_part, 0)
    down_out(step)(True)

    @pl.when(step > 0)
    def _():
        up_out(step - 1)(False)

    def up_part(part, carry):
        at = pl.ds(pl.multiple_of(part * tile, tile), tile)
        d_up[at, :] = dot_nn(low_turned[at, :], gpre[...]).astype(bf16)
        return carry

    lax.fori_loop(0, width // tile, up_part, 0)
    up_out(step)(True)

    @pl.when(step == steps - 1)
    def _():
        def finish(block, carry):
            at = pl.ds(pl.multiple_of(block * ROWS, ROWS), ROWS)
            grad = acc[at, :]
            normed = n1_ref[at, :].astype(f32)
            summed = norm_backward(grad, normed, r1_ref[at, :], small_ref[6:7, :])
            gs1_ref[at, :] = summed
            low = summed.astype(bf16)
            ga1_ref[at, :] = low
            sums_ref[3:4, :] += jnp.sum(grad * normed, axis=0, keepdims=True)
            sums_ref[4:5, :] += jnp.sum(grad, axis=0, keepdims=True)
            sums_ref[5:6, :] += jnp.sum(low.astype(f32), axis=0, keepdims=True)
            return carry

        lax.fori_loop(0, rows // ROWS, finish, 0)
        down_out(step)(False)
        up_out(step)(False)
        if carry:
            out_copy.wait()
            spread.end()


def remote_params(collective_id):
    return pltpu.CompilerParams(
        dimension_semantics=("arbitrary",),
        vmem_limit_bytes=VMEM_BYTES,
        collective_id=collective_id,
        has_side_effects=True,
    )


def ffn_backward(n, reps, grad, valid, n2, r2, low, n1, r1, small, act, slope, w_up, w_down, layer, carry, collective_id):
    rows, width = grad.shape
    units = act.shape[1]
    chunk = width
    steps = units // chunk
    chips = n // 2
    hops = len(bits_below(n, 2))
    extra_out, extra_specs, extra_scratch = [], [], []
    if carry:
        reduced = (2,) + carry[0].shape[1:]
        spread_rows = carry[4].shape[1]
        extra_out = [
            jax.ShapeDtypeStruct(reduced, f32),
            jax.ShapeDtypeStruct((1, padded(spread_rows, reps), width), bf16),
        ]
        extra_specs = [whole(reduced), ANY]
        extra_scratch = reduce_scratch(chips, carry[0].shape[1], width, hops)
        extra_scratch += spread_scratch(spread_rows, width, reps, 1) + [pltpu.SemaphoreType.DMA]
    down_half = jax.ShapeDtypeStruct((chips, units // n, width), bf16)
    up_half = jax.ShapeDtypeStruct((chips, steps, width // n, chunk), bf16)
    return pl.pallas_call(
        functools.partial(ffn_backward_kernel, n, reps, (len(w_up), len(w_up) + len(w_down)), bool(carry)),
        out_shape=(
            jax.ShapeDtypeStruct((rows, width), f32),
            jax.ShapeDtypeStruct((rows, width), bf16),
            jax.ShapeDtypeStruct((8, width), f32),
            jax.ShapeDtypeStruct((1, units), f32),
            down_half,
            down_half,
            up_half,
            up_half,
            *extra_out,
        ),
        grid_spec=pltpu.PrefetchScalarGridSpec(
            num_scalar_prefetch=0,
            grid=(steps,),
            in_specs=[
                whole((rows, width)),
                whole((rows, 1)),
                whole((rows, width)),
                whole((rows, 1)),
                whole((rows, width)),
                whole((rows, width)),
                whole((rows, 1)),
                layer_of(small, layer),
                column_block(rows, chunk),
                column_block(rows, chunk),
            ]
            + [ANY] * (len(w_up) + len(w_down) + len(carry)),
            out_specs=[
                whole((rows, width)),
                whole((rows, width)),
                whole((8, width)),
                column_block(1, chunk),
            ]
            + [ANY] * 4
            + extra_specs,
            scratch_shapes=[
                pltpu.VMEM((width, units), bf16),
                pltpu.VMEM((units, width), bf16),
                pltpu.VMEM((rows, width), bf16),
                pltpu.VMEM((rows, chunk), bf16),
                pltpu.VMEM((rows, width), f32),
                pltpu.VMEM((width, rows), bf16),
                pltpu.VMEM((chunk, width), bf16),
                pltpu.VMEM((width, chunk), bf16),
                pltpu.SemaphoreType.DMA((len(w_up) + len(w_down),)),
                pltpu.SemaphoreType.DMA((2, n)),
            ]
            + extra_scratch,
        ),
        compiler_params=remote_params(collective_id)
        if carry
        else pltpu.CompilerParams(dimension_semantics=("arbitrary",), vmem_limit_bytes=VMEM_BYTES),
        cost_estimate=cost(10 * rows * width * units, 8 * rows * units),
        name="ffn_backward",
    )(grad, valid, n2, r2, low, n1, r1, small, act, slope, *w_up, *w_down, *carry)


def attend_backward_kernel(n, reps, seqs, counts, spreads, ga_ref, gs_ref, base_ref, mask_ref, q_ref, k_ref, v_ref, ctx_ref, lse_ref, *refs):
    sources, refs = refs[: counts[1]], refs[counts[1] :]
    halves, refs = refs[:4], refs[4:]
    if spreads:
        spread_from, refs = refs[:2], refs[2:]
    gh_ref, sums_ref, a_keep, b_keep, a_send, b_send, reduced_ref = refs[:7]
    refs = refs[7:]
    if spreads:
        spread_refs, refs = refs[:2], refs[2:]
    w_qkv, w_out, acc, base_turned, gctx, gproj, d_qkv, d_out, p_all, ds_all, ctx_turned, sems, out_sems = refs[:13]
    hops = len(bits_below(n, 2))
    reduce = Reduce(halves, refs[13 : 18 + hops], bits_below(n, 2))
    step, steps = pl.program_id(0), pl.num_programs(0)
    me = lax.axis_index("fsdp")
    if spreads:
        rest = refs[18 + hops :]
        spread_list = [make_spread(reps, rest[:6], 0, 0), make_spread(reps, rest[6:12], 1, 0)]
        spread_copies = [
            pltpu.make_async_copy(spread.whole, ref, rest[12].at[at])
            for at, (spread, ref) in enumerate(zip(spread_list, spread_refs))
        ]

    @pl.when(step == 0)
    def _():
        greet_both(n, reps, bits_below(n), rep_masks(reps) if spreads else [])
        if spreads:
            for spread, source in zip(spread_list, spread_from):
                spread.begin(source)
        reduce.begin()
        if spreads:
            for spread, source in zip(spread_list[::-1], spread_from[::-1]):
                spread.loaded(source)

    if spreads:

        for at in (1, 2):

            @pl.when(step == at)
            def _():
                spread_list[1].tick(at)

    rows, width = ga_ref.shape
    seq = rows // seqs
    heads = GROUP // HEAD
    per = width // n
    tile = 256
    qkv_copies, out_copies = both_copies(sources, counts[0], (w_qkv, w_out), sems)

    @pl.when(step == 0)
    def _():
        for copy in out_copies:
            copy.start()
        for copy in qkv_copies:
            copy.start()

        def turn(block, carry):
            at = pl.ds(pl.multiple_of(block * ROWS, ROWS), ROWS)
            acc[at, :] = gs_ref[at, :]
            base_turned[:, at] = base_ref[at, :].T
            return carry

        lax.fori_loop(0, rows // ROWS, turn, 0)
        for copy in out_copies:
            copy.wait()
        for copy in qkv_copies:
            copy.wait()

    columns = pl.multiple_of(step * GROUP, GROUP)

    def through(block, carry):
        at = pl.ds(pl.multiple_of(block * ROWS, ROWS), ROWS)
        gctx[at, :] = dot_nt(ga_ref[at, :], w_out[pl.ds(columns, GROUP), :]).astype(bf16)
        return carry

    lax.fori_loop(0, rows // ROWS, through, 0)
    ctx_turned[...] = ctx_ref[...].T

    def out_part(part, carry):
        at = pl.ds(pl.multiple_of(part * tile, tile), tile)
        d_out[pl.ds(columns, GROUP), at] = dot_nn(ctx_turned[...], ga_ref[:, at]).astype(bf16)
        return carry

    lax.fori_loop(0, width // tile, out_part, 0)

    @pl.when(step == 2)
    def _():
        for hop in range(1, hops):
            reduce.hop(hop)

    def attend(s, carry):
        @pl.when((step == 0) & (s == seqs - 1))
        def _():
            reduce.hop(0)

        at = pl.ds(pl.multiple_of(s * seq, seq), seq)
        q, k, v, grad = q_ref[at, :], k_ref[at, :], v_ref[at, :], gctx[at, :]
        k_turned = k.T
        key_mask = mask_ref[at, :]
        parts, q_heads, g_heads = [], [], []
        for head in range(heads):
            inside = head_mask(q.shape, head)
            q_head = jnp.where(inside, q, jnp.zeros_like(q))
            g_head = jnp.where(inside, grad, jnp.zeros_like(grad))
            scores = dot_nt(k, q_head) + key_mask
            attention = jnp.exp(scores - lse_ref[0, pl.ds(s * heads + head, 1), :])
            weighted = attention * dot_nt(v, g_head)
            inner = jnp.sum(weighted, axis=0, keepdims=True)
            grad_scores = (weighted - attention * inner).astype(bf16)
            here = slice(head * seq, (head + 1) * seq)
            p_all[:, here] = attention.astype(bf16)
            ds_all[:, here] = grad_scores
            turned = dot_nn(k_turned[head * HEAD : (head + 1) * HEAD, :], grad_scores)
            parts.append(turned.astype(bf16) * HEAD ** (-0.5))
            q_heads.append(q_head)
            g_heads.append(g_head)
        gproj[at, 0:GROUP] = jnp.concatenate(parts, axis=0).T
        gproj[at, GROUP : 2 * GROUP] = dot_nn(ds_all[...], jnp.concatenate(q_heads, axis=0)).astype(bf16)
        gproj[at, 2 * GROUP : 3 * GROUP] = dot_nn(p_all[...], jnp.concatenate(g_heads, axis=0)).astype(bf16)
        return carry

    lax.fori_loop(0, seqs, attend, 0)
    sums_ref[...] = jnp.zeros_like(sums_ref)

    if spreads:

        for at in (1, 2):

            @pl.when(step == at)
            def _():
                spread_list[0].tick(at)


    def onward(block, carry):
        at = pl.ds(pl.multiple_of(block * ROWS, ROWS), ROWS)
        term = dot_nt(gproj[at, 0:GROUP], w_qkv[:, pl.ds(columns, GROUP)])
        term += dot_nt(gproj[at, GROUP : 2 * GROUP], w_qkv[:, pl.ds(pl.multiple_of(width + columns, GROUP), GROUP)])
        term += dot_nt(gproj[at, 2 * GROUP : 3 * GROUP], w_qkv[:, pl.ds(pl.multiple_of(2 * width + columns, GROUP), GROUP)])
        sums_ref[0:1, :] += jnp.sum(gproj[at, 0:GROUP].astype(f32), axis=0, keepdims=True)
        sums_ref[1:2, :] += jnp.sum(gproj[at, 2 * GROUP : 3 * GROUP].astype(f32), axis=0, keepdims=True)
        acc[at, :] += term
        return carry

    lax.fori_loop(0, rows // ROWS, onward, 0)

    @pl.when(step == steps - 1)
    def _():
        def finish(block, carry):
            at = pl.ds(pl.multiple_of(block * ROWS, ROWS), ROWS)
            gh_ref[at, :] = acc[at, :].astype(gh_ref.dtype)
            return carry

        lax.fori_loop(0, rows // ROWS, finish, 0)

    def place_of(part, a_half, b_half):
        return a_half if part < 2 else b_half

    def rows_of(part):
        return pl.ds((part % 2) * per, per)

    def qkv_out(which, start):
        for part in range(3):
            at = pl.ds(pl.multiple_of(which * GROUP, GROUP), GROUP)
            shard_copies(
                n,
                me,
                lambda owner: d_qkv.at[pl.ds(owner * per, per), pl.ds(part * GROUP, GROUP)],
                lambda place: place_of(part, a_keep, b_keep).at[place, rows_of(part), at],
                lambda place: place_of(part, a_send, b_send).at[place, rows_of(part), at],
                out_sems.at[part],
            )(start)

    @pl.when(step > 0)
    def _():
        qkv_out(step - 1, False)

    def weight_part(part, carry):
        at = pl.ds(pl.multiple_of(part * tile, tile), tile)
        d_qkv[at, :] = dot_nn(base_turned[at, :], gproj[...]).astype(bf16)
        return carry

    lax.fori_loop(0, width // tile, weight_part, 0)
    qkv_out(step, True)

    @pl.when(step == steps - 1)
    def _():
        out_copy = shard_copies(
            n,
            me,
            lambda owner: d_out.at[pl.ds(owner * per, per), :],
            lambda place: b_keep.at[place, rows_of(3)],
            lambda place: b_send.at[place, rows_of(3)],
            out_sems.at[3],
        )
        out_copy(True)
        qkv_out(step, False)
        out_copy(False)
        reduce.finish(reduced_ref)
        if spreads:
            for spread, copy in zip(spread_list[::-1], spread_copies[::-1]):
                for tick in range(3, spread.ticks):
                    spread.tick(tick)
                copy.start()
            for spread, copy in zip(spread_list, spread_copies):
                copy.wait()
                spread.end()


def attend_backward(n, reps, ga, gs, base, key_mask, q, k, v, ctx, lse, w_qkv, w_out, seqs, out_type, carry, collective_id):
    rows, width = ga.shape
    steps = width // GROUP
    seq = rows // seqs
    heads = GROUP // HEAD
    chips = n // 2
    half = jax.ShapeDtypeStruct((chips, 2 * width // n, width), bf16)
    hops = len(bits_below(n, 2))
    reduced = (2,) + carry[0].shape[1:]
    extra_out, extra_specs = [], []
    extra_scratch = reduce_scratch(chips, carry[0].shape[1], width, hops)
    if len(carry) > 4:
        for source, streams in zip(carry[4:], (2, 1)):
            extra_out.append(jax.ShapeDtypeStruct((streams, padded(source.shape[1], reps), width), bf16))
            extra_specs.append(ANY)
            extra_scratch += spread_scratch(source.shape[1], width, reps, streams)
        extra_scratch.append(pltpu.SemaphoreType.DMA((2,)))
    return pl.pallas_call(
        functools.partial(
            attend_backward_kernel, n, reps, seqs, (len(w_qkv), len(w_qkv) + len(w_out)), len(carry) > 4
        ),
        out_shape=(
            jax.ShapeDtypeStruct((rows, width), out_type),
            jax.ShapeDtypeStruct((8, width), f32),
            half,
            half,
            half,
            half,
            jax.ShapeDtypeStruct(reduced, f32),
            *extra_out,
        ),
        grid_spec=pltpu.PrefetchScalarGridSpec(
            num_scalar_prefetch=0,
            grid=(steps,),
            in_specs=[whole((rows, width))] * 3
            + [whole((rows, 1))]
            + [column_block(rows, GROUP)] * 4
            + [pl.BlockSpec((1, seqs * heads, seq), lambda j, *_: (j, 0, 0))]
            + [ANY] * (len(w_qkv) + len(w_out) + len(carry)),
            out_specs=[whole((rows, width)), column_block(8, GROUP)] + [ANY] * 4 + [whole(reduced)] + extra_specs,
            scratch_shapes=[
                pltpu.VMEM((width, 3 * width), bf16),
                pltpu.VMEM((width, width), bf16),
                pltpu.VMEM((rows, width), f32),
                pltpu.VMEM((width, rows), bf16),
                pltpu.VMEM((rows, GROUP), bf16),
                pltpu.VMEM((rows, 3 * GROUP), bf16),
                pltpu.VMEM((width, 3 * GROUP), bf16),
                pltpu.VMEM((width, width), bf16),
                pltpu.VMEM((seq, heads * seq), bf16),
                pltpu.VMEM((seq, heads * seq), bf16),
                pltpu.VMEM((GROUP, rows), bf16),
                pltpu.SemaphoreType.DMA((len(w_qkv) + len(w_out),)),
                pltpu.SemaphoreType.DMA((4, n)),
            ]
            + extra_scratch,
        ),
        compiler_params=remote_params(collective_id),
        cost_estimate=cost(16 * rows * width * width + 40 * rows * seq * width, 20 * rows * width),
        name="attend_backward",
    )(ga, gs, base, key_mask, q, k, v, ctx, lse, *w_qkv, *w_out, *carry)


def cost(flops, moved):
    return pl.CostEstimate(flops=int(flops), bytes_accessed=int(moved), transcendentals=0)


def last_sums_kernel(n, reps, a_keep, b_keep, a_send, b_send, spread_from, *refs):
    sums, refs = refs[: 3 * LAYERS], refs[3 * LAYERS :]
    spread_ref, attend_ref, total_ref, *scratch = refs
    bits, rep_bits = bits_below(n, 2), bits_below(reps)
    hops = len(bits)
    reduce = Reduce((a_keep, b_keep, a_send, b_send), scratch[: 5 + hops], bits)
    first = make_spread(reps, scratch[5 + hops : 11 + hops])
    second = make_spread(reps, scratch[11 + hops : 17 + hops])
    reduced, small_out, small_in, small_sems, sems = scratch[17 + hops :]
    axes = [("fsdp", bit) for bit in bits_below(n)] + [("rep", bit) for bit in rep_bits]

    def small_copy(at):
        axis, bit = axes[at]
        return pltpu.make_async_remote_copy(
            src_ref=small_out.at[at],
            dst_ref=small_in.at[at],
            send_sem=small_sems.at[0, at],
            recv_sem=small_sems.at[1, at],
            device_id={axis: flip(lax.axis_index(axis), bit)},
            device_id_type=pl.DeviceIdType.MESH,
        )

    def small_step(at):
        small_copy(at).wait_recv()
        if at + 1 < len(axes):
            small_out[at + 1] = small_out[at] + small_in[at]
            small_copy(at + 1).start()
        else:
            total_ref[...] = small_out[at] + small_in[at]

    greet_both(n, reps, bits_below(n), sorted({*rep_bits, *rep_masks(reps)}))
    first.begin(spread_from)
    width = small_out.shape[2]
    small_out[0] = jnp.zeros(small_out.shape[1:], f32)
    for layer in range(LAYERS):
        ffn_sums, proj_sums, up_sums = sums[3 * layer : 3 * layer + 3]
        small_out[0, 16 * layer : 16 * layer + 6] = ffn_sums[0:6]
        small_out[0, 16 * layer + 6 : 16 * layer + 8] = proj_sums[0:2]
        for at in range(up_sums.shape[1] // width):
            small_out[0, 16 * layer + 8 + at : 16 * layer + 9 + at] = up_sums[:, at * width : (at + 1) * width]
    small_copy(0).start()
    reduce.begin()
    first.loaded(spread_from)
    small_step(0)
    reduce.hop(0)
    small_step(1)
    first.tick(1)
    first.tick(2)
    for hop in range(1, hops):
        reduce.hop(hop)
    for at in range(2, len(bits) + 1):
        small_step(at)
    first.tick(3)
    reduce.finish(reduced)
    rows = reduced.shape[1]
    for stream in range(2):
        second.total[stream, pl.ds(0, rows)] = reduced[stream]
    second.tick(0)
    for tick in range(4, first.ticks):
        first.tick(tick)
        second.tick(tick - 3)
        if len(bits) + tick - 3 < len(axes):
            small_step(len(bits) + tick - 3)
    first_copy = pltpu.make_async_copy(first.whole, spread_ref, sems.at[0])
    first_copy.start()
    for tick in range(first.ticks - 3, second.ticks):
        second.tick(tick)
    for at in range(len(bits) + max(first.ticks - 3, 1), len(axes)):
        small_step(at)
    second_copy = pltpu.make_async_copy(second.whole, attend_ref, sems.at[1])
    second_copy.start()
    first.end()
    second.end()
    for at in range(len(axes)):
        small_copy(at).wait_send()
    first_copy.wait()
    second_copy.wait()


def last_sums(n, reps, halves, spread_rows, sums, collective_id):
    chips, rows, width = halves[0].shape
    hops = len(bits_below(n, 2))
    count = len(bits_below(n)) + len(bits_below(reps))
    vmem = pl.BlockSpec(memory_space=pltpu.VMEM)
    return pl.pallas_call(
        functools.partial(last_sums_kernel, n, reps),
        out_shape=(
            jax.ShapeDtypeStruct((2, padded(spread_rows.shape[1], reps), width), bf16),
            jax.ShapeDtypeStruct((2, padded(rows, reps), width), bf16),
            jax.ShapeDtypeStruct((16 * LAYERS, width), f32),
        ),
        in_specs=[ANY] * 5 + [vmem] * len(sums),
        out_specs=(ANY, ANY, vmem),
        scratch_shapes=reduce_scratch(chips, rows, width, hops)
        + spread_scratch(spread_rows.shape[1], width, reps)
        + spread_scratch(rows, width, reps)
        + [
            pltpu.VMEM((2, rows, width), f32),
            pltpu.VMEM((count, 16 * LAYERS, width), f32),
            pltpu.VMEM((count, 16 * LAYERS, width), f32),
            pltpu.SemaphoreType.DMA((2, count)),
            pltpu.SemaphoreType.DMA((2,)),
        ],
        compiler_params=pltpu.CompilerParams(
            vmem_limit_bytes=VMEM_BYTES, collective_id=collective_id, has_side_effects=True
        ),
        name="last_sums",
    )(*halves, spread_rows, *sums)


def on_device(n, reps, tokens, cotangent, lengths, live_batches, w_qkv, w_out, w_up, w_down, up_bias, biases, norm_gains):
    seqs, seq, width = tokens.shape
    rows = seqs * seq
    units = w_up.shape[2]
    per = width // n
    me = lax.axis_index("fsdp").astype(jnp.int32)

    places = jnp.arange(seq, dtype=jnp.int32)
    inside = places[None, :] < lengths[:, None]
    alive = jnp.arange(seqs, dtype=jnp.int32) < live_batches[0]
    key_mask = jnp.where(inside, 0.0, big_negative).astype(f32).reshape(rows, 1)
    valid = jnp.where(inside & alive[:, None], 1.0, 0.0).astype(f32).reshape(rows, 1)

    chip_bits = bits_below(n, 2)
    orders = (tuple(chip_bits + [1]), tuple(chip_bits[::-1] + [1]))

    qkv, out, up, down = ([[] for _ in range(LAYERS)] for _ in range(4))
    attend_parts = parts_of(0, w_qkv, 2, orders) + parts_of(1, w_out, 2, orders)

    own_small = jnp.concatenate([up_bias.reshape(-1), biases.reshape(-1), norm_gains.reshape(-1)])
    small_count = own_small.shape[0]
    small_rows = -(-small_count // 2048) * 16
    own_small = jnp.pad(own_small, (0, small_rows * 128 - small_count)).reshape(1, small_rows, 128)
    small_parts = [(2, 0, 128, orders[0])]
    gathered = gather_weights(n, 0, (w_qkv, w_out, own_small), small_parts + attend_parts, 0)
    small_all = gathered[0].reshape(n, small_rows * 128)[:, :small_count]
    qkv[0], out[0] = gathered[1:3], gathered[3:5]
    cut_a = LAYERS * units // n
    cut_b = cut_a + LAYERS * 6 * per
    up_bias_all = small_all[:, :cut_a].reshape(n, LAYERS, units // n).transpose(1, 0, 2).reshape(LAYERS, 1, units)
    bias_all = small_all[:, cut_a:cut_b].reshape(n, LAYERS, 6, per).transpose(1, 2, 0, 3).reshape(LAYERS, 6, width)
    gain_all = small_all[:, cut_b:].reshape(n, LAYERS, 2, per).transpose(1, 2, 0, 3).reshape(LAYERS, 2, width)
    smalls = jnp.concatenate([bias_all, gain_all], axis=1)

    current = tokens.reshape(rows, width)
    base = current
    saved = []
    for layer in range(LAYERS):
        last = layer == LAYERS - 1
        begun = EARLY if layer else 0
        parts = parts_of(0, w_up, UP_PARTS, orders, begun) + parts_of(1, w_down, 2, orders)
        results = attend_forward(
            n, current, smalls, key_mask, qkv[layer], out[layer], seqs,
            layer, (w_up, w_down), parts, 1 + 2 * layer,
        )
        q, k, v, ctx, lse, mid, low, n1, r1 = results[:9]
        up[layer] = [*up[layer], *results[9:-2]]
        down[layer] = results[-2:]
        parts = [] if last else attend_parts + parts_of(2, w_up, UP_PARTS, orders)[:EARLY]
        results = ffn_forward(
            n, mid, low, smalls, up_bias_all, valid, up[layer], down[layer], last,
            layer, () if last else (w_qkv, w_out, w_up), parts, 2 + 2 * layer,
        )
        act, slope, n2, r2, current = results[:5]
        saved.append((base, q, k, v, ctx, lse, low, n1, r1, act, slope, n2, r2))
        if not last:
            base = results[5]
            qkv[layer + 1], out[layer + 1], up[layer + 1] = results[6:8], results[8:10], list(results[10:])
    outputs = current.reshape(seqs, seq, width)

    grad = cotangent.reshape(rows, width)
    sum_rows = [None] * LAYERS
    attend_halves, attend_reduced = None, None
    down_done, up_done, attend_done = [None] * LAYERS, [None] * LAYERS, [None] * LAYERS
    ffn_reduced = None
    for layer in range(LAYERS - 1, -1, -1):
        first = layer == LAYERS - 1
        base, q, k, v, ctx, lse, low, n1, r1, act, slope, n2, r2 = saved[layer]
        results = ffn_backward(
            n, reps, grad, valid, n2, r2, low, n1, r1, smalls, act, slope, up[layer], down[layer], layer,
            () if first else (*attend_halves, ffn_reduced), 10 + layer,
        )
        gs1, ga1, sums, up_sum, down_keep, down_send, up_keep, up_send = results[:8]
        if not first:
            attend_reduced, down_done[layer + 1] = results[8:]
        ffn_halves = (
            down_keep,
            up_keep.reshape(n // 2, -1, width),
            down_send,
            up_send.reshape(n // 2, -1, width),
        )
        results = attend_backward(
            n, reps, ga1, gs1, base, key_mask, q, k, v, ctx, lse, qkv[layer], out[layer], seqs,
            f32 if layer else bf16, ffn_halves + (() if first else (attend_reduced, ffn_reduced)), 20 + layer,
        )
        grad, proj_sums = results[:2]
        attend_halves, ffn_reduced = results[2:6], results[6]
        if not first:
            attend_done[layer + 1], up_done[layer + 1] = results[7:]
        sum_rows[layer] = (sums, proj_sums, up_sum)
    grad_tokens = grad.reshape(seqs, seq, width)
    ffn_last, attend_done[0], small_total = last_sums(
        n, reps, attend_halves, ffn_reduced, [array for arrays in sum_rows for array in arrays], 30
    )
    down_done[0], up_done[0] = ffn_last[:1], ffn_last[1:]

    ffn_rows, attend_rows = units // n, 2 * per
    both_attend = jnp.stack([done[:, :attend_rows] for done in attend_done])
    grad_down = jnp.stack([done[0, :ffn_rows] for done in down_done]).astype(f32)
    grad_up = jnp.stack([done[0, :ffn_rows] for done in up_done])
    grad_up = grad_up.reshape(LAYERS, units // width, per, width).transpose(0, 2, 1, 3)
    grad_up = grad_up.reshape(LAYERS, per, units).astype(f32)
    parts = both_attend.reshape(LAYERS, 4, per, width)
    grad_qkv = parts[:, :3].transpose(0, 2, 1, 3).reshape(LAYERS, per, 3 * width).astype(f32)
    grad_out = parts[:, 3].astype(f32)

    small_total = small_total.reshape(LAYERS, 16, width)
    mine = lax.dynamic_slice_in_dim(small_total[:, :8], me * per, per, axis=2)
    grad_biases = jnp.stack([mine[:, at] for at in (6, 7, 5, 2, 4, 1)], axis=1)
    grad_gains = jnp.stack([mine[:, at] for at in (3, 0)], axis=1)
    up_rows = small_total[:, 8 : 8 + units // width].reshape(LAYERS, units)
    grad_up_bias = lax.dynamic_slice_in_dim(up_rows, me * (units // n), units // n, axis=1)
    return (outputs, grad_tokens, grad_qkv, grad_out, grad_up, grad_down, grad_up_bias, grad_biases, grad_gains)


def solution(mesh):
    both = ("rep", "fsdp")
    placed = (
        P(both, None, None),
        P(both, None, None),
        P(both),
        P(both),
        P(None, "fsdp", None),
        P(None, "fsdp", None),
        P(None, "fsdp", None),
        P(None, "fsdp", None),
        P(None, "fsdp"),
        P(None, None, "fsdp"),
        P(None, None, "fsdp"),
    )
    return jax.shard_map(
        functools.partial(on_device, mesh.shape["fsdp"], mesh.shape["rep"]),
        mesh=mesh,
        in_specs=placed,
        out_specs=(
            P(both, None, None),
            P(both, None, None),
            P(None, "fsdp", None),
            P(None, "fsdp", None),
            P(None, "fsdp", None),
            P(None, "fsdp", None),
            P(None, "fsdp"),
            P(None, None, "fsdp"),
            P(None, None, "fsdp"),
        ),
        check_vma=False,
    )
```

```python
import functools

import jax
import jax.numpy as jnp
from jax import lax
from jax.experimental import pallas as pl
from jax.experimental.pallas import tpu as pltpu
from jax.sharding import PartitionSpec as P

HEAD = 64
LAYERS = 2
GROUP = 256
ROWS = 256
VMEM_BYTES = 60 * 1024 * 1024
UP_PARTS = 4
EARLY = 2

epsilon = 1e-05
big_negative = -1000000000.0
root_half = 0.7071067811865476
inv_root_tau = 0.3989422804014327
f32 = jnp.float32
bf16 = jnp.bfloat16


def dot_nn(a, b):
    return lax.dot_general(a, b, (((1,), (0,)), ((), ())), preferred_element_type=f32)


def dot_nt(a, b):
    return lax.dot_general(a, b, (((1,), (1,)), ((), ())), preferred_element_type=f32)


def whole(shape):
    zeros = (0,) * len(shape)
    return pl.BlockSpec(shape, lambda *_: zeros, pipeline_mode=pl.Buffered(1))


def layer_of(array, layer):
    return pl.BlockSpec((None, *array.shape[1:]), lambda *_: (layer, 0, 0), pipeline_mode=pl.Buffered(1))


def column_block(rows, width):
    return pl.BlockSpec((rows, width), lambda j, *_: (0, j))


ANY = pl.BlockSpec(memory_space=pl.ANY)


def flip(index, mask):
    bit = 1
    while bit <= mask:
        if mask & bit:
            index = index + bit - 2 * bit * ((index // bit) % 2)
        bit *= 2
    return index


def exclusive_or(a, b, count):
    total, bit = 0, 1
    while bit < count:
        total = total + bit * ((a // bit + b // bit) % 2)
        bit *= 2
    return total


def greet(n, bits):
    me = lax.axis_index("fsdp")
    barrier = pltpu.get_barrier_semaphore()
    for bit in bits:
        pl.semaphore_signal(barrier, inc=1, device_id={"fsdp": flip(me, bit)}, device_id_type=pl.DeviceIdType.MESH)
    pl.semaphore_wait(barrier, len(bits))


class Gather:
    def __init__(self, own, full, order, send_sems, recv_sems, local_sem):
        self.own, self.full, self.order = own, full, order
        self.send_sems, self.recv_sems, self.local_sem = send_sems, recv_sems, local_sem
        self.me = lax.axis_index("fsdp")
        self.depth = own.shape[0]

    def rows(self, mask):
        return self.full.at[pl.ds(pl.multiple_of(flip(self.me, mask) * self.depth, 16), self.depth), :]

    def round_masks(self, round_at):
        earlier = self.order[:round_at]
        masks = [0]
        for bit in earlier:
            masks += [mask | bit for mask in masks]
        return [mask | self.order[round_at] for mask in masks]

    def copy(self, mask):
        bit = [bit for bit in self.order if bit & mask][-1]
        held = mask ^ bit
        return pltpu.make_async_remote_copy(
            src_ref=self.own if held == 0 else self.rows(held),
            dst_ref=self.rows(held),
            send_sem=self.send_sems.at[mask],
            recv_sem=self.recv_sems.at[mask],
            device_id={"fsdp": flip(self.me, bit)},
            device_id_type=pl.DeviceIdType.MESH,
        )

    def begin(self, round_at):
        if round_at == 0:
            pltpu.make_async_copy(self.own, self.rows(0), self.local_sem).start()
        self.copy(self.order[round_at]).start()

    def onward(self, round_at, which=slice(None)):
        masks = self.round_masks(round_at)[which]
        for mask in masks:
            self.copy(mask).wait_recv()
        for bit in self.order[round_at + 1 :]:
            for mask in masks:
                self.copy(mask | bit).start()

    def end(self):
        pltpu.make_async_copy(self.own, self.rows(0), self.local_sem).wait()
        for round_at in range(len(self.order)):
            for mask in self.round_masks(round_at):
                self.copy(mask).wait_send()


def begin_all(n, gathers):
    rounds = len(gathers[0].order)
    greet(n, gathers[0].order)
    for round_at in range(rounds):
        for gather in gathers:
            gather.begin(round_at)


def onward_all(gathers, round_at, which=slice(None)):
    for gather in gathers:
        gather.onward(round_at, which)


def onward_rest(gathers):
    onward_all(gathers, 1, slice(1, None))
    for round_at in range(2, len(gathers[0].order)):
        onward_all(gathers, round_at)


def end_all(gathers):
    for gather in gathers:
        gather.end()


def make_gathers(layer, parts, shards, wholes, sems):
    send_sems, recv_sems, local_sems = sems
    gathers = []
    for at, ((which, column, width, order), full) in enumerate(zip(parts, wholes)):
        own = shards[which].at[layer, :, pl.ds(column, width)]
        gathers.append(Gather(own, full, order, send_sems.at[at], recv_sems.at[at], local_sems.at[at]))
    return gathers


def parts_of(which, shard, count, orders, first=0):
    step = shard.shape[2] // count
    return [(which, at * step, step, orders[at % 2]) for at in range(first, count)]


def gather_sems(n, count):
    return [
        pltpu.SemaphoreType.DMA((count, n)),
        pltpu.SemaphoreType.DMA((count, n)),
        pltpu.SemaphoreType.DMA((count,)),
    ]


def wholes_of(n, shards, parts):
    return tuple(
        jax.ShapeDtypeStruct((shards[which].shape[1] * n, width), shards[which].dtype) for which, _, width, _ in parts
    )


def gather_kernel(n, layer, parts, shard_count, *refs):
    shards, wholes = refs[:shard_count], refs[shard_count : shard_count + len(parts)]
    gathers = make_gathers(layer, parts, shards, wholes, refs[shard_count + len(parts) :])
    begin_all(n, gathers)
    for round_at in range(len(gathers[0].order)):
        onward_all(gathers, round_at)
    end_all(gathers)


def gather_weights(n, layer, shards, parts, collective_id):
    return pl.pallas_call(
        functools.partial(gather_kernel, n, layer, parts, len(shards)),
        out_shape=wholes_of(n, shards, parts),
        in_specs=[ANY] * len(shards),
        out_specs=tuple([ANY] * len(parts)),
        scratch_shapes=gather_sems(n, len(parts)),
        compiler_params=pltpu.CompilerParams(collective_id=collective_id, has_side_effects=True),
        name="gather_weights",
    )(*shards)


def part_copies(sources, target, sems, first=0):
    copies, column = [], 0
    for at, source in enumerate(sources):
        width = source.shape[1]
        copies.append(pltpu.make_async_copy(source, target.at[:, pl.ds(column, width)], sems.at[first + at]))
        column += width
    return copies


def both_copies(sources, count, targets, sems):
    return part_copies(sources[:count], targets[0], sems), part_copies(sources[count:], targets[1], sems, count)


BLOCK = 96


def add_rows(rows, target, sources):
    def step(block, carry):
        at = pl.ds(pl.multiple_of(block * BLOCK, BLOCK), BLOCK)
        total = None
        for ref, lead in sources:
            value = ref[(*lead, at)].astype(f32)
            total = value if total is None else total + value
        ref, lead = target
        ref[(*lead, at)] = total.astype(ref.dtype)
        return carry

    lax.fori_loop(0, rows // BLOCK, step, 0)


class Reduce:
    def __init__(self, halves, scratch, bits):
        self.keep, self.send = halves[:2], halves[2:]
        self.held, self.arrived = scratch[:2]
        hops = len(bits)
        self.hop_in = scratch[2 : 2 + hops]
        self.sems, self.hop_send, self.hop_recv = scratch[2 + hops : 5 + hops]
        self.orders = (bits[::-1], bits)
        self.chips, self.rows = self.held.shape[1:3]
        self.me = lax.axis_index("fsdp")

    def load(self, stream):
        return pltpu.make_async_copy(self.keep[stream], self.held.at[stream], self.sems.at[0, stream])

    def core_copy(self, stream):
        return pltpu.make_async_remote_copy(
            src_ref=self.send[stream],
            dst_ref=self.arrived.at[stream],
            send_sem=self.sems.at[1, stream],
            recv_sem=self.sems.at[2, stream],
            device_id={"fsdp": flip(self.me, 1)},
            device_id_type=pl.DeviceIdType.MESH,
        )

    def begin(self):
        for stream in range(2):
            self.core_copy(stream).start()
            self.load(stream).start()

    def leaving(self, stream, hop):
        gone = [bit // 2 for bit in self.orders[stream][:hop]]
        half = self.orders[stream][hop] // 2
        return half, [p for p in range(self.chips) if p & half and not any(p & g for g in gone)]

    def terms(self, stream, place, hops):
        found = [(self.held, (stream, place)), (self.arrived, (stream, place))]
        for hop in range(hops):
            half, places = self.leaving(stream, hop)
            found.append((self.hop_in[hop], (stream, places.index(place | half))))
        return found

    def hop_copy(self, stream, hop, slot, place):
        return pltpu.make_async_remote_copy(
            src_ref=self.held.at[stream, place],
            dst_ref=self.hop_in[hop].at[stream, slot],
            send_sem=self.hop_send.at[stream, hop, slot],
            recv_sem=self.hop_recv.at[stream, hop, slot],
            device_id={"fsdp": flip(self.me, self.orders[stream][hop])},
            device_id_type=pl.DeviceIdType.MESH,
        )

    def wait_before(self, stream, hop):
        if hop == 0:
            self.load(stream).wait()
            self.core_copy(stream).wait_recv()
        else:
            _, places = self.leaving(stream, hop - 1)
            for slot, place in enumerate(places):
                self.hop_copy(stream, hop - 1, slot, place).wait_recv()

    def hop(self, at):
        for stream in range(2):
            self.wait_before(stream, at)
            _, places = self.leaving(stream, at)
            for place in places:
                add_rows(self.rows, (self.held, (stream, place)), self.terms(stream, place, at))
            for slot, place in enumerate(places):
                self.hop_copy(stream, at, slot, place).start()

    def finish(self, result):
        hops = len(self.hop_in)
        for stream in range(2):
            self.wait_before(stream, hops)
            add_rows(self.rows, (result, (stream,)), self.terms(stream, 0, hops))
        for stream in range(2):
            self.core_copy(stream).wait_send()
            for hop in range(hops):
                _, places = self.leaving(stream, hop)
                for slot, place in enumerate(places):
                    self.hop_copy(stream, hop, slot, place).wait_send()


def reduce_scratch(chips, rows, width, hops):
    return (
        [pltpu.VMEM((2, chips, rows, width), bf16)] * 2
        + [pltpu.VMEM((2, chips >> (hop + 1), rows, width), bf16) for hop in range(hops)]
        + [pltpu.SemaphoreType.DMA((3, 2))]
        + [pltpu.SemaphoreType.DMA((2, hops, chips // 2))] * 2
    )


class Spread:
    def __init__(self, count, scratch, first=0):
        self.first = first
        self.total, self.outgoing, self.incoming, self.whole, self.load_sems, self.sems = scratch
        self.bits = []
        bit = 1
        while bit < count:
            self.bits.append(bit)
            bit *= 2
        self.rank = lax.axis_index("rep")
        self.streams, self.rows = self.total.shape[:2]

    def load(self, stream, source):
        target = self.total.at[stream, pl.ds(0, source.shape[1])]
        return pltpu.make_async_copy(source.at[self.first + stream], target, self.load_sems.at[stream])

    def begin(self, source):
        for stream in range(self.streams):
            self.load(stream, source).start()

    def loaded(self, source):
        for stream in range(self.streams):
            self.load(stream, source).wait()
        self.tick(0)

    def side(self, bit):
        return (self.rank // bit) % 2

    def span(self, stage):
        start, size = 0, self.rows
        for bit in self.bits[:stage]:
            size //= 2
            start = start + self.side(bit) * size
        return start, size

    def down_copy(self, stream, stage):
        size = self.rows >> (stage + 1)
        at = pl.ds(self.rows - (self.rows >> stage), size)
        return pltpu.make_async_remote_copy(
            src_ref=self.outgoing.at[stream, at],
            dst_ref=self.incoming.at[stream, at],
            send_sem=self.sems.at[0, stream, stage],
            recv_sem=self.sems.at[1, stream, stage],
            device_id={"rep": flip(self.rank, self.bits[stage])},
            device_id_type=pl.DeviceIdType.MESH,
        )

    def up_copy(self, stream, stage):
        start, size = self.span(stage + 1)
        at = pl.ds(pl.multiple_of(start, 16), size)
        return pltpu.make_async_remote_copy(
            src_ref=self.whole.at[stream, at],
            dst_ref=self.whole.at[stream, at],
            send_sem=self.sems.at[2, stream, stage],
            recv_sem=self.sems.at[3, stream, stage],
            device_id={"rep": flip(self.rank, self.bits[stage])},
            device_id_type=pl.DeviceIdType.MESH,
        )

    def act(self, stream, tick):
        stages = len(self.bits)
        if 0 < tick <= stages:
            stage = tick - 1
            self.down_copy(stream, stage).wait_recv()
            start, size = self.span(tick)
            base = self.rows - (self.rows >> stage)
            at = pl.ds(pl.multiple_of(start, 16), size)
            self.total[stream, at] += self.incoming[stream, pl.ds(base, size)].astype(f32)
        if tick < stages:
            bit = self.bits[tick]
            start, size = self.span(tick)
            size //= 2
            base = self.rows - (self.rows >> tick)
            at = pl.ds(pl.multiple_of(start + (1 - self.side(bit)) * size, 16), size)
            self.outgoing[stream, pl.ds(base, size)] = self.total[stream, at].astype(bf16)
            self.down_copy(stream, tick).start()
        elif tick == stages:
            start, size = self.span(stages)
            at = pl.ds(pl.multiple_of(start, 16), size)
            self.whole[stream, at] = self.total[stream, at].astype(bf16)
            self.up_copy(stream, stages - 1).start()
        else:
            stage = 2 * stages - tick
            self.up_copy(stream, stage).wait_recv()
            if stage:
                self.up_copy(stream, stage - 1).start()

    @property
    def ticks(self):
        return 2 * len(self.bits) + self.streams

    def tick(self, tick):
        for stream in range(self.streams):
            if 0 <= tick - stream <= 2 * len(self.bits):
                self.act(stream, tick - stream)

    def end(self):
        for stream in range(self.streams):
            for stage in range(len(self.bits)):
                self.down_copy(stream, stage).wait_send()
                self.up_copy(stream, stage).wait_send()


CHAIN = 4
PIECES = 2


class Chain(Spread):
    def __init__(self, count, scratch, first=0, lag=1):
        super().__init__(count, scratch, first)
        self.lag = lag
        self.inner = (self.rank == 1) | (self.rank == 2)
        self.chunks = self.streams * PIECES

    def place(self, chunk):
        size = self.rows // PIECES
        return chunk // PIECES, pl.ds((chunk % PIECES) * size, size)

    def copy(self, leg, chunk):
        stream, at = self.place(chunk)
        source = self.whole if leg == 2 else self.outgoing
        target = self.whole.at[stream, at] if leg == 2 else self.incoming.at[leg * self.streams + stream, at]
        return pltpu.make_async_remote_copy(
            src_ref=source.at[stream, at],
            dst_ref=target,
            send_sem=self.sems.at[2 * leg, chunk],
            recv_sem=self.sems.at[2 * leg + 1, chunk],
            device_id={"rep": flip(self.rank, 3 if leg == 1 else 1)},
            device_id_type=pl.DeviceIdType.MESH,
        )

    def act(self, chunk, tick):
        stream, at = self.place(chunk)

        if tick == 0:

            @pl.when(jnp.logical_not(self.inner))
            def _():
                self.outgoing[stream, at] = self.total[stream, at].astype(bf16)
                self.copy(0, chunk).start()

        elif tick == 3:

            @pl.when(jnp.logical_not(self.inner))
            def _():
                self.copy(2, chunk).wait_recv()

        else:

            @pl.when(self.inner)
            def _():
                self.copy(tick - 1, chunk).wait_recv()
                arrived = self.incoming[(tick - 1) * self.streams + stream, at].astype(f32)
                if tick == 1:
                    self.outgoing[stream, at] = (self.total[stream, at] + arrived).astype(bf16)
                else:
                    self.whole[stream, at] = (self.outgoing[stream, at].astype(f32) + arrived).astype(bf16)
                self.copy(tick, chunk).start()

    @property
    def ticks(self):
        return (self.chunks - 1) * self.lag + 4

    def tick(self, tick):
        if tick == 0:
            for chunk in range(self.chunks):
                self.act(chunk, 0)
            return
        for chunk in range(self.chunks - 1, -1, -1) if self.lag else range(self.chunks):
            if 1 <= tick - chunk * self.lag <= 3:
                self.act(chunk, tick - chunk * self.lag)

    def end(self):
        for chunk in range(self.chunks):

            @pl.when(self.inner)
            def _():
                self.copy(1, chunk).wait_send()
                self.copy(2, chunk).wait_send()

            @pl.when(jnp.logical_not(self.inner))
            def _():
                self.copy(0, chunk).wait_send()


def make_spread(count, scratch, first=0, lag=1):
    return Chain(count, scratch, first, lag) if count == CHAIN else Spread(count, scratch, first)


def rep_masks(count):
    return [1, 3] if count == CHAIN else bits_below(count)


def padded(rows, count):
    return -(-rows // (16 * count)) * 16 * count


def spread_scratch(rows, width, count, streams=2):
    rows = padded(rows, count)
    stages = count.bit_length() - 1
    return [
        pltpu.VMEM((streams, rows, width), f32),
        pltpu.VMEM((streams, rows, width), bf16),
        pltpu.VMEM((2 * streams if count == CHAIN else streams, rows, width), bf16),
        pltpu.VMEM((streams, rows, width), bf16),
        pltpu.SemaphoreType.DMA((streams,)),
        pltpu.SemaphoreType.DMA((6, streams * PIECES) if count == CHAIN else (4, streams, stages)),
    ]


def greet_both(n, reps, fsdp_bits, rep_bits):
    me, rank = lax.axis_index("fsdp"), lax.axis_index("rep")
    barrier = pltpu.get_barrier_semaphore()
    for bit in fsdp_bits:
        pl.semaphore_signal(barrier, inc=1, device_id={"fsdp": flip(me, bit)}, device_id_type=pl.DeviceIdType.MESH)
    for bit in rep_bits:
        pl.semaphore_signal(barrier, inc=1, device_id={"rep": flip(rank, bit)}, device_id_type=pl.DeviceIdType.MESH)
    pl.semaphore_wait(barrier, len(fsdp_bits) + len(rep_bits))


def bits_below(count, first=1):
    bits = []
    while first < count:
        bits.append(first)
        first *= 2
    return bits


def norm_forward(total, gain, shift):
    middle = jnp.mean(total, axis=-1, keepdims=True)
    centred = total - middle
    spread = jnp.mean(centred * centred, axis=-1, keepdims=True)
    scaling = lax.rsqrt(spread + epsilon)
    normed = centred * scaling
    return normed * gain + shift, normed, scaling


def norm_backward(grad, normed, scaling, gain):
    scaled = grad * gain
    first = jnp.mean(scaled, axis=-1, keepdims=True)
    second = jnp.mean(scaled * normed, axis=-1, keepdims=True)
    return scaling * (scaled - first - normed * second)


def head_mask(shape, head):
    lanes = lax.broadcasted_iota(jnp.int32, shape, 1)
    return (lanes >= head * HEAD) & (lanes < (head + 1) * HEAD)


def attend_forward_kernel(n, seqs, layer, counts, parts, x_ref, small_ref, mask_ref, *refs):
    first, given, taken = counts
    sources, shards, refs = refs[:given], refs[given : given + taken], refs[given + taken :]
    count = len(parts)
    q_ref, k_ref, v_ref, ctx_ref, lse_ref, mid_ref, low_ref, n1_ref, r1_ref = refs[:9]
    wholes, refs = refs[9 : 9 + count], refs[9 + count :]
    base, w_qkv, w_out, acc, sems, mid_buffer, low_buffer, n1_buffer, out_sems = refs[:9]
    gathers = make_gathers(layer, parts, shards, wholes, refs[9:])
    out_copies = [
        pltpu.make_async_copy(source, target, out_sems.at[at])
        for at, (source, target) in enumerate(((mid_buffer, mid_ref), (low_buffer, low_ref), (n1_buffer, n1_ref)))
    ]
    step, steps = pl.program_id(0), pl.num_programs(0)
    rows, width = x_ref.shape
    seq = rows // seqs
    heads = GROUP // HEAD
    copies = sum(both_copies(sources, first, (w_qkv, w_out), sems), [])

    @pl.when(step == 0)
    def _():
        for copy in copies:
            copy.start()
        begin_all(n, gathers)

        def prepare(block, carry):
            at = pl.ds(pl.multiple_of(block * ROWS, ROWS), ROWS)
            base[at, :] = x_ref[at, :].astype(bf16)
            acc[at, :] = x_ref[at, :].astype(f32) + small_ref[2:3, :]
            return carry

        lax.fori_loop(0, rows // ROWS, prepare, 0)
        for copy in copies:
            copy.wait()

    columns = pl.multiple_of(step * GROUP, GROUP)
    q_bias = small_ref[0:1, pl.ds(columns, GROUP)]
    v_bias = small_ref[1:2, pl.ds(columns, GROUP)]

    def project(block, carry):
        at = pl.ds(pl.multiple_of(block * ROWS, ROWS), ROWS)
        low = base[at, :]
        q = dot_nn(low, w_qkv[:, pl.ds(columns, GROUP)])
        q_ref[at, :] = ((q + q_bias) * HEAD ** (-0.5)).astype(bf16)
        k = dot_nn(low, w_qkv[:, pl.ds(pl.multiple_of(width + columns, GROUP), GROUP)])
        k_ref[at, :] = k.astype(bf16)
        v = dot_nn(low, w_qkv[:, pl.ds(pl.multiple_of(2 * width + columns, GROUP), GROUP)])
        v_ref[at, :] = (v + v_bias).astype(bf16)
        return carry

    lax.fori_loop(0, rows // ROWS, project, 0)

    def attend(s, carry):
        at = pl.ds(pl.multiple_of(s * seq, seq), seq)
        q, k = q_ref[at, :], k_ref[at, :]
        v_turned = v_ref[at, :].T
        key_mask = mask_ref[at, :]
        parts = []
        for head in range(heads):
            q_head = jnp.where(head_mask(q.shape, head), q, jnp.zeros_like(q))
            scores = dot_nt(k, q_head) + key_mask
            peak = jnp.max(scores, axis=0, keepdims=True)
            raised = jnp.exp(scores - peak)
            total = jnp.sum(raised, axis=0, keepdims=True)
            mixed = dot_nn(v_turned[head * HEAD : (head + 1) * HEAD, :], raised.astype(bf16))
            parts.append((mixed / total).astype(bf16))
            lse_ref[0, pl.ds(s * heads + head, 1), :] = peak + jnp.log(total)
        ctx_ref[at, :] = jnp.concatenate(parts, axis=0).T
        return carry

    lax.fori_loop(0, seqs, attend, 0)

    @pl.when(step == 1)
    def _():
        onward_all(gathers, 0)

    @pl.when(step == steps - 1)
    def _():
        onward_all(gathers, 1, slice(1))

    def mix(block, carry):
        at = pl.ds(pl.multiple_of(block * ROWS, ROWS), ROWS)
        acc[at, :] += dot_nn(ctx_ref[at, :], w_out[pl.ds(columns, GROUP), :])
        return carry

    lax.fori_loop(0, rows // ROWS, mix, 0)

    @pl.when(step == steps - 1)
    def _():
        def finish(block, carry):
            at = pl.ds(pl.multiple_of(block * ROWS, ROWS), ROWS)
            mid, normed, scaling = norm_forward(acc[at, :], small_ref[6:7, :], small_ref[4:5, :])
            mid_buffer[at, :] = mid
            low_buffer[at, :] = mid.astype(bf16)
            n1_buffer[at, :] = normed.astype(bf16)
            r1_ref[at, :] = scaling
            return carry

        lax.fori_loop(0, rows // ROWS, finish, 0)
        for copy in out_copies:
            copy.start()
        onward_rest(gathers)
        end_all(gathers)
        for copy in out_copies:
            copy.wait()


def attend_forward(n, x, small, key_mask, w_qkv, w_out, seqs, layer, shards, parts, collective_id):
    rows, width = x.shape
    steps = width // GROUP
    seq = rows // seqs
    wide = jax.ShapeDtypeStruct((rows, width), bf16)
    heads = GROUP // HEAD
    return pl.pallas_call(
        functools.partial(
            attend_forward_kernel, n, seqs, layer, (len(w_qkv), len(w_qkv) + len(w_out), len(shards)), parts
        ),
        out_shape=(
            wide,
            wide,
            wide,
            wide,
            jax.ShapeDtypeStruct((steps, seqs * heads, seq), f32),
            jax.ShapeDtypeStruct((rows, width), f32),
            wide,
            wide,
            jax.ShapeDtypeStruct((rows, 1), f32),
        )
        + wholes_of(n, shards, parts),
        grid_spec=pltpu.PrefetchScalarGridSpec(
            num_scalar_prefetch=0,
            grid=(steps,),
            in_specs=[whole((rows, width)), layer_of(small, layer), whole((rows, 1))]
            + [ANY] * (len(w_qkv) + len(w_out) + len(shards)),
            out_specs=[column_block(rows, GROUP)] * 4
            + [
                pl.BlockSpec((1, seqs * heads, seq), lambda j, *_: (j, 0, 0)),
                ANY,
                ANY,
                ANY,
                whole((rows, 1)),
            ]
            + [ANY] * len(parts),
            scratch_shapes=[
                pltpu.VMEM((rows, width), bf16),
                pltpu.VMEM((width, 3 * width), bf16),
                pltpu.VMEM((width, width), bf16),
                pltpu.VMEM((rows, width), f32),
                pltpu.SemaphoreType.DMA((len(w_qkv) + len(w_out),)),
                pltpu.VMEM((rows, width), f32),
                pltpu.VMEM((rows, width), bf16),
                pltpu.VMEM((rows, width), bf16),
                pltpu.SemaphoreType.DMA((3,)),
            ]
            + gather_sems(n, len(parts)),
        ),
        compiler_params=pltpu.CompilerParams(
            dimension_semantics=("arbitrary",),
            vmem_limit_bytes=VMEM_BYTES,
            collective_id=collective_id,
            has_side_effects=True,
        ),
        cost_estimate=cost(8 * rows * width * width + 16 * rows * seq * width, 20 * rows * width),
        name="attend_forward",
    )(x, small, key_mask, *w_qkv, *w_out, *shards)


def ffn_forward_kernel(n, last, layer, counts, parts, mid_ref, low_ref, small_ref, up_bias_ref, valid_ref, *refs):
    first, given, taken = counts
    sources, shards, refs = refs[:given], refs[given : given + taken], refs[given + taken :]
    count = len(parts)
    act_ref, slope_ref, n2_ref, r2_ref, hid_ref = refs[:5]
    refs = refs[5:]
    if not last:
        hid_low_ref, refs = refs[0], refs[1:]
    wholes, refs = refs[:count], refs[count:]
    w_up, w_down, acc, sems, n2_buffer, hid_buffer, low_buffer, out_sems = refs[:8]
    gathers = make_gathers(layer, parts, shards, wholes, refs[8:]) if count else []
    out_pairs = [(n2_buffer, n2_ref), (hid_buffer, hid_ref)] + ([] if last else [(low_buffer, hid_low_ref)])
    out_copies = [
        pltpu.make_async_copy(source, target, out_sems.at[at]) for at, (source, target) in enumerate(out_pairs)
    ]
    step, steps = pl.program_id(0), pl.num_programs(0)
    rows, width = mid_ref.shape
    chunk = act_ref.shape[1]
    copies = sum(both_copies(sources, first, (w_up, w_down), sems), [])

    @pl.when(step == 0)
    def _():
        for copy in copies:
            copy.start()
        if gathers:
            begin_all(n, gathers)

        def prepare(block, carry):
            at = pl.ds(pl.multiple_of(block * ROWS, ROWS), ROWS)
            acc[at, :] = mid_ref[at, :] + small_ref[3:4, :]
            return carry

        lax.fori_loop(0, rows // ROWS, prepare, 0)
        for copy in copies:
            copy.wait()

    if gathers:

        @pl.when(step == 2)
        def _():
            onward_all(gathers, 0)

        @pl.when(step == 3)
        def _():
            onward_all(gathers, 1, slice(1))

    columns = pl.multiple_of(step * chunk, chunk)
    tile = 256

    def block_step(block, carry):
        at = pl.ds(pl.multiple_of(block * ROWS, ROWS), ROWS)
        low = low_ref[at, :]
        acts = []
        for part in range(chunk // tile):
            inside = slice(part * tile, (part + 1) * tile)
            at_units = pl.ds(pl.multiple_of(columns + part * tile, tile), tile)
            pre = dot_nn(low, w_up[:, at_units]) + up_bias_ref[:, inside]
            share = 0.5 * (1.0 + lax.erf(pre * root_half))
            act = (pre * share).astype(bf16)
            act_ref[at, inside] = act
            acts.append(act)
            density = inv_root_tau * jnp.exp(-0.5 * pre * pre)
            slope_ref[at, inside] = (share + pre * density).astype(bf16)
        acc[at, :] += dot_nn(jnp.concatenate(acts, axis=1), w_down[pl.ds(columns, chunk), :])
        return carry

    lax.fori_loop(0, rows // ROWS, block_step, 0)

    @pl.when(step == steps - 1)
    def _():
        def finish(block, carry):
            at = pl.ds(pl.multiple_of(block * ROWS, ROWS), ROWS)
            hidden, normed, scaling = norm_forward(acc[at, :], small_ref[7:8, :], small_ref[5:6, :])
            n2_buffer[at, :] = normed.astype(bf16)
            r2_ref[at, :] = scaling
            if last:
                hid_buffer[at, :] = (hidden * valid_ref[at, :]).astype(bf16)
            else:
                hid_buffer[at, :] = hidden
                low_buffer[at, :] = hidden.astype(bf16)
            return carry

        lax.fori_loop(0, rows // ROWS, finish, 0)
        for copy in out_copies:
            copy.start()

    if gathers:

        @pl.when(step == steps - 1)
        def _():
            onward_rest(gathers)
            end_all(gathers)

    @pl.when(step == steps - 1)
    def _():
        for copy in out_copies:
            copy.wait()


def ffn_forward(n, mid, low, small, up_bias, valid, w_up, w_down, last, layer, shards, parts, collective_id):
    rows, width = mid.shape
    units = up_bias.shape[2]
    chunk = width
    steps = units // chunk
    out_shape = [
        jax.ShapeDtypeStruct((rows, units), bf16),
        jax.ShapeDtypeStruct((rows, units), bf16),
        jax.ShapeDtypeStruct((rows, width), bf16),
        jax.ShapeDtypeStruct((rows, 1), f32),
        jax.ShapeDtypeStruct((rows, width), bf16 if last else f32),
    ]
    out_specs = [column_block(rows, chunk)] * 2 + [ANY, whole((rows, 1)), ANY]
    if not last:
        out_shape.append(jax.ShapeDtypeStruct((rows, width), bf16))
        out_specs.append(ANY)
    out_shape += wholes_of(n, shards, parts)
    out_specs += [ANY] * len(parts)
    if parts:
        params = pltpu.CompilerParams(
            dimension_semantics=("arbitrary",),
            vmem_limit_bytes=VMEM_BYTES,
            collective_id=collective_id,
            has_side_effects=True,
        )
    else:
        params = pltpu.CompilerParams(dimension_semantics=("arbitrary",), vmem_limit_bytes=VMEM_BYTES)
    return pl.pallas_call(
        functools.partial(
            ffn_forward_kernel, n, last, layer + 1, (len(w_up), len(w_up) + len(w_down), len(shards)), parts
        ),
        out_shape=tuple(out_shape),
        grid_spec=pltpu.PrefetchScalarGridSpec(
            num_scalar_prefetch=0,
            grid=(steps,),
            in_specs=[
                whole((rows, width)),
                whole((rows, width)),
                layer_of(small, layer),
                pl.BlockSpec((None, 1, chunk), lambda j, *_: (layer, 0, j)),
                whole((rows, 1)),
            ]
            + [ANY] * (len(w_up) + len(w_down) + len(shards)),
            out_specs=out_specs,
            scratch_shapes=[
                pltpu.VMEM((width, units), bf16),
                pltpu.VMEM((units, width), bf16),
                pltpu.VMEM((rows, width), f32),
                pltpu.SemaphoreType.DMA((len(w_up) + len(w_down),)),
                pltpu.VMEM((rows, width), bf16),
                pltpu.VMEM((rows, width), bf16 if last else f32),
                pltpu.VMEM((rows, width), bf16),
                pltpu.SemaphoreType.DMA((3,)),
            ]
            + (gather_sems(n, len(parts)) if parts else []),
        ),
        compiler_params=params,
        cost_estimate=cost(8 * rows * width * units, 8 * rows * units),
        name="ffn_forward",
    )(mid, low, small, up_bias, valid, *w_up, *w_down, *shards)


def shard_copies(n, me, source_of, keep_of, send_of, sems):
    def each(start):
        for owner in range(n):
            mask = flip(me, owner)
            place = mask // 2

            @pl.when(mask % 2 == 0)
            def _():
                copy = pltpu.make_async_copy(source_of(owner), keep_of(place), sems.at[owner])
                copy.start() if start else copy.wait()

            @pl.when(mask % 2 == 1)
            def _():
                copy = pltpu.make_async_copy(source_of(owner), send_of(place), sems.at[owner])
                copy.start() if start else copy.wait()

    return each


def ffn_backward_kernel(n, reps, counts, carry, g_ref, valid_ref, n2_ref, r2_ref, low_ref, n1_ref, r1_ref, small_ref, act_ref, slope_ref, *refs):
    sources, refs = refs[: counts[1]], refs[counts[1] :]
    if carry:
        halves, spread_from, refs = refs[:4], refs[4], refs[5:]
    gs1_ref, ga1_ref, sums_ref, up_sum_ref, down_keep, down_send, up_keep, up_send = refs[:8]
    refs = refs[8:]
    if carry:
        reduced_ref, spread_ref, refs = refs[0], refs[1], refs[2:]
    w_up, w_down, gffn, gpre, acc, low_turned, d_down, d_up, sems, out_sems = refs[:10]
    if carry:
        hops = len(bits_below(n, 2))
        reduce = Reduce(halves, refs[10 : 15 + hops], bits_below(n, 2))
        spread = make_spread(reps, refs[15 + hops : 21 + hops])
        spread_sem = refs[21 + hops]
    carry_in = carry
    step, steps = pl.program_id(0), pl.num_programs(0)
    me = lax.axis_index("fsdp")
    rows, width = acc.shape
    last_step = steps - 1
    if carry:
        out_copy = pltpu.make_async_copy(spread.whole, spread_ref, spread_sem)

        @pl.when(step == 0)
        def _():
            greet_both(n, reps, bits_below(n), rep_masks(reps))
            spread.begin(spread_from)
            reduce.begin()
            spread.loaded(spread_from)

        @pl.when(step == 1)
        def _():
            spread.tick(1)

        @pl.when(step == 2)
        def _():
            spread.tick(2)
            for hop in range(1, hops):
                reduce.hop(hop)

        @pl.when(step == 3)
        def _():
            spread.tick(4)
            reduce.finish(reduced_ref)
    chunk = act_ref.shape[1]
    per_down = down_keep.shape[1]
    per_up = up_keep.shape[2]
    tile = 256
    up_copies, down_copies = both_copies(sources, counts[0], (w_up, w_down), sems)

    @pl.when(step == 0)
    def _():
        for copy in down_copies:
            copy.start()
        for copy in up_copies:
            copy.start()
        sums_ref[...] = jnp.zeros_like(sums_ref)

        def prepare(block, carry):
            at = pl.ds(pl.multiple_of(block * ROWS, ROWS), ROWS)
            grad = g_ref[at, :].astype(f32)
            if not carry_in:
                grad = grad * valid_ref[at, :]
            normed = n2_ref[at, :].astype(f32)
            summed = norm_backward(grad, normed, r2_ref[at, :], small_ref[7:8, :])
            acc[at, :] = summed
            low = summed.astype(bf16)
            gffn[at, :] = low
            sums_ref[0:1, :] += jnp.sum(grad * normed, axis=0, keepdims=True)
            sums_ref[1:2, :] += jnp.sum(grad, axis=0, keepdims=True)
            sums_ref[2:3, :] += jnp.sum(low.astype(f32), axis=0, keepdims=True)
            low_turned[:, at] = low_ref[at, :].T
            return carry

        lax.fori_loop(0, rows // ROWS, prepare, 0)
        for copy in down_copies:
            copy.wait()
        for copy in up_copies:
            copy.wait()

    columns = pl.multiple_of(step * chunk, chunk)
    up_sum_ref[...] = jnp.zeros_like(up_sum_ref)

    def through(block, carry):
        at = pl.ds(pl.multiple_of(block * ROWS, ROWS), ROWS)
        grad = gffn[at, :]
        lows = []
        for part in range(chunk // tile):
            inside = slice(part * tile, (part + 1) * tile)
            at_units = pl.ds(pl.multiple_of(columns + part * tile, tile), tile)
            grad_act = dot_nt(grad, w_down[at_units, :])
            low = (grad_act * slope_ref[at, inside].astype(f32)).astype(bf16)
            gpre[at, inside] = low
            lows.append(low)
            up_sum_ref[:, inside] += jnp.sum(low.astype(f32), axis=0, keepdims=True)
        acc[at, :] += dot_nt(jnp.concatenate(lows, axis=1), w_up[:, pl.ds(columns, chunk)])
        return carry

    lax.fori_loop(0, rows // ROWS, through, 0)
    if carry:

        @pl.when(step == 0)
        def _():
            reduce.hop(0)

        for at in (2, 3):

            @pl.when(step == at)
            def _():
                spread.tick(2 * at - 1)

    def down_out(which):
        def run(start):
            for local in range(chunk // per_down):
                owner = which * (chunk // per_down) + local
                mask = exclusive_or(me, owner, n)
                source = d_down.at[pl.ds(local * per_down, per_down), :]
                place = mask // 2

                @pl.when(mask % 2 == 0)
                def _():
                    copy = pltpu.make_async_copy(source, down_keep.at[place], out_sems.at[0, local])
                    copy.start() if start else copy.wait()

                @pl.when(mask % 2 == 1)
                def _():
                    copy = pltpu.make_async_copy(source, down_send.at[place], out_sems.at[0, local])
                    copy.start() if start else copy.wait()

        return run

    def up_out(which):
        return shard_copies(
            n,
            me,
            lambda owner: d_up.at[pl.ds(owner * per_up, per_up), :],
            lambda place: up_keep.at[place, which],
            lambda place: up_send.at[place, which],
            out_sems.at[1],
        )

    @pl.when(step > 0)
    def _():
        down_out(step - 1)(False)

    def down_part(part, carry):
        at = pl.ds(pl.multiple_of(part * tile, tile), tile)
        turned = act_ref[:, at].T
        d_down[at, :] = dot_nn(turned, gffn[...]).astype(bf16)
        return carry

    lax.fori_loop(0, chunk // tile, down_part, 0)
    down_out(step)(True)

    @pl.when(step > 0)
    def _():
        up_out(step - 1)(False)

    def up_part(part, carry):
        at = pl.ds(pl.multiple_of(part * tile, tile), tile)
        d_up[at, :] = dot_nn(low_turned[at, :], gpre[...]).astype(bf16)
        return carry

    lax.fori_loop(0, width // tile, up_part, 0)
    up_out(step)(True)

    @pl.when(step == steps - 1)
    def _():
        def finish(block, carry):
            at = pl.ds(pl.multiple_of(block * ROWS, ROWS), ROWS)
            grad = acc[at, :]
            normed = n1_ref[at, :].astype(f32)
            summed = norm_backward(grad, normed, r1_ref[at, :], small_ref[6:7, :])
            gs1_ref[at, :] = summed
            low = summed.astype(bf16)
            ga1_ref[at, :] = low
            sums_ref[3:4, :] += jnp.sum(grad * normed, axis=0, keepdims=True)
            sums_ref[4:5, :] += jnp.sum(grad, axis=0, keepdims=True)
            sums_ref[5:6, :] += jnp.sum(low.astype(f32), axis=0, keepdims=True)
            return carry

        lax.fori_loop(0, rows // ROWS, finish, 0)
        down_out(step)(False)
        up_out(step)(False)
        if carry:
            for tick in range(6, spread.ticks):
                spread.tick(tick)
            out_copy.start()
            out_copy.wait()
            spread.end()


def remote_params(collective_id):
    return pltpu.CompilerParams(
        dimension_semantics=("arbitrary",),
        vmem_limit_bytes=VMEM_BYTES,
        collective_id=collective_id,
        has_side_effects=True,
    )


def ffn_backward(n, reps, grad, valid, n2, r2, low, n1, r1, small, act, slope, w_up, w_down, layer, carry, collective_id):
    rows, width = grad.shape
    units = act.shape[1]
    chunk = width
    steps = units // chunk
    chips = n // 2
    hops = len(bits_below(n, 2))
    extra_out, extra_specs, extra_scratch = [], [], []
    if carry:
        reduced = (2,) + carry[0].shape[1:]
        spread_rows = carry[4].shape[1]
        extra_out = [
            jax.ShapeDtypeStruct(reduced, f32),
            jax.ShapeDtypeStruct((2, padded(spread_rows, reps), width), bf16),
        ]
        extra_specs = [whole(reduced), ANY]
        extra_scratch = reduce_scratch(chips, carry[0].shape[1], width, hops)
        extra_scratch += spread_scratch(spread_rows, width, reps) + [pltpu.SemaphoreType.DMA]
    down_half = jax.ShapeDtypeStruct((chips, units // n, width), bf16)
    up_half = jax.ShapeDtypeStruct((chips, steps, width // n, chunk), bf16)
    return pl.pallas_call(
        functools.partial(ffn_backward_kernel, n, reps, (len(w_up), len(w_up) + len(w_down)), bool(carry)),
        out_shape=(
            jax.ShapeDtypeStruct((rows, width), f32),
            jax.ShapeDtypeStruct((rows, width), bf16),
            jax.ShapeDtypeStruct((8, width), f32),
            jax.ShapeDtypeStruct((1, units), f32),
            down_half,
            down_half,
            up_half,
            up_half,
            *extra_out,
        ),
        grid_spec=pltpu.PrefetchScalarGridSpec(
            num_scalar_prefetch=0,
            grid=(steps,),
            in_specs=[
                whole((rows, width)),
                whole((rows, 1)),
                whole((rows, width)),
                whole((rows, 1)),
                whole((rows, width)),
                whole((rows, width)),
                whole((rows, 1)),
                layer_of(small, layer),
                column_block(rows, chunk),
                column_block(rows, chunk),
            ]
            + [ANY] * (len(w_up) + len(w_down) + len(carry)),
            out_specs=[
                whole((rows, width)),
                whole((rows, width)),
                whole((8, width)),
                column_block(1, chunk),
            ]
            + [ANY] * 4
            + extra_specs,
            scratch_shapes=[
                pltpu.VMEM((width, units), bf16),
                pltpu.VMEM((units, width), bf16),
                pltpu.VMEM((rows, width), bf16),
                pltpu.VMEM((rows, chunk), bf16),
                pltpu.VMEM((rows, width), f32),
                pltpu.VMEM((width, rows), bf16),
                pltpu.VMEM((chunk, width), bf16),
                pltpu.VMEM((width, chunk), bf16),
                pltpu.SemaphoreType.DMA((len(w_up) + len(w_down),)),
                pltpu.SemaphoreType.DMA((2, n)),
            ]
            + extra_scratch,
        ),
        compiler_params=remote_params(collective_id)
        if carry
        else pltpu.CompilerParams(dimension_semantics=("arbitrary",), vmem_limit_bytes=VMEM_BYTES),
        cost_estimate=cost(10 * rows * width * units, 8 * rows * units),
        name="ffn_backward",
    )(grad, valid, n2, r2, low, n1, r1, small, act, slope, *w_up, *w_down, *carry)


def attend_backward_kernel(n, reps, seqs, counts, spreads, ga_ref, gs_ref, base_ref, mask_ref, q_ref, k_ref, v_ref, ctx_ref, lse_ref, *refs):
    sources, refs = refs[: counts[1]], refs[counts[1] :]
    halves, refs = refs[:4], refs[4:]
    if spreads:
        spread_from, refs = refs[0], refs[1:]
    gh_ref, sums_ref, a_keep, b_keep, a_send, b_send, reduced_ref = refs[:7]
    refs = refs[7:]
    if spreads:
        spread_ref, refs = refs[0], refs[1:]
    w_qkv, w_out, acc, base_turned, gctx, gproj, d_qkv, d_out, p_all, ds_all, ctx_turned, sems, out_sems = refs[:13]
    hops = len(bits_below(n, 2))
    reduce = Reduce(halves, refs[13 : 18 + hops], bits_below(n, 2))
    step, steps = pl.program_id(0), pl.num_programs(0)
    me = lax.axis_index("fsdp")
    if spreads:
        spread = make_spread(reps, refs[18 + hops : 24 + hops], 0, 0)
        spread_copy = pltpu.make_async_copy(spread.whole, spread_ref, refs[24 + hops])

    @pl.when(step == 0)
    def _():
        greet_both(n, reps, bits_below(n), rep_masks(reps) if spreads else [])
        if spreads:
            spread.begin(spread_from)
        reduce.begin()
        if spreads:
            spread.loaded(spread_from)

    if spreads:

        for at in (1, 2):

            @pl.when(step == at)
            def _():
                spread.tick(at)

    rows, width = ga_ref.shape
    seq = rows // seqs
    heads = GROUP // HEAD
    per = width // n
    tile = 256
    qkv_copies, out_copies = both_copies(sources, counts[0], (w_qkv, w_out), sems)

    @pl.when(step == 0)
    def _():
        for copy in out_copies:
            copy.start()
        for copy in qkv_copies:
            copy.start()

        def turn(block, carry):
            at = pl.ds(pl.multiple_of(block * ROWS, ROWS), ROWS)
            acc[at, :] = gs_ref[at, :]
            base_turned[:, at] = base_ref[at, :].T
            return carry

        lax.fori_loop(0, rows // ROWS, turn, 0)
        for copy in out_copies:
            copy.wait()
        for copy in qkv_copies:
            copy.wait()

    columns = pl.multiple_of(step * GROUP, GROUP)

    def through(block, carry):
        at = pl.ds(pl.multiple_of(block * ROWS, ROWS), ROWS)
        gctx[at, :] = dot_nt(ga_ref[at, :], w_out[pl.ds(columns, GROUP), :]).astype(bf16)
        return carry

    lax.fori_loop(0, rows // ROWS, through, 0)
    ctx_turned[...] = ctx_ref[...].T

    def out_part(part, carry):
        at = pl.ds(pl.multiple_of(part * tile, tile), tile)
        d_out[pl.ds(columns, GROUP), at] = dot_nn(ctx_turned[...], ga_ref[:, at]).astype(bf16)
        return carry

    lax.fori_loop(0, width // tile, out_part, 0)

    @pl.when(step == 2)
    def _():
        for hop in range(1, hops):
            reduce.hop(hop)

    def attend(s, carry):
        @pl.when((step == 0) & (s == seqs - 1))
        def _():
            reduce.hop(0)

        at = pl.ds(pl.multiple_of(s * seq, seq), seq)
        q, k, v, grad = q_ref[at, :], k_ref[at, :], v_ref[at, :], gctx[at, :]
        k_turned = k.T
        key_mask = mask_ref[at, :]
        parts, q_heads, g_heads = [], [], []
        for head in range(heads):
            inside = head_mask(q.shape, head)
            q_head = jnp.where(inside, q, jnp.zeros_like(q))
            g_head = jnp.where(inside, grad, jnp.zeros_like(grad))
            scores = dot_nt(k, q_head) + key_mask
            attention = jnp.exp(scores - lse_ref[0, pl.ds(s * heads + head, 1), :])
            weighted = attention * dot_nt(v, g_head)
            inner = jnp.sum(weighted, axis=0, keepdims=True)
            grad_scores = (weighted - attention * inner).astype(bf16)
            here = slice(head * seq, (head + 1) * seq)
            p_all[:, here] = attention.astype(bf16)
            ds_all[:, here] = grad_scores
            turned = dot_nn(k_turned[head * HEAD : (head + 1) * HEAD, :], grad_scores)
            parts.append(turned.astype(bf16) * HEAD ** (-0.5))
            q_heads.append(q_head)
            g_heads.append(g_head)
        gproj[at, 0:GROUP] = jnp.concatenate(parts, axis=0).T
        gproj[at, GROUP : 2 * GROUP] = dot_nn(ds_all[...], jnp.concatenate(q_heads, axis=0)).astype(bf16)
        gproj[at, 2 * GROUP : 3 * GROUP] = dot_nn(p_all[...], jnp.concatenate(g_heads, axis=0)).astype(bf16)
        return carry

    lax.fori_loop(0, seqs, attend, 0)
    sums_ref[...] = jnp.zeros_like(sums_ref)


    def onward(block, carry):
        at = pl.ds(pl.multiple_of(block * ROWS, ROWS), ROWS)
        term = dot_nt(gproj[at, 0:GROUP], w_qkv[:, pl.ds(columns, GROUP)])
        term += dot_nt(gproj[at, GROUP : 2 * GROUP], w_qkv[:, pl.ds(pl.multiple_of(width + columns, GROUP), GROUP)])
        term += dot_nt(gproj[at, 2 * GROUP : 3 * GROUP], w_qkv[:, pl.ds(pl.multiple_of(2 * width + columns, GROUP), GROUP)])
        sums_ref[0:1, :] += jnp.sum(gproj[at, 0:GROUP].astype(f32), axis=0, keepdims=True)
        sums_ref[1:2, :] += jnp.sum(gproj[at, 2 * GROUP : 3 * GROUP].astype(f32), axis=0, keepdims=True)
        acc[at, :] += term
        return carry

    lax.fori_loop(0, rows // ROWS, onward, 0)

    @pl.when(step == steps - 1)
    def _():
        def finish(block, carry):
            at = pl.ds(pl.multiple_of(block * ROWS, ROWS), ROWS)
            gh_ref[at, :] = acc[at, :].astype(gh_ref.dtype)
            return carry

        lax.fori_loop(0, rows // ROWS, finish, 0)

    def place_of(part, a_half, b_half):
        return a_half if part < 2 else b_half

    def rows_of(part):
        return pl.ds((part % 2) * per, per)

    def qkv_out(which, start):
        for part in range(3):
            at = pl.ds(pl.multiple_of(which * GROUP, GROUP), GROUP)
            shard_copies(
                n,
                me,
                lambda owner: d_qkv.at[pl.ds(owner * per, per), pl.ds(part * GROUP, GROUP)],
                lambda place: place_of(part, a_keep, b_keep).at[place, rows_of(part), at],
                lambda place: place_of(part, a_send, b_send).at[place, rows_of(part), at],
                out_sems.at[part],
            )(start)

    @pl.when(step > 0)
    def _():
        qkv_out(step - 1, False)

    def weight_part(part, carry):
        at = pl.ds(pl.multiple_of(part * tile, tile), tile)
        d_qkv[at, :] = dot_nn(base_turned[at, :], gproj[...]).astype(bf16)
        return carry

    lax.fori_loop(0, width // tile, weight_part, 0)
    qkv_out(step, True)

    @pl.when(step == steps - 1)
    def _():
        out_copy = shard_copies(
            n,
            me,
            lambda owner: d_out.at[pl.ds(owner * per, per), :],
            lambda place: b_keep.at[place, rows_of(3)],
            lambda place: b_send.at[place, rows_of(3)],
            out_sems.at[3],
        )
        out_copy(True)
        qkv_out(step, False)
        out_copy(False)
        reduce.finish(reduced_ref)
        if spreads:
            for tick in range(3, spread.ticks):
                spread.tick(tick)
            spread_copy.start()
            spread_copy.wait()
            spread.end()


def attend_backward(n, reps, ga, gs, base, key_mask, q, k, v, ctx, lse, w_qkv, w_out, seqs, out_type, carry, collective_id):
    rows, width = ga.shape
    steps = width // GROUP
    seq = rows // seqs
    heads = GROUP // HEAD
    chips = n // 2
    half = jax.ShapeDtypeStruct((chips, 2 * width // n, width), bf16)
    hops = len(bits_below(n, 2))
    reduced = (2,) + carry[0].shape[1:]
    extra_out, extra_specs = [], []
    extra_scratch = reduce_scratch(chips, carry[0].shape[1], width, hops)
    if len(carry) > 4:
        spread_rows = carry[4].shape[1]
        extra_out = [jax.ShapeDtypeStruct((2, padded(spread_rows, reps), width), bf16)]
        extra_specs = [ANY]
        extra_scratch += spread_scratch(spread_rows, width, reps) + [pltpu.SemaphoreType.DMA]
    return pl.pallas_call(
        functools.partial(
            attend_backward_kernel, n, reps, seqs, (len(w_qkv), len(w_qkv) + len(w_out)), len(carry) > 4
        ),
        out_shape=(
            jax.ShapeDtypeStruct((rows, width), out_type),
            jax.ShapeDtypeStruct((8, width), f32),
            half,
            half,
            half,
            half,
            jax.ShapeDtypeStruct(reduced, f32),
            *extra_out,
        ),
        grid_spec=pltpu.PrefetchScalarGridSpec(
            num_scalar_prefetch=0,
            grid=(steps,),
            in_specs=[whole((rows, width))] * 3
            + [whole((rows, 1))]
            + [column_block(rows, GROUP)] * 4
            + [pl.BlockSpec((1, seqs * heads, seq), lambda j, *_: (j, 0, 0))]
            + [ANY] * (len(w_qkv) + len(w_out) + len(carry)),
            out_specs=[whole((rows, width)), column_block(8, GROUP)] + [ANY] * 4 + [whole(reduced)] + extra_specs,
            scratch_shapes=[
                pltpu.VMEM((width, 3 * width), bf16),
                pltpu.VMEM((width, width), bf16),
                pltpu.VMEM((rows, width), f32),
                pltpu.VMEM((width, rows), bf16),
                pltpu.VMEM((rows, GROUP), bf16),
                pltpu.VMEM((rows, 3 * GROUP), bf16),
                pltpu.VMEM((width, 3 * GROUP), bf16),
                pltpu.VMEM((width, width), bf16),
                pltpu.VMEM((seq, heads * seq), bf16),
                pltpu.VMEM((seq, heads * seq), bf16),
                pltpu.VMEM((GROUP, rows), bf16),
                pltpu.SemaphoreType.DMA((len(w_qkv) + len(w_out),)),
                pltpu.SemaphoreType.DMA((4, n)),
            ]
            + extra_scratch,
        ),
        compiler_params=remote_params(collective_id),
        cost_estimate=cost(16 * rows * width * width + 40 * rows * seq * width, 20 * rows * width),
        name="attend_backward",
    )(ga, gs, base, key_mask, q, k, v, ctx, lse, *w_qkv, *w_out, *carry)


def cost(flops, moved):
    return pl.CostEstimate(flops=int(flops), bytes_accessed=int(moved), transcendentals=0)


def last_sums_kernel(n, reps, a_keep, b_keep, a_send, b_send, spread_from, *refs):
    sums, refs = refs[: 3 * LAYERS], refs[3 * LAYERS :]
    spread_ref, attend_ref, total_ref, *scratch = refs
    bits, rep_bits = bits_below(n, 2), bits_below(reps)
    hops = len(bits)
    reduce = Reduce((a_keep, b_keep, a_send, b_send), scratch[: 5 + hops], bits)
    first = make_spread(reps, scratch[5 + hops : 11 + hops])
    second = make_spread(reps, scratch[11 + hops : 17 + hops])
    reduced, small_out, small_in, small_sems, sems = scratch[17 + hops :]
    axes = [("fsdp", bit) for bit in bits_below(n)] + [("rep", bit) for bit in rep_bits]

    def small_copy(at):
        axis, bit = axes[at]
        return pltpu.make_async_remote_copy(
            src_ref=small_out.at[at],
            dst_ref=small_in.at[at],
            send_sem=small_sems.at[0, at],
            recv_sem=small_sems.at[1, at],
            device_id={axis: flip(lax.axis_index(axis), bit)},
            device_id_type=pl.DeviceIdType.MESH,
        )

    def small_step(at):
        small_copy(at).wait_recv()
        if at + 1 < len(axes):
            small_out[at + 1] = small_out[at] + small_in[at]
            small_copy(at + 1).start()
        else:
            total_ref[...] = small_out[at] + small_in[at]

    greet_both(n, reps, bits_below(n), sorted({*rep_bits, *rep_masks(reps)}))
    first.begin(spread_from)
    width = small_out.shape[2]
    small_out[0] = jnp.zeros(small_out.shape[1:], f32)
    for layer in range(LAYERS):
        ffn_sums, proj_sums, up_sums = sums[3 * layer : 3 * layer + 3]
        small_out[0, 16 * layer : 16 * layer + 6] = ffn_sums[0:6]
        small_out[0, 16 * layer + 6 : 16 * layer + 8] = proj_sums[0:2]
        for at in range(up_sums.shape[1] // width):
            small_out[0, 16 * layer + 8 + at : 16 * layer + 9 + at] = up_sums[:, at * width : (at + 1) * width]
    small_copy(0).start()
    reduce.begin()
    first.loaded(spread_from)
    small_step(0)
    reduce.hop(0)
    small_step(1)
    first.tick(1)
    first.tick(2)
    for hop in range(1, hops):
        reduce.hop(hop)
    for at in range(2, len(bits) + 1):
        small_step(at)
    first.tick(3)
    reduce.finish(reduced)
    rows = reduced.shape[1]
    for stream in range(2):
        second.total[stream, pl.ds(0, rows)] = reduced[stream]
    second.tick(0)
    for tick in range(4, first.ticks):
        first.tick(tick)
        second.tick(tick - 3)
        if len(bits) + tick - 3 < len(axes):
            small_step(len(bits) + tick - 3)
    first_copy = pltpu.make_async_copy(first.whole, spread_ref, sems.at[0])
    first_copy.start()
    for tick in range(first.ticks - 3, second.ticks):
        second.tick(tick)
    for at in range(len(bits) + max(first.ticks - 3, 1), len(axes)):
        small_step(at)
    second_copy = pltpu.make_async_copy(second.whole, attend_ref, sems.at[1])
    second_copy.start()
    first.end()
    second.end()
    for at in range(len(axes)):
        small_copy(at).wait_send()
    first_copy.wait()
    second_copy.wait()


def last_sums(n, reps, halves, spread_rows, sums, collective_id):
    chips, rows, width = halves[0].shape
    hops = len(bits_below(n, 2))
    count = len(bits_below(n)) + len(bits_below(reps))
    vmem = pl.BlockSpec(memory_space=pltpu.VMEM)
    return pl.pallas_call(
        functools.partial(last_sums_kernel, n, reps),
        out_shape=(
            jax.ShapeDtypeStruct((2, padded(spread_rows.shape[1], reps), width), bf16),
            jax.ShapeDtypeStruct((2, padded(rows, reps), width), bf16),
            jax.ShapeDtypeStruct((16 * LAYERS, width), f32),
        ),
        in_specs=[ANY] * 5 + [vmem] * len(sums),
        out_specs=(ANY, ANY, vmem),
        scratch_shapes=reduce_scratch(chips, rows, width, hops)
        + spread_scratch(spread_rows.shape[1], width, reps)
        + spread_scratch(rows, width, reps)
        + [
            pltpu.VMEM((2, rows, width), f32),
            pltpu.VMEM((count, 16 * LAYERS, width), f32),
            pltpu.VMEM((count, 16 * LAYERS, width), f32),
            pltpu.SemaphoreType.DMA((2, count)),
            pltpu.SemaphoreType.DMA((2,)),
        ],
        compiler_params=pltpu.CompilerParams(
            vmem_limit_bytes=VMEM_BYTES, collective_id=collective_id, has_side_effects=True
        ),
        name="last_sums",
    )(*halves, spread_rows, *sums)


def on_device(n, reps, tokens, cotangent, lengths, live_batches, w_qkv, w_out, w_up, w_down, up_bias, biases, norm_gains):
    seqs, seq, width = tokens.shape
    rows = seqs * seq
    units = w_up.shape[2]
    per = width // n
    me = lax.axis_index("fsdp").astype(jnp.int32)

    places = jnp.arange(seq, dtype=jnp.int32)
    inside = places[None, :] < lengths[:, None]
    alive = jnp.arange(seqs, dtype=jnp.int32) < live_batches[0]
    key_mask = jnp.where(inside, 0.0, big_negative).astype(f32).reshape(rows, 1)
    valid = jnp.where(inside & alive[:, None], 1.0, 0.0).astype(f32).reshape(rows, 1)

    chip_bits = bits_below(n, 2)
    orders = (tuple(chip_bits + [1]), tuple(chip_bits[::-1] + [1]))

    qkv, out, up, down = ([[] for _ in range(LAYERS)] for _ in range(4))
    attend_parts = parts_of(0, w_qkv, 2, orders) + parts_of(1, w_out, 2, orders)

    own_small = jnp.concatenate([up_bias.reshape(-1), biases.reshape(-1), norm_gains.reshape(-1)])
    small_count = own_small.shape[0]
    small_rows = -(-small_count // 2048) * 16
    own_small = jnp.pad(own_small, (0, small_rows * 128 - small_count)).reshape(1, small_rows, 128)
    small_parts = [(2, 0, 128, orders[0])]
    gathered = gather_weights(n, 0, (w_qkv, w_out, own_small), small_parts + attend_parts, 0)
    small_all = gathered[0].reshape(n, small_rows * 128)[:, :small_count]
    qkv[0], out[0] = gathered[1:3], gathered[3:5]
    cut_a = LAYERS * units // n
    cut_b = cut_a + LAYERS * 6 * per
    up_bias_all = small_all[:, :cut_a].reshape(n, LAYERS, units // n).transpose(1, 0, 2).reshape(LAYERS, 1, units)
    bias_all = small_all[:, cut_a:cut_b].reshape(n, LAYERS, 6, per).transpose(1, 2, 0, 3).reshape(LAYERS, 6, width)
    gain_all = small_all[:, cut_b:].reshape(n, LAYERS, 2, per).transpose(1, 2, 0, 3).reshape(LAYERS, 2, width)
    smalls = jnp.concatenate([bias_all, gain_all], axis=1)

    current = tokens.reshape(rows, width)
    base = current
    saved = []
    for layer in range(LAYERS):
        last = layer == LAYERS - 1
        begun = EARLY if layer else 0
        parts = parts_of(0, w_up, UP_PARTS, orders, begun) + parts_of(1, w_down, 2, orders)
        results = attend_forward(
            n, current, smalls, key_mask, qkv[layer], out[layer], seqs,
            layer, (w_up, w_down), parts, 1 + 2 * layer,
        )
        q, k, v, ctx, lse, mid, low, n1, r1 = results[:9]
        up[layer] = [*up[layer], *results[9:-2]]
        down[layer] = results[-2:]
        parts = [] if last else attend_parts + parts_of(2, w_up, UP_PARTS, orders)[:EARLY]
        results = ffn_forward(
            n, mid, low, smalls, up_bias_all, valid, up[layer], down[layer], last,
            layer, () if last else (w_qkv, w_out, w_up), parts, 2 + 2 * layer,
        )
        act, slope, n2, r2, current = results[:5]
        saved.append((base, q, k, v, ctx, lse, low, n1, r1, act, slope, n2, r2))
        if not last:
            base = results[5]
            qkv[layer + 1], out[layer + 1], up[layer + 1] = results[6:8], results[8:10], list(results[10:])
    outputs = current.reshape(seqs, seq, width)

    grad = cotangent.reshape(rows, width)
    sum_rows = [None] * LAYERS
    attend_halves, attend_reduced = None, None
    ffn_done, attend_done = [None] * LAYERS, [None] * LAYERS
    ffn_reduced = None
    for layer in range(LAYERS - 1, -1, -1):
        first = layer == LAYERS - 1
        base, q, k, v, ctx, lse, low, n1, r1, act, slope, n2, r2 = saved[layer]
        results = ffn_backward(
            n, reps, grad, valid, n2, r2, low, n1, r1, smalls, act, slope, up[layer], down[layer], layer,
            () if first else (*attend_halves, ffn_reduced), 10 + layer,
        )
        gs1, ga1, sums, up_sum, down_keep, down_send, up_keep, up_send = results[:8]
        if not first:
            attend_reduced, ffn_done[layer + 1] = results[8:]
        ffn_halves = (
            down_keep,
            up_keep.reshape(n // 2, -1, width),
            down_send,
            up_send.reshape(n // 2, -1, width),
        )
        results = attend_backward(
            n, reps, ga1, gs1, base, key_mask, q, k, v, ctx, lse, qkv[layer], out[layer], seqs,
            f32 if layer else bf16, ffn_halves + (() if first else (attend_reduced,)), 20 + layer,
        )
        grad, proj_sums = results[:2]
        attend_halves, ffn_reduced = results[2:6], results[6]
        if not first:
            attend_done[layer + 1] = results[7]
        sum_rows[layer] = (sums, proj_sums, up_sum)
    grad_tokens = grad.reshape(seqs, seq, width)
    ffn_done[0], attend_done[0], small_total = last_sums(
        n, reps, attend_halves, ffn_reduced, [array for arrays in sum_rows for array in arrays], 30
    )

    ffn_rows, attend_rows = units // n, 2 * per
    both_attend = jnp.stack([done[:, :attend_rows] for done in attend_done])
    grad_down = jnp.stack([done[0, :ffn_rows] for done in ffn_done]).astype(f32)
    grad_up = jnp.stack([done[1, :ffn_rows] for done in ffn_done])
    grad_up = grad_up.reshape(LAYERS, units // width, per, width).transpose(0, 2, 1, 3)
    grad_up = grad_up.reshape(LAYERS, per, units).astype(f32)
    parts = both_attend.reshape(LAYERS, 4, per, width)
    grad_qkv = parts[:, :3].transpose(0, 2, 1, 3).reshape(LAYERS, per, 3 * width).astype(f32)
    grad_out = parts[:, 3].astype(f32)

    small_total = small_total.reshape(LAYERS, 16, width)
    mine = lax.dynamic_slice_in_dim(small_total[:, :8], me * per, per, axis=2)
    grad_biases = jnp.stack([mine[:, at] for at in (6, 7, 5, 2, 4, 1)], axis=1)
    grad_gains = jnp.stack([mine[:, at] for at in (3, 0)], axis=1)
    up_rows = small_total[:, 8 : 8 + units // width].reshape(LAYERS, units)
    grad_up_bias = lax.dynamic_slice_in_dim(up_rows, me * (units // n), units // n, axis=1)
    return (outputs, grad_tokens, grad_qkv, grad_out, grad_up, grad_down, grad_up_bias, grad_biases, grad_gains)


def solution(mesh):
    both = ("rep", "fsdp")
    placed = (
        P(both, None, None),
        P(both, None, None),
        P(both),
        P(both),
        P(None, "fsdp", None),
        P(None, "fsdp", None),
        P(None, "fsdp", None),
        P(None, "fsdp", None),
        P(None, "fsdp"),
        P(None, None, "fsdp"),
        P(None, None, "fsdp"),
    )
    return jax.shard_map(
        functools.partial(on_device, mesh.shape["fsdp"], mesh.shape["rep"]),
        mesh=mesh,
        in_specs=placed,
        out_specs=(
            P(both, None, None),
            P(both, None, None),
            P(None, "fsdp", None),
            P(None, "fsdp", None),
            P(None, "fsdp", None),
            P(None, "fsdp", None),
            P(None, "fsdp"),
            P(None, None, "fsdp"),
            P(None, None, "fsdp"),
        ),
        check_vma=False,
    )
```
